128 devices in a mesh: gx: 8 (over x, core), gy: 16 (over z, y).
Axes of the slice: x: 4, y: 4, z: 4, core: 2. Of those that a mesh axis runs over, the one named last changes fastest.
Arguments:
- forcing: float32 [2048, 8192], P('gx', 'gy'), may hold values from -8 to 8
- bathymetry: float32 [2048, 8192], P('gx', 'gy'), may hold values from 0.1 to 10
- ocean_mask: int32 [2048, 8192], P('gx', 'gy'), may hold values 0 or 1
- aggregate_id: int32 [32, 128], P('gx', 'gy'), may hold values from 0 to 511, as said below
- coarse_inverse: float32 [512, 512], P(('gx', 'gy')), may hold values from -1 to 1
Outputs:
- solution: float32 [2048, 8192], P('gx', 'gy')
- residual: float32 [2048, 8192], P('gx', 'gy')
The draws below stay inside these ranges and needn't reach their ends.
Inputs may be any that keep to these rules, and one draw needn't show every extreme that they name: `aggregate_id`: each aggregate holds exactly 8 tiles, consecutive in the row-major order of tiles.
All inputs are finite; a program needn't handle non-finite values. No bound on the sum of `ocean_mask` on one device may be relied on, other than what follows from the above.
Results may differ from the reference program's by a relative error of at most 0.00075.
Values sent between devices are 32-bit elements; how exact they have to be, the bound alone decides.
A program may use at most 128 MiB of HBM per device.

```python
import math
import jax
import jax.numpy as jnp
from jax import lax

TILE = 64
NAGG = 512
KB = 8
CYCLES = 2
NX = 2048
NY = 8192
PER = 8
CELLS_AGG = 32768


def draw_forcing(key, part):
    key_rough = jax.random.fold_in(key, 11)
    key_waves = jax.random.fold_in(key, 12)
    key_phase = jax.random.fold_in(key, 13)
    row_pos = jnp.arange(NX, dtype=jnp.float32)[:, None] / NX
    col_pos = jnp.arange(NY, dtype=jnp.float32)[None, :] / NY
    numbers = jax.random.randint(key_waves, (3, 2), 1, 4).astype(jnp.float32)
    phases = jax.random.uniform(key_phase, (3,), minval=0.0, maxval=2.0 * math.pi)
    smooth = jnp.zeros((NX, NY), jnp.float32)
    for wave in range(3):
        smooth = smooth + jnp.sin(2.0 * math.pi * (numbers[wave, 0] * row_pos + numbers[wave, 1] * col_pos) + phases[wave])
    jagged = jnp.clip(jax.random.normal(key_rough, (NX, NY)), -4.0, 4.0)
    return (jagged + smooth).astype(jnp.float32)


def draw_aggregate_id(key, part):
    labels = jax.random.permutation(jax.random.fold_in(key, 21), NAGG).astype(jnp.int32)
    run_index = jnp.arange(NX // TILE * (NY // TILE), dtype=jnp.int32) // PER
    return labels[run_index].reshape(NX // TILE, NY // TILE).astype(jnp.int32)


def draw_coarse_inverse(key, part):
    key_diag = jax.random.fold_in(key, 31)
    key_off = jax.random.fold_in(key, 32)
    diag_part = jax.random.uniform(key_diag, (NAGG,), minval=0.5, maxval=1.5)
    off_part = jnp.clip(jax.random.normal(key_off, (NAGG, NAGG)), -4.0, 4.0) * (0.5 / math.sqrt(NAGG))
    return ((off_part + jnp.diag(diag_part)) / CELLS_AGG).astype(jnp.float32)


def with_ends(values, stream_key, smallest, top_value):
    shape = values.shape
    index_at = [jax.random.randint(jax.random.fold_in(stream_key, axis), (), 0, shape[axis]) for axis in range(len(shape))]
    values = values.at[tuple(index_at)].set(smallest)
    longest = shape.index(max(shape))
    index_at[longest] = (index_at[longest] + 1) % shape[longest]
    return values.at[tuple(index_at)].set(top_value)


def levels(stream_key, extent, split, smallest, high):
    loudness = 1.0
    for axis_at, blocks in split:
        heights = jax.random.uniform(jax.random.fold_in(jax.random.fold_in(stream_key, 6), axis_at), (blocks,), jnp.float32, smallest / len(split), high / len(split))
        loudness = loudness * jnp.repeat(jnp.exp(heights), extent[axis_at] // blocks).reshape((-1,) + (1,) * (len(extent) - 1 - axis_at))
    return loudness


def setup_inputs(seed: int = 0) -> dict:
    arg_keys = jax.random.split(jax.random.key(seed), 6)
    forcing = draw_forcing(jax.random.fold_in(arg_keys[5], 71), 0)
    bathymetry = jnp.clip(jnp.exp(math.log(10.0) - 4.6051702 * jax.random.uniform(arg_keys[1], (NX, NY), jnp.float32) ** levels(arg_keys[1], (NX, NY), ((0, 8), (1, 16)), -0.2, 0.2)), 0.1, 10.0)
    ocean_mask = with_ends((jax.random.randint(arg_keys[2], (NX, NY), 0, 10) < 9).astype(jnp.int32), jax.random.fold_in(arg_keys[2], 1), 0, 1)
    aggregate_id = draw_aggregate_id(jax.random.fold_in(arg_keys[5], 71), 0)
    coarse_inverse = draw_coarse_inverse(jax.random.fold_in(arg_keys[5], 71), 0)
    return {"forcing": forcing, "bathymetry": bathymetry, "ocean_mask": ocean_mask, "aggregate_id": aggregate_id, "coarse_inverse": coarse_inverse}


highest = lax.Precision.HIGHEST
SHIFT_REL = 0.001

def face_coefficients(wet_padded):
    row_faces = jnp.minimum(wet_padded[1:, :], wet_padded[:-1, :])
    col_faces = jnp.minimum(wet_padded[:, 1:], wet_padded[:, :-1])
    return (row_faces, col_faces)

def operate(padded, row_faces, col_faces):
    row_flux = row_faces * (padded[1:, :] - padded[:-1, :])
    col_flux = col_faces * (padded[:, 1:] - padded[:, :-1])
    centre = padded[1:-1, 1:-1]
    return centre - row_flux[1:, 1:-1] + row_flux[:-1, 1:-1] - col_flux[1:-1, 1:] + col_flux[1:-1, :-1]

def change_matrix(spectral_shift):
    row_ids = jnp.arange(KB + 1)[:, None]
    col_ids = jnp.arange(KB)[None, :]
    below = jnp.where(col_ids == 0, 1.0, 0.5)
    values = jnp.where(row_ids == col_ids, 1.0, jnp.where(row_ids == col_ids + 1, below, jnp.where(row_ids == col_ids - 1, 0.5, 0.0)))
    return spectral_shift * values.astype(jnp.float32)

def lower_factor(matrix):
    order = matrix.shape[0]
    row_ids = jnp.arange(order)
    factor = jnp.zeros_like(matrix)
    for column in range(order):
        reduced = matrix[:, column] - lax.optimization_barrier(jnp.sum(factor[:, :column] * factor[column, :column][None, :], axis=1))
        pivot = jnp.sqrt(reduced[column])
        entries = jnp.where(row_ids >= column, reduced / pivot, 0.0)
        factor = factor.at[:, column].set(entries)
    return factor

def upper_solve(triangle, right):
    order = triangle.shape[0]
    solved = jnp.zeros_like(right)
    for row in range(order - 1, -1, -1):
        rest = jnp.sum(triangle[row, row + 1:] * solved[row + 1:])
        solved = solved.at[row].set((right[row] - rest) / triangle[row, row])
    return solved

def small_solve(gram, spectral_shift):
    shifted = gram + SHIFT_REL * jnp.diag(jnp.diagonal(gram))
    chol_lower = lower_factor(shifted)
    chol_upper = chol_lower.T
    change = change_matrix(spectral_shift)
    projected = jnp.dot(chol_upper, change, precision=highest)
    target = chol_upper[:, 0]
    ortho_list = []
    triangle = jnp.zeros((KB, KB), jnp.float32)
    for column in range(KB):
        vector = projected[:, column]
        for passes in range(2):
            if column > 0:
                earlier_cols = jnp.stack(ortho_list, axis=1)
                amounts = jnp.dot(earlier_cols.T, vector, precision=highest)
                triangle = triangle.at[:column, column].add(amounts)
                vector = vector - jnp.dot(earlier_cols, amounts, precision=highest)
        length = jnp.sqrt(jnp.sum(vector * vector))
        triangle = triangle.at[column, column].set(length)
        ortho_list.append(vector / length)
    ortho_cols = jnp.stack(ortho_list, axis=1)
    small_rhs = jnp.dot(ortho_cols.T, target, precision=highest)
    weights = upper_solve(triangle, small_rhs)
    combined = jnp.dot(change, weights, precision=highest)
    return (weights, combined)

def reference(forcing, bathymetry, ocean_mask, aggregate_id, coarse_inverse):
    ocean = ocean_mask.astype(jnp.float32)
    wet_depth = bathymetry * ocean
    row_faces, col_faces = face_coefficients(jnp.pad(wet_depth, 1))
    diagonal = 1.0 + row_faces[1:, 1:-1] + row_faces[:-1, 1:-1] + col_faces[1:-1, 1:] + col_faces[1:-1, :-1]
    spectral_shift = jnp.max(diagonal)
    tile_index = aggregate_id.reshape(-1)

    def collect(field):
        tiles = (field * ocean).reshape(NX // TILE, TILE, NY // TILE, TILE).sum(axis=(1, 3))
        return jax.ops.segment_sum(tiles.reshape(-1), tile_index, num_segments=NAGG)

    def expand(values):
        tiles = values[aggregate_id]
        return jnp.repeat(jnp.repeat(tiles, TILE, axis=0), TILE, axis=1) * ocean

    def apply_operator(field):
        return operate(jnp.pad(field, 1), row_faces, col_faces)
    solution = jnp.zeros_like(forcing)
    residual = forcing * ocean
    for cycle in range(CYCLES):
        coarse_values = jnp.dot(coarse_inverse, collect(residual), precision=highest)
        correction = expand(coarse_values)
        solution = solution + correction
        residual = residual - apply_operator(correction)
        krylov = [residual]
        for index in range(KB):
            current = krylov[-1]
            applied = apply_operator(current) / spectral_shift - current
            if index == 0:
                krylov.append(applied)
            else:
                krylov.append(2.0 * applied - krylov[-2])
        gram = jnp.stack([jnp.stack([jnp.sum(left * right) for right in krylov]) for left in krylov])
        weights, combined = small_solve(gram, spectral_shift)
        for index in range(KB):
            solution = solution + weights[index] * krylov[index]
        for index in range(KB + 1):
            residual = residual - combined[index] * krylov[index]
    return (solution, residual)
```

```python
import functools

import jax
import jax.numpy as jnp
from jax import lax
from jax.experimental import pallas as pl
from jax.experimental.pallas import tpu as pltpu
from jax.sharding import PartitionSpec as P

TILE = 64
KB = 8
CYCLES = 2
SHIFT_REL = 0.001
DEPTH = KB * CYCLES
LANES = 128
PAD = 8
OWN = PAD + DEPTH
ROW_STEP = 16
GROUPS = 4
MESH = pl.DeviceIdType.MESH
highest = lax.Precision.HIGHEST
SIDES = ((-1, 0), (1, 0), (0, -1), (0, 1), (-1, -1), (-1, 1), (1, -1), (1, 1))
NORTH, SOUTH, WEST, EAST, NW, NE, SW, SE = range(8)


def sub_total(x):
    for shift in (4, 2, 1):
        x = x + pltpu.roll(x, shift, 0)
    return x


def splat_sum(x):
    return jnp.broadcast_to(jnp.sum(sub_total(x), axis=1, keepdims=True), x.shape)


def fold(x):
    total = x[0:8]
    for start in range(8, x.shape[0], 8):
        total = total + x[start : start + 8]
    return total


def tall(x, rows):
    return jnp.concatenate([x] * (rows // 8), axis=0)


def small_solve(vv, vp):
    n = KB + 1
    moment = [None] * (2 * KB + 1)
    moment[0], moment[1] = vv[0], vp[1]
    for k in range(1, n):
        moment[2 * k] = 2.0 * vv[k] - vv[0]
    for k in range(2, n):
        moment[2 * k - 1] = 2.0 * vp[k] - vp[1]
    upper = [[None] * n for _ in range(n)]
    for j in range(n):
        reduced = vv[j] * (1.0 + SHIFT_REL)
        for k in range(j):
            reduced = reduced - upper[k][j] * upper[k][j]
        root = jnp.sqrt(reduced)
        upper[j][j] = root
        inverse = 1.0 / root
        for i in range(j + 1, n):
            if i - j == 1:
                entry = vp[i]
            else:
                entry = 0.5 * (moment[i + j] + moment[i - j])
            for k in range(j):
                entry = entry - upper[k][j] * upper[k][i]
            upper[j][i] = entry * inverse
    hess = [[None] * KB for _ in range(n)]
    for j in range(KB):
        below = 1.0 if j == 0 else 0.5
        for i in range(j + 2):
            entry = below * upper[i][j + 1]
            if i <= j:
                entry = entry + upper[i][j]
            if i <= j - 1:
                entry = entry + 0.5 * upper[i][j - 1]
            hess[i][j] = entry
    right = [upper[0][0]] + [None] * KB
    for j in range(KB):
        a, b = hess[j][j], hess[j + 1][j]
        inverse = 1.0 / jnp.sqrt(a * a + b * b)
        c, s = a * inverse, b * inverse
        for k in range(j, KB):
            x, y = hess[j][k], hess[j + 1][k]
            if k == j:
                hess[j][k] = c * x + s * y
            else:
                hess[j][k] = c * x + s * y
                hess[j + 1][k] = c * y - s * x
        x = right[j]
        right[j] = c * x
        right[j + 1] = -s * x
    weight = [None] * KB
    for j in range(KB - 1, -1, -1):
        rest = right[j]
        for k in range(j + 1, KB):
            rest = rest - hess[j][k] * weight[k]
        weight[j] = rest / hess[j][j]
    combined = []
    for i in range(n):
        terms = []
        if i < KB:
            terms.append(weight[i])
        if i >= 1:
            terms.append((1.0 if i == 1 else 0.5) * weight[i - 1])
        if i + 1 < KB:
            terms.append(0.5 * weight[i + 1])
        combined.append(functools.reduce(jnp.add, terms))
    return weight, combined


def kernel(
    size_x,
    size_y,
    forcing_ref,
    depth_ref,
    mask_ref,
    agg_ref,
    inverse_ref,
    inverse_smem,
    solution_ref,
    residual_ref,
    in_f,
    in_b,
    in_m,
    wet,
    ocean,
    res,
    sol,
    basis,
    k_south,
    k_north,
    k_east,
    k_west,
    centre,
    send_col,
    got_col,
    send_corner,
    got_corner,
    got_row,
    inverse_rows,
    perm_rows,
    sums,
    factors,
    first_x,
    first_y,
    max_x,
    max_y,
    coarse_x,
    coarse_y,
    gram_x,
    gram_y,
    in_sem,
    halo_send,
    halo_recv,
    phase_send,
    phase_recv,
):
    height = in_f.shape[1]
    own_panels = in_f.shape[0]
    panels = own_panels + 1
    bands = height // TILE
    n_agg = inverse_ref.shape[1]
    rows_all = wet.shape[1]
    group_rows = height // GROUPS
    edge = own_panels
    gx, gy = lax.axis_index("gx"), lax.axis_index("gy")
    first_row = (gx * size_y + gy) * bands

    loads = []
    for index, (source, target) in enumerate(((depth_ref, in_b), (mask_ref, in_m), (forcing_ref, in_f))):
        for p in range(own_panels):
            copy = pltpu.make_async_copy(
                source.at[:, pl.ds(LANES * p, LANES)], target.at[p], in_sem.at[index * own_panels + p]
            )
            copy.start()
            loads.append(copy)
    barrier = pltpu.get_barrier_semaphore()

    def peer_x(d):
        return (lax.rem(gx + d, size_x), gy)

    def peer_y(d):
        return (gx, lax.rem(gy + d, size_y))

    def neighbour(side):
        dx, dy = SIDES[side]
        return (lax.rem(gx + dx + size_x, size_x), lax.rem(gy + dy + size_y, size_y))

    for d in range(1, size_x):
        pl.semaphore_signal(barrier, inc=1, device_id=peer_x(d), device_id_type=MESH)
    for d in range(1, size_y):
        pl.semaphore_signal(barrier, inc=1, device_id=peer_y(d), device_id_type=MESH)
    for side in (NW, NE, SW, SE):
        pl.semaphore_signal(barrier, inc=1, device_id=neighbour(side), device_id_type=MESH)

    sub = lax.broadcasted_iota(jnp.int32, (8, LANES), 0)
    lane8 = lax.broadcasted_iota(jnp.int32, (8, LANES), 1)
    lane16 = lax.broadcasted_iota(jnp.int32, (ROW_STEP, LANES), 1)
    zero8 = jnp.zeros((8, LANES), jnp.float32)

    for p in range(panels):
        for start in (0, rows_all - PAD):
            wet[p, start : start + PAD, :] = zero8

    def clear(j, carry):
        for p in range(panels):
            for start in (0, rows_all - PAD):
                basis[j, p, start : start + PAD, :] = zero8
        return carry

    lax.fori_loop(0, KB + 1, clear, 0)
    sums[...] = jnp.zeros_like(sums)
    inverse_rows[...] = jnp.zeros_like(inverse_rows)
    for s in range(bands):
        for c in range(-(-n_agg // LANES)):
            width = min(LANES, n_agg - c * LANES)
            inverse_rows[s, c : c + 1, 0:width] = inverse_ref[s : s + 1, c * LANES : c * LANES + width]

    for copy in loads:
        copy.wait()

    band_sums = []
    for t in range(bands):

        def prepare(c, total, t=t):
            r = t * TILE + c * ROW_STEP
            for p in range(own_panels):
                rows = pl.ds(r, ROW_STEP)
                at = pl.ds(OWN + r, ROW_STEP)
                sea = in_m[p, rows, :].astype(jnp.float32)
                value = in_f[p, rows, :] * sea
                wet[p, at, :] = in_b[p, rows, :] * sea
                ocean[p, at, :] = sea
                res[p, at, :] = value
                total = total + fold(value * sea)
            return total

        band_sums.append(splat_sum(lax.fori_loop(0, TILE // ROW_STEP, prepare, zero8)))

    def pack(c, carry):
        r = c * ROW_STEP
        for side, p, base in ((WEST, 0, 0), (EAST, own_panels - 1, LANES - DEPTH)):
            packed = jnp.zeros((ROW_STEP, LANES), jnp.float32)
            for g in range(GROUPS):
                at = pl.ds(OWN + g * group_rows + r, ROW_STEP)
                for part, array in enumerate((wet, res)):
                    start = (2 * g + part) * DEPTH
                    moved = pltpu.roll(array[p, at, :], (start - base) % LANES, 1)
                    packed = jnp.where((lane16 >= start) & (lane16 < start + DEPTH), moved, packed)
            send_col[side - WEST, pl.ds(r, ROW_STEP), :] = packed
        return carry

    lax.fori_loop(0, group_rows // ROW_STEP, pack, 0)
    for index, side in enumerate((NW, NE, SW, SE)):
        dx, dy = SIDES[side]
        p, base = (0, 0) if dy < 0 else (own_panels - 1, LANES - DEPTH)
        start = OWN if dx < 0 else OWN + height - DEPTH
        packed = jnp.zeros((DEPTH, LANES), jnp.float32)
        for part, array in enumerate((wet, res)):
            moved = pltpu.roll(array[p, start : start + DEPTH, :], (part * DEPTH - base) % LANES, 1)
            packed = jnp.where((lane16 >= part * DEPTH) & (lane16 < (part + 1) * DEPTH), moved, packed)
        send_corner[index] = packed

    halos = []
    for side in range(8):
        if side in (NORTH, SOUTH):
            start = OWN if side == NORTH else OWN + height - DEPTH
            pairs = [
                (array.at[pl.ds(0, own_panels), pl.ds(start, DEPTH), :], got_row.at[side, part])
                for part, array in enumerate((wet, res))
            ]
        elif side in (WEST, EAST):
            pairs = [(send_col.at[side - WEST], got_col.at[side - WEST])]
        else:
            pairs = [(send_corner.at[side - NW], got_corner.at[side - NW])]
        for part, (source, target) in enumerate(pairs):
            slot = side if part == 0 else 8 + side
            halos.append(
                pltpu.make_async_remote_copy(
                    src_ref=source,
                    dst_ref=target,
                    send_sem=halo_send.at[slot],
                    recv_sem=halo_recv.at[slot],
                    device_id=neighbour(side),
                    device_id_type=MESH,
                )
            )

    def phase(buffer, index, along_x):
        size, me, peer = (size_x, gx, peer_x) if along_x else (size_y, gy, peer_y)

        def start():
            for d in range(1, size):
                pltpu.make_async_remote_copy(
                    src_ref=buffer.at[me],
                    dst_ref=buffer.at[me],
                    send_sem=phase_send.at[index],
                    recv_sem=phase_recv.at[index],
                    device_id=peer(d),
                    device_id_type=MESH,
                ).start()

        def whole():
            part = buffer.at[pl.ds(0, size - 1)]
            return pltpu.make_async_remote_copy(
                src_ref=part,
                dst_ref=part,
                send_sem=phase_send.at[index],
                recv_sem=phase_recv.at[index],
                device_id=peer(1),
                device_id_type=MESH,
            )

        return start, (lambda: whole().wait_recv()), (lambda: whole().wait_send())

    def total_of(buffer, size, *index):
        return functools.reduce(jnp.add, [buffer[(i,) + index] for i in range(size)])

    finish = []

    aggregate = sub * LANES + lane8
    by_aggregate, where_table = zero8, zero8
    for t in range(bands):
        label = agg_ref[t, 0]
        by_aggregate = jnp.where(aggregate == label, band_sums[t], by_aggregate)
        here = (sub == gx) & (lane8 == gy * bands + t)
        where_table = jnp.where(here, (label + 1).astype(jnp.float32), where_table)
    first_x[gx, 0] = by_aggregate
    first_x[gx, 1] = where_table

    pl.semaphore_wait(barrier, size_x + size_y - 2 + 4)
    for copy in halos:
        copy.start()
    start_fx, wait_fx, done_fx = phase(first_x, 0, True)
    start_fy, wait_fy, done_fy = phase(first_y, 1, False)
    start_mx, wait_mx, done_mx = phase(max_x, 2, True)
    start_my, wait_my, done_my = phase(max_y, 3, False)
    finish += [done_fx, done_fy, done_mx, done_my]
    start_fx()
    wait_fx()
    for part in range(2):
        first_y[gy, part] = total_of(first_x, size_x, part)
    start_fy()

    for copy in halos:
        copy.wait()

    east_lanes = jnp.where(gy < size_y - 1, DEPTH, 0)
    west_lane = jnp.where(gy > 0, LANES - DEPTH, LANES)
    for side, start, inside in ((SOUTH, PAD, gx > 0), (NORTH, OWN + height, gx < size_x - 1)):
        keep = jnp.where(inside, LANES, 0)
        for p in range(own_panels):
            depth = jnp.where(lane16 < keep, got_row[side, 0, p], 0.0)
            wet[p, start : start + DEPTH, :] = depth
            res[p, start : start + DEPTH, :] = jnp.where(lane16 < keep, got_row[side, 1, p], 0.0)
            ocean[p, start : start + DEPTH, :] = jnp.where(depth > 0.0, 1.0, 0.0)
        from_east, from_west = (SW, SE) if side == SOUTH else (NW, NE)
        parts = []
        for part in range(2):
            east = pltpu.roll(got_corner[from_east - NW], (-part * DEPTH) % LANES, 1)
            west = pltpu.roll(got_corner[from_west - NW], (-(part + 1) * DEPTH) % LANES, 1)
            value = jnp.where(lane16 < east_lanes, east, jnp.where(lane16 >= west_lane, west, 0.0))
            parts.append(jnp.where(inside, value, 0.0))
        wet[edge, start : start + DEPTH, :] = parts[0]
        res[edge, start : start + DEPTH, :] = parts[1]
        ocean[edge, start : start + DEPTH, :] = jnp.where(parts[0] > 0.0, 1.0, 0.0)

    def unpack(c, carry):
        r = c * ROW_STEP
        east_all = got_col[WEST - WEST, pl.ds(r, ROW_STEP), :]
        west_all = got_col[EAST - WEST, pl.ds(r, ROW_STEP), :]
        for g in range(GROUPS):
            at = pl.ds(OWN + g * group_rows + r, ROW_STEP)
            parts = []
            for part in range(2):
                start = (2 * g + part) * DEPTH
                east = pltpu.roll(east_all, (-start) % LANES, 1)
                west = pltpu.roll(west_all, (LANES - DEPTH - start) % LANES, 1)
                parts.append(
                    jnp.where(lane16 < east_lanes, east, jnp.where(lane16 >= west_lane, west, 0.0))
                )
            wet[edge, at, :] = parts[0]
            res[edge, at, :] = parts[1]
            ocean[edge, at, :] = jnp.where(parts[0] > 0.0, 1.0, 0.0)
        return carry

    lax.fori_loop(0, group_rows // ROW_STEP, unpack, 0)

    def east_west(values):
        left = [pltpu.roll(v, LANES - 1, 1) for v in values]
        right = [pltpu.roll(v, 1, 1) for v in values]
        easts = [jnp.where(lane16 == LANES - 1, left[(p + 1) % panels], left[p]) for p in range(panels)]
        wests = [jnp.where(lane16 == 0, right[p - 1], right[p]) for p in range(panels)]
        return easts, wests

    def faces(r, top):
        values = [wet[p, pl.ds(r, ROW_STEP), :] for p in range(panels)]
        easts, wests = east_west(values)
        for p in range(panels):
            at = pl.ds(r, ROW_STEP)
            south = jnp.minimum(values[p], wet[p, pl.ds(r + 1, ROW_STEP), :])
            north = jnp.minimum(values[p], wet[p, pl.ds(r - 1, ROW_STEP), :])
            east = jnp.minimum(values[p], easts[p])
            west = jnp.minimum(values[p], wests[p])
            k_south[p, at, :] = south
            k_north[p, at, :] = north
            k_east[p, at, :] = east
            k_west[p, at, :] = west
            diagonal = 1.0 + south + north + east + west
            centre[p, at, :] = diagonal
            if p < own_panels and top is not None:
                for start in range(0, ROW_STEP, 8):
                    top = jnp.maximum(top, diagonal[start : start + 8])
        return top

    top = lax.fori_loop(
        0, height // ROW_STEP, lambda c, top: faces(OWN + c * ROW_STEP, top), jnp.ones((8, LANES), jnp.float32)
    )
    max_x[gx] = top
    start_mx()
    faces(PAD, None)
    faces(OWN + height, None)

    wait_fy()
    rhs = total_of(first_y, size_y, 0)
    table = total_of(first_y, size_y, 1).astype(jnp.int32) - 1

    def spread_coarse(rhs, rows, buffer):
        tile = zero8
        for s in range(bands):
            tile = jnp.where(table == first_row + s, splat_sum(rows[s] * rhs), tile)
        buffer[gx] = tile

    spread_coarse(rhs, inverse_rows, coarse_x.at[0])
    starts = [phase(coarse_x.at[c], 4 + 2 * c, True) for c in range(CYCLES)]
    starts_y = [phase(coarse_y.at[c], 5 + 2 * c, False) for c in range(CYCLES)]
    finish += [s[2] for s in starts] + [s[2] for s in starts_y]
    starts[0][0]()

    wait_mx()
    max_y[gy] = functools.reduce(jnp.maximum, [max_x[i] for i in range(size_x)])
    start_my()

    def permute(q, carry):
        match = table == q
        return tuple(jnp.where(match, inverse_smem[s, q], carry[s]) for s in range(bands))

    permuted = lax.fori_loop(0, n_agg, permute, (zero8,) * bands, unroll=8)
    for s in range(bands):
        perm_rows[s] = permuted[s]

    starts[0][1]()
    coarse_y[0, gy] = total_of(coarse_x.at[0], size_x)
    starts_y[0][0]()
    wait_my()
    largest = functools.reduce(jnp.maximum, [max_y[i] for i in range(size_y)])
    for move in (4, 2, 1):
        largest = jnp.maximum(largest, pltpu.roll(largest, move, 0))
    shift = jnp.broadcast_to(jnp.max(largest, axis=1, keepdims=True), (8, LANES))
    scale = 2.0 / shift
    scale16 = tall(scale, ROW_STEP)

    def rescale(c, carry):
        at = pl.ds(PAD + c * ROW_STEP, ROW_STEP)
        for p in range(panels):
            for array in (k_south, k_north, k_east, k_west):
                array[p, at, :] = array[p, at, :] * scale16
            centre[p, at, :] = centre[p, at, :] * scale16 - 2.0
        return carry

    chunks_all = (rows_all - 2 * PAD) // ROW_STEP
    lax.fori_loop(0, chunks_all, rescale, 0)

    def stencil(index, r):
        at = pl.ds(r, ROW_STEP)
        values = [basis[index, p, at, :] for p in range(panels)]
        easts, wests = east_west(values)
        out = []
        for p in range(panels):
            south = basis[index, p, pl.ds(r + 1, ROW_STEP), :]
            north = basis[index, p, pl.ds(r - 1, ROW_STEP), :]
            flow = k_south[p, at, :] * south + k_north[p, at, :] * north
            flow = flow + (k_east[p, at, :] * easts[p] + k_west[p, at, :] * wests[p])
            out.append(centre[p, at, :] * values[p] - flow)
        return out, values

    shift16 = tall(shift, ROW_STEP)
    gram_phases = [(phase(gram_x.at[c], 8 + 2 * c, True), phase(gram_y.at[c], 9 + 2 * c, False)) for c in range(CYCLES)]
    finish += [p[2] for pair in gram_phases for p in pair]

    for cycle in range(CYCLES):
        starts_y[cycle][1]()
        tile = total_of(coarse_y.at[cycle], size_y)
        rows_of = {dx: sub_total(jnp.where(sub == gx + dx, tile, 0.0)) for dx in (-1, 0, 1)}

        def value_at(dx, t, dy):
            picked = jnp.where(lane8 == (gy + dy) * bands + t, rows_of[dx], 0.0)
            return jnp.broadcast_to(jnp.sum(picked, axis=1, keepdims=True), (8, LANES))

        def spread_band(dx, t, start, chunks):
            own = tall(value_at(dx, t, 0), ROW_STEP)
            side = tall(jnp.where(lane8 < LANES // 2, value_at(dx, t, 1), value_at(dx, t, -1)), ROW_STEP)

            def body(c, carry):
                at = pl.ds(start + c * ROW_STEP, ROW_STEP)
                for p in range(panels):
                    value = ocean[p, at, :] * (side if p == edge else own)
                    basis[KB, p, at, :] = value
                    if dx == 0 and p < own_panels:
                        inner = pl.ds(start - OWN + c * ROW_STEP, ROW_STEP)
                        sol[p, inner, :] = value if cycle == 0 else sol[p, inner, :] + value
                return carry

            lax.fori_loop(0, chunks, body, 0)

        spread_band(-1, bands - 1, PAD, DEPTH // ROW_STEP)
        for t in range(bands):
            spread_band(0, t, OWN + t * TILE, TILE // ROW_STEP)
        spread_band(1, 0, OWN + height, DEPTH // ROW_STEP)

        def first(r, carry):
            out, values = stencil(KB, r)
            at = pl.ds(r, ROW_STEP)
            for p in range(panels):
                v = res[p, at, :] - shift16 * (0.5 * out[p] + values[p])
                basis[0, p, at, :] = v
                if p < own_panels and carry is not None:
                    square, total = carry
                    carry = (square + fold(v * v), total + fold(v * ocean[p, at, :]))
            return carry

        first(PAD, None)
        first(OWN + height, None)
        square = zero8
        for t in range(bands):
            square, total = lax.fori_loop(
                0,
                TILE // ROW_STEP,
                lambda c, carry, t=t: first(OWN + t * TILE + c * ROW_STEP, carry),
                (square, zero8),
            )
            sums[t : t + 1, :] = jnp.sum(total, axis=0, keepdims=True)
        sums[64:65, :] = jnp.sum(square, axis=0, keepdims=True)

        def step(j, carry):
            previous = jnp.maximum(j - 2, 0)
            new_part = jnp.where(j == 1, 0.5, 1.0)
            old_part = jnp.where(j == 1, 0.0, 1.0)

            def chunk(r, carry):
                out, values = stencil(j - 1, r)
                at = pl.ds(r, ROW_STEP)
                for p in range(panels):
                    v = new_part * out[p] - old_part * basis[previous, p, at, :]
                    basis[j, p, at, :] = v
                    if p < own_panels and carry is not None:
                        square, cross, total = carry
                        carry = (
                            square + fold(v * v),
                            cross + fold(v * values[p]),
                            total + fold(v * ocean[p, at, :]),
                        )
                return carry

            chunk(PAD, None)
            chunk(OWN + height, None)
            square, cross = zero8, zero8
            for t in range(bands):
                square, cross, total = lax.fori_loop(
                    0,
                    TILE // ROW_STEP,
                    lambda c, carry, t=t: chunk(OWN + t * TILE + c * ROW_STEP, carry),
                    (square, cross, zero8),
                )
                sums[pl.ds(j * bands + t, 1), :] = jnp.sum(total, axis=0, keepdims=True)
            sums[pl.ds(64 + j, 1), :] = jnp.sum(square, axis=0, keepdims=True)
            sums[pl.ds(80 + j, 1), :] = jnp.sum(cross, axis=0, keepdims=True)
            return carry

        lax.fori_loop(1, KB + 1, step, 0)

        row = lax.dot_general(
            jnp.ones((8, LANES), jnp.float32),
            sums[...],
            (((1,), (1,)), ((), ())),
            precision=highest,
            preferred_element_type=jnp.float32,
        )
        (start_gx, wait_gx, _), (start_gy, wait_gy, _) = gram_phases[cycle]
        gram_x[cycle, gx] = jnp.where(sub == gx, row, 0.0)
        start_gx()
        wait_gx()
        gram_y[cycle, gy] = total_of(gram_x.at[cycle], size_x)
        start_gy()
        wait_gy()
        gathered = [gram_y[cycle, i] for i in range(size_y)]
        whole = sub_total(functools.reduce(jnp.add, gathered))

        def at_lane(k):
            return jnp.broadcast_to(whole[:, k : k + 1], (8, LANES))

        vv = [at_lane(64 + a) for a in range(KB + 1)]
        vp = [None] + [at_lane(80 + a) for a in range(1, KB + 1)]
        weight, combined = small_solve(vv, vp)
        for j in range(KB):
            factors[j] = weight[j] / shift
        for a in range(KB + 1):
            factors[KB + a] = combined[a]

        if cycle < CYCLES - 1:
            group = lane8 // bands
            mix = jnp.where(group == 0, 1.0, 0.0)
            for a in range(KB + 1):
                mix = jnp.where(group == a, mix - combined[a], mix)
            rhs = zero8
            for i in range(size_y):
                part = gathered[i] * jnp.where(lane8 < (KB + 1) * bands, mix, 0.0)
                move = bands
                while move < LANES:
                    part = part + pltpu.roll(part, move, 1)
                    move *= 2
                rhs = jnp.where(group == i, part, rhs)
            spread_coarse(rhs, perm_rows, coarse_x.at[cycle + 1])
            starts[cycle + 1][0]()

        w = [tall(factors[j], ROW_STEP) for j in range(KB)]
        c_all = [tall(factors[KB + a], ROW_STEP) for a in range(KB + 1)]

        def update(r, p, inner):
            at = pl.ds(r, ROW_STEP)
            values = [basis[a, p, at, :] for a in range(KB + 1)]
            residual = values[0]
            for a in range(KB + 1):
                residual = residual - c_all[a] * values[a]
            if inner is None:
                res[p, at, :] = residual
                return
            rows = pl.ds(inner, ROW_STEP)
            answer = sol[p, rows, :]
            for j in range(KB):
                answer = answer + w[j] * values[j]
            if cycle < CYCLES - 1:
                res[p, at, :] = residual
                sol[p, rows, :] = answer
            else:
                columns = pl.ds(p * LANES, LANES)
                residual_ref[rows, columns] = residual
                solution_ref[rows, columns] = answer

        def update_own(c, carry):
            for p in range(own_panels):
                update(OWN + c * ROW_STEP, p, c * ROW_STEP)
            if cycle < CYCLES - 1:
                update(OWN + c * ROW_STEP, edge, None)
            return carry

        lax.fori_loop(0, height // ROW_STEP, update_own, 0)
        if cycle < CYCLES - 1:
            for p in range(panels):
                update(PAD, p, None)
                update(OWN + height, p, None)
            starts[cycle + 1][1]()
            coarse_y[cycle + 1, gy] = total_of(coarse_x.at[cycle + 1], size_x)
            starts_y[cycle + 1][0]()

    for done in finish:
        done()


def on_device(size_x, size_y, forcing, bathymetry, ocean_mask, aggregate_id, coarse_inverse):
    height, breadth = forcing.shape
    own_panels = breadth // LANES
    panels = own_panels + 1
    rows = height + 2 * (DEPTH + PAD)
    bands = height // TILE
    f32 = jnp.float32
    field = pltpu.VMEM((panels, rows, LANES), f32)
    block = pltpu.VMEM((own_panels, height, LANES), f32)
    any_spec = pl.BlockSpec(memory_space=pl.ANY)
    vmem = pl.BlockSpec(memory_space=pltpu.VMEM)
    smem = pl.BlockSpec(memory_space=pltpu.SMEM)
    tiles = lambda *lead: pltpu.VMEM(lead + (8, LANES), f32)
    dma = pltpu.SemaphoreType.DMA
    return pl.pallas_call(
        functools.partial(kernel, size_x, size_y),
        out_shape=(jax.ShapeDtypeStruct((height, breadth), f32),) * 2,
        in_specs=[any_spec, any_spec, any_spec, smem, vmem, smem],
        out_specs=(vmem, vmem),
        scratch_shapes=[
            block,
            block,
            pltpu.VMEM((own_panels, height, LANES), jnp.int32),
            field,
            field,
            field,
            block,
            pltpu.VMEM((KB + 1, panels, rows, LANES), f32),
            field,
            field,
            field,
            field,
            field,
            pltpu.VMEM((2, height // GROUPS, LANES), f32),
            pltpu.VMEM((2, height // GROUPS, LANES), f32),
            pltpu.VMEM((4, DEPTH, LANES), f32),
            pltpu.VMEM((4, DEPTH, LANES), f32),
            pltpu.VMEM((2, 2, own_panels, DEPTH, LANES), f32),
            tiles(bands),
            tiles(bands),
            pltpu.VMEM((LANES, LANES), f32),
            tiles(2 * KB + 1),
            tiles(size_x, 2),
            tiles(size_y, 2),
            tiles(size_x),
            tiles(size_y),
            tiles(CYCLES, size_x),
            tiles(CYCLES, size_y),
            tiles(CYCLES, size_x),
            tiles(CYCLES, size_y),
            dma((3 * own_panels,)),
            dma((10,)),
            dma((10,)),
            dma((12,)),
            dma((12,)),
        ],
        compiler_params=pltpu.CompilerParams(
            collective_id=0, has_side_effects=True, vmem_limit_bytes=48 * 1024 * 1024
        ),
    )(forcing, bathymetry, ocean_mask, aggregate_id, coarse_inverse, coarse_inverse)


def solution(mesh):
    return jax.shard_map(
        functools.partial(on_device, mesh.shape["gx"], mesh.shape["gy"]),
        mesh=mesh,
        in_specs=(
            P("gx", "gy"),
            P("gx", "gy"),
            P("gx", "gy"),
            P("gx", "gy"),
            P(("gx", "gy"), None),
        ),
        out_specs=(P("gx", "gy"), P("gx", "gy")),
        check_vma=False,
    )
```

```python
import functools

import jax
import jax.numpy as jnp
from jax import lax
from jax.experimental import pallas as pl
from jax.experimental.pallas import tpu as pltpu
from jax.sharding import PartitionSpec as P

TILE = 64
KB = 8
CYCLES = 2
SHIFT_REL = 0.001
DEPTH = KB * CYCLES
LANES = 128
PAD = 8
OWN = PAD + DEPTH
ROW_STEP = 16
GROUPS = 4
FIRST = 20
MESH = pl.DeviceIdType.MESH
highest = lax.Precision.HIGHEST
SIDES = ((-1, 0), (1, 0), (0, -1), (0, 1), (-1, -1), (-1, 1), (1, -1), (1, 1))
NORTH, SOUTH, WEST, EAST, NW, NE, SW, SE = range(8)


def sub_total(x):
    for shift in (4, 2, 1):
        x = x + pltpu.roll(x, shift, 0)
    return x


def splat_sum(x):
    return jnp.broadcast_to(jnp.sum(sub_total(x), axis=1, keepdims=True), x.shape)


def fold(x):
    total = x[0:8]
    for start in range(8, x.shape[0], 8):
        total = total + x[start : start + 8]
    return total


def tall(x, rows):
    return jnp.concatenate([x] * (rows // 8), axis=0)


def split(x):
    high = x.astype(jnp.bfloat16)
    return high, (x - high.astype(jnp.float32)).astype(jnp.bfloat16)


def placed(x, chooser):
    high, low = split(x)
    return jnp.dot(high, chooser, preferred_element_type=jnp.float32) + jnp.dot(
        low, chooser, preferred_element_type=jnp.float32
    )


def small_solve(vv, vp):
    n = KB + 1
    moment = [None] * (2 * KB + 1)
    moment[0], moment[1] = vv[0], vp[1]
    for k in range(1, n):
        moment[2 * k] = 2.0 * vv[k] - vv[0]
    for k in range(2, n):
        moment[2 * k - 1] = 2.0 * vp[k] - vp[1]
    upper = [[None] * n for _ in range(n)]
    for j in range(n):
        reduced = vv[j] * (1.0 + SHIFT_REL)
        for k in range(j):
            reduced = reduced - upper[k][j] * upper[k][j]
        root = jnp.sqrt(reduced)
        upper[j][j] = root
        inverse = 1.0 / root
        for i in range(j + 1, n):
            if i - j == 1:
                entry = vp[i]
            else:
                entry = 0.5 * (moment[i + j] + moment[i - j])
            for k in range(j):
                entry = entry - upper[k][j] * upper[k][i]
            upper[j][i] = entry * inverse
    hess = [[None] * KB for _ in range(n)]
    for j in range(KB):
        below = 1.0 if j == 0 else 0.5
        for i in range(j + 2):
            entry = below * upper[i][j + 1]
            if i <= j:
                entry = entry + upper[i][j]
            if i <= j - 1:
                entry = entry + 0.5 * upper[i][j - 1]
            hess[i][j] = entry
    right = [upper[0][0]] + [None] * KB
    for j in range(KB):
        a, b = hess[j][j], hess[j + 1][j]
        inverse = 1.0 / jnp.sqrt(a * a + b * b)
        c, s = a * inverse, b * inverse
        for k in range(j, KB):
            x, y = hess[j][k], hess[j + 1][k]
            if k == j:
                hess[j][k] = c * x + s * y
            else:
                hess[j][k] = c * x + s * y
                hess[j + 1][k] = c * y - s * x
        x = right[j]
        right[j] = c * x
        right[j + 1] = -s * x
    weight = [None] * KB
    for j in range(KB - 1, -1, -1):
        rest = right[j]
        for k in range(j + 1, KB):
            rest = rest - hess[j][k] * weight[k]
        weight[j] = rest / hess[j][j]
    combined = []
    for i in range(n):
        terms = []
        if i < KB:
            terms.append(weight[i])
        if i >= 1:
            terms.append((1.0 if i == 1 else 0.5) * weight[i - 1])
        if i + 1 < KB:
            terms.append(0.5 * weight[i + 1])
        combined.append(functools.reduce(jnp.add, terms))
    return weight, combined


def kernel(
    size_x,
    size_y,
    forcing_ref,
    depth_ref,
    mask_ref,
    agg_ref,
    inverse_ref,
    inverse_smem,
    solution_ref,
    residual_ref,
    in_f,
    in_b,
    in_m,
    side_w,
    side_r,
    chooser,
    back,
    wet,
    ocean,
    res,
    sol,
    basis,
    even,
    odd,
    k_south,
    k_north,
    k_east,
    k_west,
    centre,
    send_col,
    got_col,
    send_corner,
    got_corner,
    got_row,
    inverse_rows,
    perm_rows,
    sums,
    factors,
    first_x,
    first_y,
    max_x,
    max_y,
    coarse_x,
    coarse_y,
    gram_x,
    gram_y,
    in_sem,
    halo_send,
    halo_recv,
    phase_send,
    phase_recv,
):
    height, breadth = in_f.shape
    own_panels = breadth // LANES
    panels = own_panels + 1
    bands = height // TILE
    n_agg = inverse_ref.shape[1]
    rows_all = wet.shape[1]
    group_rows = height // GROUPS
    gx, gy = lax.axis_index("gx"), lax.axis_index("gy")
    first_row = (gx * size_y + gy) * bands

    loads = []
    for index, (source, target) in enumerate(((depth_ref, in_b), (mask_ref, in_m), (forcing_ref, in_f))):
        copy = pltpu.make_async_copy(source, target, in_sem.at[index])
        copy.start()
        loads.append(copy)
    barrier = pltpu.get_barrier_semaphore()

    def peer_x(d):
        return (lax.rem(gx + d, size_x), gy)

    def peer_y(d):
        return (gx, lax.rem(gy + d, size_y))

    def neighbour(side):
        dx, dy = SIDES[side]
        return (lax.rem(gx + dx + size_x, size_x), lax.rem(gy + dy + size_y, size_y))

    for d in range(1, size_x):
        pl.semaphore_signal(barrier, inc=1, device_id=peer_x(d), device_id_type=MESH)
    for d in range(1, size_y):
        pl.semaphore_signal(barrier, inc=1, device_id=peer_y(d), device_id_type=MESH)
    for side in (NW, NE, SW, SE):
        pl.semaphore_signal(barrier, inc=1, device_id=neighbour(side), device_id_type=MESH)

    sub = lax.broadcasted_iota(jnp.int32, (8, LANES), 0)
    lane8 = lax.broadcasted_iota(jnp.int32, (8, LANES), 1)
    lane16 = lax.broadcasted_iota(jnp.int32, (ROW_STEP, LANES), 1)
    zero8 = jnp.zeros((8, LANES), jnp.float32)

    for p in range(panels):
        for start in (0, rows_all - PAD):
            for array in (wet, even, odd):
                array[p, start : start + PAD, :] = zero8
    sums[...] = jnp.zeros_like(sums)
    inverse_rows[...] = jnp.zeros_like(inverse_rows)
    for s in range(bands):
        for c in range(-(-n_agg // LANES)):
            width = min(LANES, n_agg - c * LANES)
            inverse_rows[s, c : c + 1, 0:width] = inverse_ref[s : s + 1, c * LANES : c * LANES + width]

    def place(rows, columns, column_base, transposed):
        line = lax.broadcasted_iota(jnp.int32, (rows, columns), 1 if transposed else 0) + column_base
        spot = lax.broadcasted_iota(jnp.int32, (rows, columns), 0 if transposed else 1)
        return jnp.where(line < breadth + LANES // 2, line, line - panels * LANES) + FIRST, spot

    def choose(c, carry):
        rows = pl.ds(c * 16, 16)
        for p in range(panels):
            goal, lane = place(16, LANES, c * 16, False)
            chooser[rows, p * LANES : (p + 1) * LANES] = jnp.where(goal == lane * panels + p, 1.0, 0.0).astype(
                jnp.bfloat16
            )
        return carry

    lax.fori_loop(0, panels * LANES // 16, choose, 0)

    for copy in loads:
        copy.wait()

    band_sums = []
    for t in range(bands):

        def prepare(c, total, t=t):
            rows = pl.ds(t * TILE + c * ROW_STEP, ROW_STEP)
            for p in range(own_panels):
                at = pl.ds(p * LANES, LANES)
                sea = in_m[rows, at].astype(jnp.float32)
                value = in_f[rows, at] * sea
                in_b[rows, at] = in_b[rows, at] * sea
                in_f[rows, at] = value
                total = total + fold(value * sea)
            return total

        band_sums.append(splat_sum(lax.fori_loop(0, TILE // ROW_STEP, prepare, zero8)))

    def pack(c, carry):
        r = c * ROW_STEP
        for side, p, base in ((WEST, 0, 0), (EAST, own_panels - 1, LANES - DEPTH)):
            packed = jnp.zeros((ROW_STEP, LANES), jnp.float32)
            for g in range(GROUPS):
                at = pl.ds(g * group_rows + r, ROW_STEP)
                for part, array in enumerate((in_b, in_f)):
                    start = (2 * g + part) * DEPTH
                    moved = pltpu.roll(array[at, p * LANES : (p + 1) * LANES], (start - base) % LANES, 1)
                    packed = jnp.where((lane16 >= start) & (lane16 < start + DEPTH), moved, packed)
            send_col[side - WEST, pl.ds(r, ROW_STEP), :] = packed
        return carry

    lax.fori_loop(0, group_rows // ROW_STEP, pack, 0)
    for index, side in enumerate((NW, NE, SW, SE)):
        dx, dy = SIDES[side]
        p, base = (0, 0) if dy < 0 else (own_panels - 1, LANES - DEPTH)
        start = 0 if dx < 0 else height - DEPTH
        packed = jnp.zeros((DEPTH, LANES), jnp.float32)
        for part, array in enumerate((in_b, in_f)):
            corner = array[start : start + DEPTH, p * LANES : (p + 1) * LANES]
            moved = pltpu.roll(corner, (part * DEPTH - base) % LANES, 1)
            packed = jnp.where((lane16 >= part * DEPTH) & (lane16 < (part + 1) * DEPTH), moved, packed)
        send_corner[index] = packed

    halos = []
    for side in range(8):
        if side in (NORTH, SOUTH):
            start = 0 if side == NORTH else height - DEPTH
            pairs = [
                (array.at[pl.ds(start, DEPTH), :], got_row.at[side, part]) for part, array in enumerate((in_b, in_f))
            ]
        elif side in (WEST, EAST):
            pairs = [(send_col.at[side - WEST], got_col.at[side - WEST])]
        else:
            pairs = [(send_corner.at[side - NW], got_corner.at[side - NW])]
        for part, (source, target) in enumerate(pairs):
            slot = side if part == 0 else 8 + side
            halos.append(
                pltpu.make_async_remote_copy(
                    src_ref=source,
                    dst_ref=target,
                    send_sem=halo_send.at[slot],
                    recv_sem=halo_recv.at[slot],
                    device_id=neighbour(side),
                    device_id_type=MESH,
                )
            )

    def phase(buffer, index, along_x):
        size, me, peer = (size_x, gx, peer_x) if along_x else (size_y, gy, peer_y)

        def start():
            for d in range(1, size):
                pltpu.make_async_remote_copy(
                    src_ref=buffer.at[me],
                    dst_ref=buffer.at[me],
                    send_sem=phase_send.at[index],
                    recv_sem=phase_recv.at[index],
                    device_id=peer(d),
                    device_id_type=MESH,
                ).start()

        def whole():
            part = buffer.at[pl.ds(0, size - 1)]
            return pltpu.make_async_remote_copy(
                src_ref=part,
                dst_ref=part,
                send_sem=phase_send.at[index],
                recv_sem=phase_recv.at[index],
                device_id=peer(1),
                device_id_type=MESH,
            )

        return start, (lambda: whole().wait_recv()), (lambda: whole().wait_send())

    def total_of(buffer, size, *index):
        return functools.reduce(jnp.add, [buffer[(i,) + index] for i in range(size)])

    finish = []

    aggregate = sub * LANES + lane8
    by_aggregate, where_table = zero8, zero8
    for t in range(bands):
        label = agg_ref[t, 0]
        by_aggregate = jnp.where(aggregate == label, band_sums[t], by_aggregate)
        here = (sub == gx) & (lane8 == gy * bands + t)
        where_table = jnp.where(here, (label + 1).astype(jnp.float32), where_table)
    first_x[gx, 0] = by_aggregate
    first_x[gx, 1] = where_table

    pl.semaphore_wait(barrier, size_x + size_y - 2 + 4)
    for copy in halos:
        copy.start()
    start_fx, wait_fx, done_fx = phase(first_x, 0, True)
    start_fy, wait_fy, done_fy = phase(first_y, 1, False)
    start_mx, wait_mx, done_mx = phase(max_x, 2, True)
    start_my, wait_my, done_my = phase(max_y, 3, False)
    finish += [done_fx, done_fy, done_mx, done_my]
    start_fx()

    own_rows = pl.ds(0, breadth)
    block_rows = 64

    def settle(c, carry):
        rows = pl.ds(c * block_rows, block_rows)
        for source, target in ((in_b, wet), (in_f, res)):
            moved = placed(source[rows, :], chooser[own_rows, :])
            for p in range(panels):
                target[p, pl.ds(OWN + c * block_rows, block_rows), :] = moved[:, p * LANES : (p + 1) * LANES]
        return carry

    lax.fori_loop(0, height // block_rows, settle, 0)

    wait_fx()
    for part in range(2):
        first_y[gy, part] = total_of(first_x, size_x, part)
    start_fy()

    for copy in halos:
        copy.wait()

    east_lanes = jnp.where(gy < size_y - 1, DEPTH, 0)
    west_lane = jnp.where(gy > 0, LANES - DEPTH, LANES)
    for side, start, inside in ((SOUTH, PAD, gx > 0), (NORTH, OWN + height, gx < size_x - 1)):
        from_east, from_west = (SW, SE) if side == SOUTH else (NW, NE)
        for part, target in enumerate((wet, res)):
            east = pltpu.roll(got_corner[from_east - NW], (-part * DEPTH) % LANES, 1)
            west = pltpu.roll(got_corner[from_west - NW], (-(part + 1) * DEPTH) % LANES, 1)
            corner = jnp.where(lane16 < east_lanes, east, jnp.where(lane16 >= west_lane, west, 0.0))
            whole_row = jnp.concatenate([got_row[side, part], corner], axis=1)
            moved = placed(jnp.where(inside, whole_row, 0.0), chooser[...])
            for p in range(panels):
                target[p, start : start + DEPTH, :] = moved[:, p * LANES : (p + 1) * LANES]

    def unpack(c, carry):
        r = c * ROW_STEP
        east_all = got_col[WEST - WEST, pl.ds(r, ROW_STEP), :]
        west_all = got_col[EAST - WEST, pl.ds(r, ROW_STEP), :]
        for g in range(GROUPS):
            for part, target in enumerate((side_w, side_r)):
                start = (2 * g + part) * DEPTH
                east = pltpu.roll(east_all, (-start) % LANES, 1)
                west = pltpu.roll(west_all, (LANES - DEPTH - start) % LANES, 1)
                target[pl.ds(g * group_rows + r, ROW_STEP), :] = jnp.where(
                    lane16 < east_lanes, east, jnp.where(lane16 >= west_lane, west, 0.0)
                )
        return carry

    lax.fori_loop(0, group_rows // ROW_STEP, unpack, 0)

    def settle_sides(c, carry):
        rows = pl.ds(c * block_rows, block_rows)
        at = pl.ds(OWN + c * block_rows, block_rows)
        for source, target in ((side_w, wet), (side_r, res)):
            moved = placed(source[rows, :], chooser[pl.ds(breadth, LANES), :])
            for p in range(panels):
                target[p, at, :] = target[p, at, :] + moved[:, p * LANES : (p + 1) * LANES]
        return carry

    lax.fori_loop(0, height // block_rows, settle_sides, 0)

    def east_west(values):
        easts = values[1:] + [pltpu.roll(values[0], LANES - 1, 1)]
        wests = [pltpu.roll(values[-1], 1, 1)] + values[:-1]
        return easts, wests

    last, extra = divmod(breadth + FIRST, panels)
    first_lane = FIRST // panels

    def own_lanes(x, p):
        lane = lax.broadcasted_iota(jnp.int32, x.shape, 1)
        return (lane >= first_lane) & (lane < last + (1 if p < extra else 0))

    def kind(p):
        return 0 if p < extra else 1

    def own_total(parts):
        return jnp.where(own_lanes(parts[0], 0), parts[0], 0.0) + jnp.where(
            own_lanes(parts[1], panels - 1), parts[1], 0.0
        )

    def add_to(pair, p, x):
        return tuple(total + x if i == kind(p) else total for i, total in enumerate(pair))

    zero_pair = (zero8, zero8)

    def faces(r, top):
        values = [wet[p, pl.ds(r, ROW_STEP), :] for p in range(panels)]
        easts, wests = east_west(values)
        for p in range(panels):
            at = pl.ds(r, ROW_STEP)
            south = jnp.minimum(values[p], wet[p, pl.ds(r + 1, ROW_STEP), :])
            north = jnp.minimum(values[p], wet[p, pl.ds(r - 1, ROW_STEP), :])
            east = jnp.minimum(values[p], easts[p])
            west = jnp.minimum(values[p], wests[p])
            k_south[p, at, :] = south
            k_north[p, at, :] = north
            k_east[p, at, :] = east
            k_west[p, at, :] = west
            diagonal = 1.0 + south + north + east + west
            centre[p, at, :] = diagonal
            ocean[p, at, :] = jnp.where(values[p] > 0.0, 1.0, 0.0)
            if top is not None:
                for start in range(0, ROW_STEP, 8):
                    part = diagonal[start : start + 8]
                    top = tuple(jnp.maximum(t, part) if i == kind(p) else t for i, t in enumerate(top))
        return top

    top = lax.fori_loop(
        0, height // ROW_STEP, lambda c, top: faces(OWN + c * ROW_STEP, top), (jnp.ones((8, LANES), jnp.float32),) * 2
    )
    max_x[gx] = jnp.maximum(
        jnp.where(own_lanes(top[0], 0), top[0], 1.0), jnp.where(own_lanes(top[1], panels - 1), top[1], 1.0)
    )
    start_mx()
    faces(PAD, None)
    faces(OWN + height, None)

    wait_fy()
    rhs = total_of(first_y, size_y, 0)
    table = total_of(first_y, size_y, 1).astype(jnp.int32) - 1

    def spread_coarse(rhs, rows, buffer):
        tile = zero8
        for s in range(bands):
            tile = jnp.where(table == first_row + s, splat_sum(rows[s] * rhs), tile)
        buffer[gx] = tile

    spread_coarse(rhs, inverse_rows, coarse_x.at[0])
    starts = [phase(coarse_x.at[c], 4 + 2 * c, True) for c in range(CYCLES)]
    starts_y = [phase(coarse_y.at[c], 5 + 2 * c, False) for c in range(CYCLES)]
    finish += [s[2] for s in starts] + [s[2] for s in starts_y]
    starts[0][0]()

    wait_mx()
    max_y[gy] = functools.reduce(jnp.maximum, [max_x[i] for i in range(size_x)])
    start_my()

    def permute(q, carry):
        match = table == q
        return tuple(jnp.where(match, inverse_smem[s, q], carry[s]) for s in range(bands))

    permuted = lax.fori_loop(0, n_agg, permute, (zero8,) * bands, unroll=8)
    for s in range(bands):
        perm_rows[s] = permuted[s]

    starts[0][1]()
    coarse_y[0, gy] = total_of(coarse_x.at[0], size_x)
    starts_y[0][0]()
    wait_my()
    largest = functools.reduce(jnp.maximum, [max_y[i] for i in range(size_y)])
    for move in (4, 2, 1):
        largest = jnp.maximum(largest, pltpu.roll(largest, move, 0))
    shift = jnp.broadcast_to(jnp.max(largest, axis=1, keepdims=True), (8, LANES))
    scale = 2.0 / shift
    scale16 = tall(scale, ROW_STEP)

    def rescale(c, carry):
        at = pl.ds(PAD + c * ROW_STEP, ROW_STEP)
        for p in range(panels):
            for array in (k_south, k_north, k_east, k_west):
                array[p, at, :] = array[p, at, :] * scale16
            centre[p, at, :] = centre[p, at, :] * scale16 - 2.0
        return carry

    chunks_all = (rows_all - 2 * PAD) // ROW_STEP
    lax.fori_loop(0, chunks_all, rescale, 0)

    def stencil(array, r):
        at = pl.ds(r, ROW_STEP)
        values = [array[p, at, :] for p in range(panels)]
        easts, wests = east_west(values)
        out = []
        for p in range(panels):
            south = array[p, pl.ds(r + 1, ROW_STEP), :]
            north = array[p, pl.ds(r - 1, ROW_STEP), :]
            flow = k_south[p, at, :] * south + k_north[p, at, :] * north
            flow = flow + (k_east[p, at, :] * easts[p] + k_west[p, at, :] * wests[p])
            out.append(centre[p, at, :] * values[p] - flow)
        return out, values

    def over_bands(chunk, first_sums, run):
        chunk(PAD, None)
        chunk(OWN + height, None)

        def band(t, carry):
            carry = carry + (zero_pair,)
            for c in range(TILE // ROW_STEP):
                carry = chunk(pl.multiple_of(OWN + t * TILE + c * ROW_STEP, 8), carry)
            sums[pl.ds(first_sums + t, 1), :] = jnp.sum(own_total(carry[-1]), axis=0, keepdims=True)
            return carry[:-1]

        return lax.fori_loop(0, bands, band, run)

    shift16 = tall(shift, ROW_STEP)
    gram_phases = [(phase(gram_x.at[c], 8 + 2 * c, True), phase(gram_y.at[c], 9 + 2 * c, False)) for c in range(CYCLES)]
    finish += [p[2] for pair in gram_phases for p in pair]

    for cycle in range(CYCLES):
        starts_y[cycle][1]()
        tile = total_of(coarse_y.at[cycle], size_y)
        rows_of = {dx: sub_total(jnp.where(sub == gx + dx, tile, 0.0)) for dx in (-1, 0, 1)}

        def value_at(dx, t, dy):
            picked = jnp.where(lane8 == (gy + dy) * bands + t, rows_of[dx], 0.0)
            return jnp.broadcast_to(jnp.sum(picked, axis=1, keepdims=True), (8, LANES))

        def spread_band(dx, t, start, chunks):
            own, east, west = (value_at(dx, t, dy) for dy in (0, 1, -1))
            side = jnp.where(lane8 < LANES // 2, west, east)
            values = [tall(jnp.where(own_lanes(own, p), own, side), ROW_STEP) for p in range(panels)]

            def body(c, carry):
                at = pl.ds(start + c * ROW_STEP, ROW_STEP)
                for p in range(panels):
                    value = ocean[p, at, :] * values[p]
                    odd[p, at, :] = value
                    if dx == 0:
                        inner = pl.ds(start - OWN + c * ROW_STEP, ROW_STEP)
                        sol[p, inner, :] = value if cycle == 0 else sol[p, inner, :] + value
                return carry

            lax.fori_loop(0, chunks, body, 0)

        spread_band(-1, bands - 1, PAD, DEPTH // ROW_STEP)
        for t in range(bands):
            spread_band(0, t, OWN + t * TILE, TILE // ROW_STEP)
        spread_band(1, 0, OWN + height, DEPTH // ROW_STEP)

        def first(r, carry):
            out, values = stencil(odd, r)
            at = pl.ds(r, ROW_STEP)
            for p in range(panels):
                v = res[p, at, :] - shift16 * (0.5 * out[p] + values[p])
                even[p, at, :] = v
                basis[0, p, at, :] = v
                if carry is not None:
                    square, total = carry
                    carry = (add_to(square, p, fold(v * v)), add_to(total, p, fold(v * ocean[p, at, :])))
            return carry

        (square,) = over_bands(first, 0, (zero_pair,))
        sums[64:65, :] = jnp.sum(own_total(square), axis=0, keepdims=True)

        def step(j, source, target):
            new_part = jnp.where(j == 1, 0.5, 1.0)
            old_part = jnp.where(j == 1, 0.0, 1.0)

            def chunk(r, carry):
                out, values = stencil(source, r)
                at = pl.ds(r, ROW_STEP)
                for p in range(panels):
                    v = new_part * out[p] - old_part * target[p, at, :]
                    target[p, at, :] = v
                    basis[j, p, at, :] = v
                    if carry is not None:
                        square, cross, total = carry
                        carry = (
                            add_to(square, p, fold(v * v)),
                            add_to(cross, p, fold(v * values[p])),
                            add_to(total, p, fold(v * ocean[p, at, :])),
                        )
                return carry

            square, cross = over_bands(chunk, j * bands, (zero_pair, zero_pair))
            sums[pl.ds(64 + j, 1), :] = jnp.sum(own_total(square), axis=0, keepdims=True)
            sums[pl.ds(80 + j, 1), :] = jnp.sum(own_total(cross), axis=0, keepdims=True)

        def two_steps(i, carry):
            step(2 * i + 1, even, odd)
            step(2 * i + 2, odd, even)
            return carry

        lax.fori_loop(0, KB // 2, two_steps, 0)

        row = lax.dot_general(
            jnp.ones((8, LANES), jnp.float32),
            sums[...],
            (((1,), (1,)), ((), ())),
            precision=highest,
            preferred_element_type=jnp.float32,
        )
        (start_gx, wait_gx, _), (start_gy, wait_gy, _) = gram_phases[cycle]
        gram_x[cycle, gx] = jnp.where(sub == gx, row, 0.0)
        start_gx()
        wait_gx()
        gram_y[cycle, gy] = total_of(gram_x.at[cycle], size_x)
        start_gy()
        wait_gy()
        gathered = [gram_y[cycle, i] for i in range(size_y)]
        whole = sub_total(functools.reduce(jnp.add, gathered))

        def at_lane(k):
            return jnp.broadcast_to(whole[:, k : k + 1], (8, LANES))

        vv = [at_lane(64 + a) for a in range(KB + 1)]
        vp = [None] + [at_lane(80 + a) for a in range(1, KB + 1)]
        weight, combined = small_solve(vv, vp)
        for j in range(KB):
            factors[j] = weight[j] / shift
        for a in range(KB + 1):
            factors[KB + a] = combined[a]

        if cycle < CYCLES - 1:
            group = lane8 // bands
            mix = jnp.where(group == 0, 1.0, 0.0)
            for a in range(KB + 1):
                mix = jnp.where(group == a, mix - combined[a], mix)
            rhs = zero8
            for i in range(size_y):
                part = gathered[i] * jnp.where(lane8 < (KB + 1) * bands, mix, 0.0)
                move = bands
                while move < LANES:
                    part = part + pltpu.roll(part, move, 1)
                    move *= 2
                rhs = jnp.where(group == i, part, rhs)
            spread_coarse(rhs, perm_rows, coarse_x.at[cycle + 1])
            starts[cycle + 1][0]()

        w = [tall(factors[j], ROW_STEP) for j in range(KB)]
        c_all = [tall(factors[KB + a], ROW_STEP) for a in range(KB + 1)]

        def update(r, p, inner):
            at = pl.ds(r, ROW_STEP)
            values = [basis[a, p, at, :] for a in range(KB + 1)]
            residual = values[0]
            for a in range(KB + 1):
                residual = residual - c_all[a] * values[a]
            if inner is None:
                res[p, at, :] = residual
                return
            rows = pl.ds(inner, ROW_STEP)
            answer = sol[p, rows, :]
            for j in range(KB):
                answer = answer + w[j] * values[j]
            res[p, at, :] = residual
            sol[p, rows, :] = answer

        def update_own(c, carry):
            for p in range(panels):
                update(OWN + c * ROW_STEP, p, c * ROW_STEP)
            return carry

        lax.fori_loop(0, height // ROW_STEP, update_own, 0)
        if cycle < CYCLES - 1:
            for p in range(panels):
                update(PAD, p, None)
                update(OWN + height, p, None)
            starts[cycle + 1][1]()
            coarse_y[cycle + 1, gy] = total_of(coarse_x.at[cycle + 1], size_x)
            starts_y[cycle + 1][0]()

    def choose_back(c, carry):
        for p in range(panels):
            for q in range(own_panels):
                goal, lane = place(16, LANES, q * LANES, True)
                rows = pl.ds(p * LANES + c * 16, 16)
                back[rows, q * LANES : (q + 1) * LANES] = jnp.where(
                    goal == (lane + c * 16) * panels + p, 1.0, 0.0
                ).astype(jnp.bfloat16)
        return carry

    lax.fori_loop(0, LANES // 16, choose_back, 0)

    def unsettle(c, carry):
        rows = pl.ds(c * block_rows, block_rows)
        at = pl.ds(OWN + c * block_rows, block_rows)
        solution_ref[rows, :] = placed(jnp.concatenate([sol[p, rows, :] for p in range(panels)], axis=1), back[...])
        residual_ref[rows, :] = placed(jnp.concatenate([res[p, at, :] for p in range(panels)], axis=1), back[...])
        return carry

    lax.fori_loop(0, height // block_rows, unsettle, 0)

    for done in finish:
        done()


def on_device(size_x, size_y, forcing, bathymetry, ocean_mask, aggregate_id, coarse_inverse):
    height, breadth = forcing.shape
    own_panels = breadth // LANES
    panels = own_panels + 1
    rows = height + 2 * (DEPTH + PAD)
    bands = height // TILE
    f32 = jnp.float32
    field = pltpu.VMEM((panels, rows, LANES), f32)
    block = pltpu.VMEM((height, breadth), f32)
    any_spec = pl.BlockSpec(memory_space=pl.ANY)
    vmem = pl.BlockSpec(memory_space=pltpu.VMEM)
    smem = pl.BlockSpec(memory_space=pltpu.SMEM)
    tiles = lambda *lead: pltpu.VMEM(lead + (8, LANES), f32)
    dma = pltpu.SemaphoreType.DMA
    return pl.pallas_call(
        functools.partial(kernel, size_x, size_y),
        out_shape=(jax.ShapeDtypeStruct((height, breadth), f32),) * 2,
        in_specs=[any_spec, any_spec, any_spec, smem, vmem, smem],
        out_specs=(vmem, vmem),
        scratch_shapes=[
            block,
            block,
            pltpu.VMEM((height, breadth), jnp.int32),
            pltpu.VMEM((height, LANES), f32),
            pltpu.VMEM((height, LANES), f32),
            pltpu.VMEM((panels * LANES, panels * LANES), jnp.bfloat16),
            pltpu.VMEM((panels * LANES, breadth), jnp.bfloat16),
            field,
            field,
            field,
            pltpu.VMEM((panels, height, LANES), f32),
            pltpu.VMEM((KB + 1, panels, rows, LANES), f32),
            field,
            field,
            field,
            field,
            field,
            field,
            field,
            pltpu.VMEM((2, height // GROUPS, LANES), f32),
            pltpu.VMEM((2, height // GROUPS, LANES), f32),
            pltpu.VMEM((4, DEPTH, LANES), f32),
            pltpu.VMEM((4, DEPTH, LANES), f32),
            pltpu.VMEM((2, 2, DEPTH, breadth), f32),
            tiles(bands),
            tiles(bands),
            pltpu.VMEM((LANES, LANES), f32),
            tiles(2 * KB + 1),
            tiles(size_x, 2),
            tiles(size_y, 2),
            tiles(size_x),
            tiles(size_y),
            tiles(CYCLES, size_x),
            tiles(CYCLES, size_y),
            tiles(CYCLES, size_x),
            tiles(CYCLES, size_y),
            dma((3,)),
            dma((10,)),
            dma((10,)),
            dma((12,)),
            dma((12,)),
        ],
        compiler_params=pltpu.CompilerParams(
            collective_id=0, has_side_effects=True, vmem_limit_bytes=60 * 1024 * 1024
        ),
    )(forcing, bathymetry, ocean_mask, aggregate_id, coarse_inverse, coarse_inverse)


def solution(mesh):
    return jax.shard_map(
        functools.partial(on_device, mesh.shape["gx"], mesh.shape["gy"]),
        mesh=mesh,
        in_specs=(
            P("gx", "gy"),
            P("gx", "gy"),
            P("gx", "gy"),
            P("gx", "gy"),
            P(("gx", "gy"), None),
        ),
        out_specs=(P("gx", "gy"), P("gx", "gy")),
        check_vma=False,
    )
```

```python
import functools

import jax
import jax.numpy as jnp
from jax import lax
from jax.experimental import pallas as pl
from jax.experimental.pallas import tpu as pltpu
from jax.sharding import PartitionSpec as P

TILE = 64
KB = 8
CYCLES = 2
SHIFT_REL = 0.001
DEPTH = KB * CYCLES
LANES = 128
PAD = 8
OWN = PAD + DEPTH
ROW_STEP = 16
GROUPS = 4
FIRST = 20
MESH = pl.DeviceIdType.MESH
highest = lax.Precision.HIGHEST
SIDES = ((-1, 0), (1, 0), (0, -1), (0, 1), (-1, -1), (-1, 1), (1, -1), (1, 1))
NORTH, SOUTH, WEST, EAST, NW, NE, SW, SE = range(8)


def sub_total(x):
    for shift in (4, 2, 1):
        x = x + pltpu.roll(x, shift, 0)
    return x


def splat_sum(x):
    return jnp.broadcast_to(jnp.sum(sub_total(x), axis=1, keepdims=True), x.shape)


def fold(x):
    total = x[0:8]
    for start in range(8, x.shape[0], 8):
        total = total + x[start : start + 8]
    return total


def tall(x, rows):
    return jnp.concatenate([x] * (rows // 8), axis=0)


def split(x):
    high = x.astype(jnp.bfloat16)
    return high, (x - high.astype(jnp.float32)).astype(jnp.bfloat16)


def placed(x, chooser):
    high, low = split(x)
    return jnp.dot(high, chooser, preferred_element_type=jnp.float32) + jnp.dot(
        low, chooser, preferred_element_type=jnp.float32
    )


def exact_placed(chooser, x):
    high, rest = split(x)
    low = (x - high.astype(jnp.float32) - rest.astype(jnp.float32)).astype(jnp.bfloat16)
    return sum(jnp.dot(chooser, part, preferred_element_type=jnp.float32) for part in (high, rest, low))


def exact_moved(x, chooser):
    high, rest = split(x)
    low = (x - high.astype(jnp.float32) - rest.astype(jnp.float32)).astype(jnp.bfloat16)
    return sum(jnp.dot(part, chooser, preferred_element_type=jnp.float32) for part in (high, rest, low))


def small_solve(vv, vp):
    n = KB + 1
    moment = [None] * (2 * KB + 1)
    moment[0], moment[1] = vv[0], vp[1]
    for k in range(1, n):
        moment[2 * k] = 2.0 * vv[k] - vv[0]
    for k in range(2, n):
        moment[2 * k - 1] = 2.0 * vp[k] - vp[1]
    upper = [[None] * n for _ in range(n)]
    for j in range(n):
        reduced = vv[j] * (1.0 + SHIFT_REL)
        for k in range(j):
            reduced = reduced - upper[k][j] * upper[k][j]
        root = jnp.sqrt(reduced)
        upper[j][j] = root
        inverse = 1.0 / root
        for i in range(j + 1, n):
            if i - j == 1:
                entry = vp[i]
            else:
                entry = 0.5 * (moment[i + j] + moment[i - j])
            for k in range(j):
                entry = entry - upper[k][j] * upper[k][i]
            upper[j][i] = entry * inverse
    hess = [[None] * KB for _ in range(n)]
    for j in range(KB):
        below = 1.0 if j == 0 else 0.5
        for i in range(j + 2):
            entry = below * upper[i][j + 1]
            if i <= j:
                entry = entry + upper[i][j]
            if i <= j - 1:
                entry = entry + 0.5 * upper[i][j - 1]
            hess[i][j] = entry
    right = [upper[0][0]] + [None] * KB
    for j in range(KB):
        a, b = hess[j][j], hess[j + 1][j]
        inverse = 1.0 / jnp.sqrt(a * a + b * b)
        c, s = a * inverse, b * inverse
        for k in range(j, KB):
            x, y = hess[j][k], hess[j + 1][k]
            if k == j:
                hess[j][k] = c * x + s * y
            else:
                hess[j][k] = c * x + s * y
                hess[j + 1][k] = c * y - s * x
        x = right[j]
        right[j] = c * x
        right[j + 1] = -s * x
    weight = [None] * KB
    for j in range(KB - 1, -1, -1):
        rest = right[j]
        for k in range(j + 1, KB):
            rest = rest - hess[j][k] * weight[k]
        weight[j] = rest / hess[j][j]
    combined = []
    for i in range(n):
        terms = []
        if i < KB:
            terms.append(weight[i])
        if i >= 1:
            terms.append((1.0 if i == 1 else 0.5) * weight[i - 1])
        if i + 1 < KB:
            terms.append(0.5 * weight[i + 1])
        combined.append(functools.reduce(jnp.add, terms))
    return weight, combined


def kernel(
    size_x,
    size_y,
    forcing_ref,
    depth_ref,
    mask_ref,
    agg_ref,
    inverse_ref,
    solution_ref,
    residual_ref,
    back,
    in_f,
    in_b,
    in_m,
    side_w,
    side_r,
    chooser,
    wet,
    ocean,
    res,
    sol,
    basis,
    even,
    odd,
    k_south,
    k_north,
    k_east,
    k_west,
    centre,
    send_col,
    got_col,
    send_corner,
    got_corner,
    got_row,
    inverse_rows,
    selector,
    permuted,
    bulk_x,
    bulk_y,
    sums,
    factors,
    first_x,
    first_y,
    max_x,
    max_y,
    coarse_x,
    coarse_y,
    gram_x,
    gram_y,
    in_sem,
    halo_send,
    halo_recv,
    phase_send,
    phase_recv,
):
    height, breadth = in_f.shape
    own_panels = breadth // LANES
    panels = own_panels + 1
    bands = height // TILE
    n_agg = inverse_ref.shape[1]
    rows_all = wet.shape[1]
    group_rows = height // GROUPS
    gx, gy = lax.axis_index("gx"), lax.axis_index("gy")
    first_row = (gx * size_y + gy) * bands

    loads = []
    for index, (source, target) in enumerate(
        ((depth_ref, in_b), (mask_ref, in_m), (forcing_ref, in_f), (inverse_ref, bulk_x.at[gx]))
    ):
        copy = pltpu.make_async_copy(source, target, in_sem.at[index])
        copy.start()
        loads.append(copy)
    barrier = pltpu.get_barrier_semaphore()

    def peer_x(d):
        return (lax.rem(gx + d, size_x), gy)

    def peer_y(d):
        return (gx, lax.rem(gy + d, size_y))

    def neighbour(side):
        dx, dy = SIDES[side]
        return (lax.rem(gx + dx + size_x, size_x), lax.rem(gy + dy + size_y, size_y))

    for d in range(1, size_x):
        pl.semaphore_signal(barrier, inc=1, device_id=peer_x(d), device_id_type=MESH)
    for d in range(1, size_y):
        pl.semaphore_signal(barrier, inc=1, device_id=peer_y(d), device_id_type=MESH)
    for side in (NW, NE, SW, SE):
        pl.semaphore_signal(barrier, inc=1, device_id=neighbour(side), device_id_type=MESH)

    sub = lax.broadcasted_iota(jnp.int32, (8, LANES), 0)
    lane8 = lax.broadcasted_iota(jnp.int32, (8, LANES), 1)
    lane16 = lax.broadcasted_iota(jnp.int32, (ROW_STEP, LANES), 1)
    zero8 = jnp.zeros((8, LANES), jnp.float32)

    for p in range(panels):
        for start in (0, rows_all - PAD):
            for array in (wet, even, odd):
                array[p, start : start + PAD, :] = zero8
    sums[...] = jnp.zeros_like(sums)
    def place(rows, columns, column_base, transposed):
        line = lax.broadcasted_iota(jnp.int32, (rows, columns), 1 if transposed else 0) + column_base
        spot = lax.broadcasted_iota(jnp.int32, (rows, columns), 0 if transposed else 1)
        return jnp.where(line < breadth + LANES // 2, line, line - panels * LANES) + FIRST, spot

    def choose(c, carry):
        rows = pl.ds(c * 16, 16)
        for p in range(panels):
            goal, lane = place(16, LANES, c * 16, False)
            chooser[rows, p * LANES : (p + 1) * LANES] = jnp.where(goal == lane * panels + p, 1.0, 0.0).astype(
                jnp.bfloat16
            )
        return carry

    lax.fori_loop(0, panels * LANES // 16, choose, 0)

    for copy in loads:
        copy.wait()
    inverse_rows[...] = jnp.zeros_like(inverse_rows)
    for s in range(bands):
        for c in range(-(-n_agg // LANES)):
            width = min(LANES, n_agg - c * LANES)
            inverse_rows[s, c : c + 1, 0:width] = bulk_x[gx, s : s + 1, c * LANES : c * LANES + width]

    band_sums = []
    for t in range(bands):

        def prepare(c, total, t=t):
            rows = pl.ds(t * TILE + c * ROW_STEP, ROW_STEP)
            for p in range(own_panels):
                at = pl.ds(p * LANES, LANES)
                sea = in_m[rows, at].astype(jnp.float32)
                value = in_f[rows, at] * sea
                in_b[rows, at] = in_b[rows, at] * sea
                in_f[rows, at] = value
                total = total + fold(value * sea)
            return total

        band_sums.append(splat_sum(lax.fori_loop(0, TILE // ROW_STEP, prepare, zero8)))

    def pack(c, carry):
        r = c * ROW_STEP
        for side, p, base in ((WEST, 0, 0), (EAST, own_panels - 1, LANES - DEPTH)):
            packed = jnp.zeros((ROW_STEP, LANES), jnp.float32)
            for g in range(GROUPS):
                at = pl.ds(g * group_rows + r, ROW_STEP)
                for part, array in enumerate((in_b, in_f)):
                    start = (2 * g + part) * DEPTH
                    moved = pltpu.roll(array[at, p * LANES : (p + 1) * LANES], (start - base) % LANES, 1)
                    packed = jnp.where((lane16 >= start) & (lane16 < start + DEPTH), moved, packed)
            send_col[side - WEST, pl.ds(r, ROW_STEP), :] = packed
        return carry

    lax.fori_loop(0, group_rows // ROW_STEP, pack, 0)
    for index, side in enumerate((NW, NE, SW, SE)):
        dx, dy = SIDES[side]
        p, base = (0, 0) if dy < 0 else (own_panels - 1, LANES - DEPTH)
        start = 0 if dx < 0 else height - DEPTH
        packed = jnp.zeros((DEPTH, LANES), jnp.float32)
        for part, array in enumerate((in_b, in_f)):
            corner = array[start : start + DEPTH, p * LANES : (p + 1) * LANES]
            moved = pltpu.roll(corner, (part * DEPTH - base) % LANES, 1)
            packed = jnp.where((lane16 >= part * DEPTH) & (lane16 < (part + 1) * DEPTH), moved, packed)
        send_corner[index] = packed

    halos = []
    for side in range(8):
        if side in (NORTH, SOUTH):
            start = 0 if side == NORTH else height - DEPTH
            pairs = [
                (array.at[pl.ds(start, DEPTH), :], got_row.at[side, part]) for part, array in enumerate((in_b, in_f))
            ]
        elif side in (WEST, EAST):
            pairs = [(send_col.at[side - WEST], got_col.at[side - WEST])]
        else:
            pairs = [(send_corner.at[side - NW], got_corner.at[side - NW])]
        for part, (source, target) in enumerate(pairs):
            slot = side if part == 0 else 8 + side
            halos.append(
                pltpu.make_async_remote_copy(
                    src_ref=source,
                    dst_ref=target,
                    send_sem=halo_send.at[slot],
                    recv_sem=halo_recv.at[slot],
                    device_id=neighbour(side),
                    device_id_type=MESH,
                )
            )

    def phase(buffer, index, along_x):
        size, me, peer = (size_x, gx, peer_x) if along_x else (size_y, gy, peer_y)

        def start():
            for d in range(1, size):
                pltpu.make_async_remote_copy(
                    src_ref=buffer.at[me],
                    dst_ref=buffer.at[me],
                    send_sem=phase_send.at[index],
                    recv_sem=phase_recv.at[index],
                    device_id=peer(d),
                    device_id_type=MESH,
                ).start()

        def whole():
            part = buffer.at[pl.ds(0, size - 1)]
            return pltpu.make_async_remote_copy(
                src_ref=part,
                dst_ref=part,
                send_sem=phase_send.at[index],
                recv_sem=phase_recv.at[index],
                device_id=peer(1),
                device_id_type=MESH,
            )

        return start, (lambda: whole().wait_recv()), (lambda: whole().wait_send())

    def total_of(buffer, size, *index):
        return functools.reduce(jnp.add, [buffer[(i,) + index] for i in range(size)])

    finish = []

    aggregate = sub * LANES + lane8
    by_aggregate, where_table = zero8, zero8
    for t in range(bands):
        label = agg_ref[t, 0]
        by_aggregate = jnp.where(aggregate == label, band_sums[t], by_aggregate)
        here = (sub == gx) & (lane8 == gy * bands + t)
        where_table = jnp.where(here, (label + 1).astype(jnp.float32), where_table)
    first_x[gx, 0] = by_aggregate
    first_x[gx, 1] = where_table

    pl.semaphore_wait(barrier, size_x + size_y - 2 + 4)
    for copy in halos:
        copy.start()
    start_fx, wait_fx, done_fx = phase(first_x, 0, True)
    start_fy, wait_fy, done_fy = phase(first_y, 1, False)
    start_mx, wait_mx, done_mx = phase(max_x, 2, True)
    start_my, wait_my, done_my = phase(max_y, 3, False)
    finish += [done_fx, done_fy, done_mx, done_my]
    start_fx()
    start_bx, wait_bx, done_bx = phase(bulk_x, 12, True)
    start_by, wait_by, done_by = phase(bulk_y, 13, False)
    finish += [done_bx, done_by]
    start_bx()

    own_rows = pl.ds(0, breadth)
    block_rows = 64

    def settle(c, carry):
        rows = pl.ds(c * block_rows, block_rows)
        for source, target in ((in_b, wet), (in_f, res)):
            moved = placed(source[rows, :], chooser[own_rows, :])
            for p in range(panels):
                target[p, pl.ds(OWN + c * block_rows, block_rows), :] = moved[:, p * LANES : (p + 1) * LANES]
        return carry

    lax.fori_loop(0, height // block_rows, settle, 0)

    wait_fx()
    for part in range(2):
        first_y[gy, part] = total_of(first_x, size_x, part)
    start_fy()

    for copy in halos:
        copy.wait()

    east_lanes = jnp.where(gy < size_y - 1, DEPTH, 0)
    west_lane = jnp.where(gy > 0, LANES - DEPTH, LANES)
    for side, start, inside in ((SOUTH, PAD, gx > 0), (NORTH, OWN + height, gx < size_x - 1)):
        from_east, from_west = (SW, SE) if side == SOUTH else (NW, NE)
        for part, target in enumerate((wet, res)):
            east = pltpu.roll(got_corner[from_east - NW], (-part * DEPTH) % LANES, 1)
            west = pltpu.roll(got_corner[from_west - NW], (-(part + 1) * DEPTH) % LANES, 1)
            corner = jnp.where(lane16 < east_lanes, east, jnp.where(lane16 >= west_lane, west, 0.0))
            whole_row = jnp.concatenate([got_row[side, part], corner], axis=1)
            moved = placed(jnp.where(inside, whole_row, 0.0), chooser[...])
            for p in range(panels):
                target[p, start : start + DEPTH, :] = moved[:, p * LANES : (p + 1) * LANES]

    def unpack(c, carry):
        r = c * ROW_STEP
        east_all = got_col[WEST - WEST, pl.ds(r, ROW_STEP), :]
        west_all = got_col[EAST - WEST, pl.ds(r, ROW_STEP), :]
        for g in range(GROUPS):
            for part, target in enumerate((side_w, side_r)):
                start = (2 * g + part) * DEPTH
                east = pltpu.roll(east_all, (-start) % LANES, 1)
                west = pltpu.roll(west_all, (LANES - DEPTH - start) % LANES, 1)
                target[pl.ds(g * group_rows + r, ROW_STEP), :] = jnp.where(
                    lane16 < east_lanes, east, jnp.where(lane16 >= west_lane, west, 0.0)
                )
        return carry

    lax.fori_loop(0, group_rows // ROW_STEP, unpack, 0)

    def settle_sides(c, carry):
        rows = pl.ds(c * block_rows, block_rows)
        at = pl.ds(OWN + c * block_rows, block_rows)
        for source, target in ((side_w, wet), (side_r, res)):
            moved = placed(source[rows, :], chooser[pl.ds(breadth, LANES), :])
            for p in range(panels):
                target[p, at, :] = target[p, at, :] + moved[:, p * LANES : (p + 1) * LANES]
        return carry

    lax.fori_loop(0, height // block_rows, settle_sides, 0)

    def east_west(values):
        easts = values[1:] + [pltpu.roll(values[0], LANES - 1, 1)]
        wests = [pltpu.roll(values[-1], 1, 1)] + values[:-1]
        return easts, wests

    last, extra = divmod(breadth + FIRST, panels)
    first_lane = FIRST // panels

    def own_lanes(x, p):
        lane = lax.broadcasted_iota(jnp.int32, x.shape, 1)
        return (lane >= first_lane) & (lane < last + (1 if p < extra else 0))

    def kind(p):
        return 0 if p < extra else 1

    def own_total(parts):
        return jnp.where(own_lanes(parts[0], 0), parts[0], 0.0) + jnp.where(
            own_lanes(parts[1], panels - 1), parts[1], 0.0
        )

    def add_to(pair, p, x):
        return tuple(total + x if i == kind(p) else total for i, total in enumerate(pair))

    zero_pair = (zero8, zero8)

    def faces(r, top):
        values = [wet[p, pl.ds(r, ROW_STEP), :] for p in range(panels)]
        easts, wests = east_west(values)
        for p in range(panels):
            at = pl.ds(r, ROW_STEP)
            south = jnp.minimum(values[p], wet[p, pl.ds(r + 1, ROW_STEP), :])
            north = jnp.minimum(values[p], wet[p, pl.ds(r - 1, ROW_STEP), :])
            east = jnp.minimum(values[p], easts[p])
            west = jnp.minimum(values[p], wests[p])
            k_south[p, at, :] = south
            k_north[p, at, :] = north
            k_east[p, at, :] = east
            k_west[p, at, :] = west
            diagonal = 1.0 + south + north + east + west
            centre[p, at, :] = diagonal
            ocean[p, at, :] = jnp.where(values[p] > 0.0, 1.0, 0.0)
            if top is not None:
                for start in range(0, ROW_STEP, 8):
                    part = diagonal[start : start + 8]
                    top = tuple(jnp.maximum(t, part) if i == kind(p) else t for i, t in enumerate(top))
        return top

    top = lax.fori_loop(
        0, height // ROW_STEP, lambda c, top: faces(OWN + c * ROW_STEP, top), (jnp.ones((8, LANES), jnp.float32),) * 2
    )
    max_x[gx] = jnp.maximum(
        jnp.where(own_lanes(top[0], 0), top[0], 1.0), jnp.where(own_lanes(top[1], panels - 1), top[1], 1.0)
    )
    start_mx()
    faces(PAD, None)
    faces(OWN + height, None)

    wait_fy()
    rhs = total_of(first_y, size_y, 0)
    labels = total_of(first_y, size_y, 1)
    table = labels.astype(jnp.int32) - 1

    def spread_coarse(rhs, rows, buffer):
        tile = zero8
        for s in range(bands):
            tile = jnp.where(table == first_row + s, splat_sum(rows[s] * rhs), tile)
        buffer[gx] = tile

    spread_coarse(rhs, inverse_rows, coarse_x)
    start_cx, wait_cx, done_cx = phase(coarse_x, 4, True)
    start_cy, wait_cy, done_cy = phase(coarse_y, 5, False)
    finish += [done_cx, done_cy]
    start_cx()

    wait_mx()
    max_y[gy] = functools.reduce(jnp.maximum, [max_x[i] for i in range(size_x)])
    start_my()

    wait_cx()
    coarse_y[gy] = total_of(coarse_x, size_x)
    start_cy()

    wait_bx()
    for i in range(size_x):
        bulk_y[gy, i * bands : (i + 1) * bands, :] = bulk_x[i]

    wait_my()
    largest = functools.reduce(jnp.maximum, [max_y[i] for i in range(size_y)])
    for move in (4, 2, 1):
        largest = jnp.maximum(largest, pltpu.roll(largest, move, 0))
    shift = jnp.broadcast_to(jnp.max(largest, axis=1, keepdims=True), (8, LANES))
    scale = 2.0 / shift
    scale16 = tall(scale, ROW_STEP)

    def rescale(c, carry):
        at = pl.ds(PAD + c * ROW_STEP, ROW_STEP)
        for p in range(panels):
            for array in (k_south, k_north, k_east, k_west):
                array[p, at, :] = array[p, at, :] * scale16
            centre[p, at, :] = centre[p, at, :] * scale16 - 2.0
        return carry

    chunks_all = (rows_all - 2 * PAD) // ROW_STEP
    lax.fori_loop(0, chunks_all, rescale, 0)

    def stencil(array, r):
        at = pl.ds(r, ROW_STEP)
        values = [array[p, at, :] for p in range(panels)]
        easts, wests = east_west(values)
        out = []
        for p in range(panels):
            south = array[p, pl.ds(r + 1, ROW_STEP), :]
            north = array[p, pl.ds(r - 1, ROW_STEP), :]
            flow = k_south[p, at, :] * south + k_north[p, at, :] * north
            flow = flow + (k_east[p, at, :] * easts[p] + k_west[p, at, :] * wests[p])
            out.append(centre[p, at, :] * values[p] - flow)
        return out, values

    def over_bands(chunk, first_sums, run):
        chunk(PAD, None)
        chunk(OWN + height, None)

        def band(t, carry):
            carry = carry + (zero_pair,)
            for c in range(TILE // ROW_STEP):
                carry = chunk(pl.multiple_of(OWN + t * TILE + c * ROW_STEP, 8), carry)
            sums[pl.ds(first_sums + t, 1), :] = jnp.sum(own_total(carry[-1]), axis=0, keepdims=True)
            return carry[:-1]

        return lax.fori_loop(0, bands, band, run)

    shift16 = tall(shift, ROW_STEP)
    gram_phases = [(phase(gram_x.at[c], 8 + 2 * c, True), phase(gram_y.at[c], 9 + 2 * c, False)) for c in range(CYCLES)]
    finish += [p[2] for pair in gram_phases for p in pair]

    strips = [(-1, bands - 1)] + [(0, t) for t in range(bands)] + [(1, 0)]

    def around(tile):
        rows_of = {dx: sub_total(jnp.where(sub == gx + dx, tile, 0.0)) for dx in (-1, 0, 1)}
        found = []
        for dx, t in strips:
            for dy in (-1, 0, 1):
                picked = jnp.where(lane8 == (gy + dy) * bands + t, rows_of[dx], 0.0)
                found.append(jnp.broadcast_to(jnp.sum(picked, axis=1, keepdims=True), (8, LANES)))
        return found

    def choose_rows():
        slot = lax.broadcasted_iota(jnp.int32, (1, n_agg), 1)
        in_slot = lax.rem(slot, size_x * bands)
        row = (lax.div(in_slot, bands) * size_y + lax.div(slot, size_x * bands)) * bands + lax.rem(in_slot, bands)
        selector[...] = jnp.zeros_like(selector)
        for k, label in enumerate(around(labels)):
            wide = jnp.concatenate([label[0:1]] * max(1, n_agg // LANES), axis=1)[:, 0:n_agg]
            selector[k : k + 1, :] = jnp.where((row + 1).astype(jnp.float32) == wide, 1.0, 0.0)

    def permute_rows():
        chunks = max(1, n_agg // LANES)
        width, per = n_agg // chunks, size_y // chunks
        rows = None
        for c in range(chunks):
            part = exact_placed(
                selector[:, c * width : (c + 1) * width].astype(jnp.bfloat16),
                jnp.concatenate([bulk_y[c * per + i] for i in range(per)], axis=0),
            )
            rows = part if rows is None else rows + part
        column = lax.broadcasted_iota(jnp.int32, (n_agg, LANES), 0)
        for i in range(size_x):
            unit = jnp.where(column == table[i : i + 1, :], 1.0, 0.0).astype(jnp.bfloat16)
            permuted[i] = exact_moved(rows, unit)

    def choose_back(c, carry):
        for p in range(panels):
            for q in range(own_panels):
                goal, lane = place(16, LANES, q * LANES, True)
                rows = pl.ds(p * LANES + c * 16, 16)
                back[rows, q * LANES : (q + 1) * LANES] = jnp.where(
                    goal == (lane + c * 16) * panels + p, 1.0, 0.0
                ).astype(jnp.bfloat16)
        return carry

    next_values = None
    for cycle in range(CYCLES):
        if cycle == 0:
            wait_cy()
            values_at = around(total_of(coarse_y, size_y))
        else:
            values_at = next_values

        def spread_band(strip, start, chunks):
            west, own, east = values_at[3 * strip : 3 * strip + 3]
            dx = strips[strip][0]
            side = jnp.where(lane8 < LANES // 2, west, east)
            values = [tall(jnp.where(own_lanes(own, p), own, side), ROW_STEP) for p in range(panels)]

            def body(c, carry):
                at = pl.ds(start + c * ROW_STEP, ROW_STEP)
                for p in range(panels):
                    value = ocean[p, at, :] * values[p]
                    odd[p, at, :] = value
                    if dx == 0:
                        inner = pl.ds(start - OWN + c * ROW_STEP, ROW_STEP)
                        sol[p, inner, :] = value if cycle == 0 else sol[p, inner, :] + value
                return carry

            lax.fori_loop(0, chunks, body, 0)

        spread_band(0, PAD, DEPTH // ROW_STEP)
        for t in range(bands):
            spread_band(1 + t, OWN + t * TILE, TILE // ROW_STEP)
        spread_band(1 + bands, OWN + height, DEPTH // ROW_STEP)
        if cycle == 0:
            start_by()

        def first(r, carry):
            out, values = stencil(odd, r)
            at = pl.ds(r, ROW_STEP)
            for p in range(panels):
                v = res[p, at, :] - shift16 * (0.5 * out[p] + values[p])
                even[p, at, :] = v
                basis[0, p, at, :] = v
                if carry is not None:
                    square, total = carry
                    carry = (add_to(square, p, fold(v * v)), add_to(total, p, fold(v * ocean[p, at, :])))
            return carry

        (square,) = over_bands(first, 0, (zero_pair,))
        sums[64:65, :] = jnp.sum(own_total(square), axis=0, keepdims=True)

        def step(j, source, target):
            new_part = jnp.where(j == 1, 0.5, 1.0)
            old_part = jnp.where(j == 1, 0.0, 1.0)

            def chunk(r, carry):
                out, values = stencil(source, r)
                at = pl.ds(r, ROW_STEP)
                for p in range(panels):
                    v = new_part * out[p] - old_part * target[p, at, :]
                    target[p, at, :] = v
                    basis[j, p, at, :] = v
                    if carry is not None:
                        square, cross, total = carry
                        carry = (
                            add_to(square, p, fold(v * v)),
                            add_to(cross, p, fold(v * values[p])),
                            add_to(total, p, fold(v * ocean[p, at, :])),
                        )
                return carry

            square, cross = over_bands(chunk, j * bands, (zero_pair, zero_pair))
            sums[pl.ds(64 + j, 1), :] = jnp.sum(own_total(square), axis=0, keepdims=True)
            sums[pl.ds(80 + j, 1), :] = jnp.sum(own_total(cross), axis=0, keepdims=True)

        def two_steps(i, carry):
            step(2 * i + 1, even, odd)
            step(2 * i + 2, odd, even)
            return carry

        lax.fori_loop(0, KB // 2, two_steps, 0)

        row = lax.dot_general(
            jnp.ones((8, LANES), jnp.float32),
            sums[...],
            (((1,), (1,)), ((), ())),
            precision=highest,
            preferred_element_type=jnp.float32,
        )
        (start_gx, wait_gx, _), (start_gy, wait_gy, _) = gram_phases[cycle]
        gram_x[cycle, gx] = jnp.where(sub == gx, row, 0.0)
        start_gx()
        if cycle == 0:
            choose_rows()
        else:
            lax.fori_loop(0, LANES // 16, choose_back, 0)
        wait_gx()
        gram_y[cycle, gy] = total_of(gram_x.at[cycle], size_x)
        start_gy()
        if cycle == 0:
            wait_by()
            permute_rows()
        wait_gy()
        gathered = [gram_y[cycle, i] for i in range(size_y)]
        whole = sub_total(functools.reduce(jnp.add, gathered))

        def at_lane(k):
            return jnp.broadcast_to(whole[:, k : k + 1], (8, LANES))

        vv = [at_lane(64 + a) for a in range(KB + 1)]
        vp = [None] + [at_lane(80 + a) for a in range(1, KB + 1)]
        weight, combined = small_solve(vv, vp)
        for j in range(KB):
            factors[j] = weight[j] / shift
        for a in range(KB + 1):
            factors[KB + a] = combined[a]

        if cycle < CYCLES - 1:
            group = lane8 // bands
            mix = jnp.where(group == 0, 1.0, 0.0)
            for a in range(KB + 1):
                mix = jnp.where(group == a, mix - combined[a], mix)
            rhs = zero8
            for i in range(size_y):
                part = gathered[i] * jnp.where(lane8 < (KB + 1) * bands, mix, 0.0)
                move = bands
                while move < LANES:
                    part = part + pltpu.roll(part, move, 1)
                    move *= 2
                rhs = jnp.where(group == i, part, rhs)
            found = permuted[0] * rhs[0:1, :]
            for i in range(1, size_x):
                found = found + permuted[i] * rhs[i : i + 1, :]
            found = jnp.broadcast_to(jnp.sum(found, axis=1, keepdims=True), found.shape)
            next_values = [jnp.broadcast_to(found[k : k + 1, :], (8, LANES)) for k in range(3 * len(strips))]

        w = [tall(factors[j], ROW_STEP) for j in range(KB)]
        c_all = [tall(factors[KB + a], ROW_STEP) for a in range(KB + 1)]

        def update(r, p, inner):
            at = pl.ds(r, ROW_STEP)
            values = [basis[a, p, at, :] for a in range(KB + 1)]
            residual = values[0]
            for a in range(KB + 1):
                residual = residual - c_all[a] * values[a]
            if inner is None:
                res[p, at, :] = residual
                return
            rows = pl.ds(inner, ROW_STEP)
            answer = sol[p, rows, :]
            for j in range(KB):
                answer = answer + w[j] * values[j]
            if cycle < CYCLES - 1:
                res[p, at, :] = residual
                sol[p, rows, :] = answer
            else:
                residual_ref[p, rows, :] = residual
                solution_ref[p, rows, :] = answer

        def update_own(c, carry):
            for p in range(panels):
                update(OWN + c * ROW_STEP, p, c * ROW_STEP)
            return carry

        lax.fori_loop(0, height // ROW_STEP, update_own, 0)
        if cycle < CYCLES - 1:
            for p in range(panels):
                update(PAD, p, None)
                update(OWN + height, p, None)

    for done in finish:
        done()


def to_natural(solution_ref, residual_ref, back, solution_out, residual_out, parts, sems):
    panels, height = solution_ref.shape[:2]
    rows = parts.shape[1]
    copies = []
    for index in range(height // rows):
        at = pl.ds(index * rows, rows)
        for which, (source, target) in enumerate(((solution_ref, solution_out), (residual_ref, residual_out))):
            slot = 2 * index + which
            parts[slot] = placed(jnp.concatenate([source[p, at, :] for p in range(panels)], axis=1), back[...])
            copies.append(pltpu.make_async_copy(parts.at[slot], target.at[at, :], sems.at[slot]))
            copies[-1].start()
    for copy in copies:
        copy.wait()


def on_device(size_x, size_y, forcing, bathymetry, ocean_mask, aggregate_id, coarse_inverse):
    height, breadth = forcing.shape
    own_panels = breadth // LANES
    panels = own_panels + 1
    rows = height + 2 * (DEPTH + PAD)
    bands = height // TILE
    f32 = jnp.float32
    field = pltpu.VMEM((panels, rows, LANES), f32)
    block = pltpu.VMEM((height, breadth), f32)
    any_spec = pl.BlockSpec(memory_space=pltpu.MemorySpace.HBM)
    vmem = pl.BlockSpec(memory_space=pltpu.VMEM)
    smem = pl.BlockSpec(memory_space=pltpu.SMEM)
    tiles = lambda *lead: pltpu.VMEM(lead + (8, LANES), f32)
    dma = pltpu.SemaphoreType.DMA
    n_agg = coarse_inverse.shape[1]
    wanted = -(-3 * (bands + 2) // 8) * 8
    dealt = jax.ShapeDtypeStruct((panels, height, LANES), f32)
    back = jax.ShapeDtypeStruct((panels * LANES, breadth), jnp.bfloat16)
    forcing, bathymetry, ocean_mask, aggregate_id, coarse_inverse = (
        pltpu.with_memory_space_constraint(x, pltpu.MemorySpace.HBM)
        for x in (forcing, bathymetry, ocean_mask, aggregate_id, coarse_inverse)
    )
    answer, residual, back = pl.pallas_call(
        functools.partial(kernel, size_x, size_y),
        out_shape=(dealt, dealt, back),
        in_specs=[any_spec, any_spec, any_spec, smem, any_spec],
        out_specs=(vmem, vmem, vmem),
        scratch_shapes=[
            block,
            block,
            pltpu.VMEM((height, breadth), jnp.int32),
            pltpu.VMEM((height, LANES), f32),
            pltpu.VMEM((height, LANES), f32),
            pltpu.VMEM((panels * LANES, panels * LANES), jnp.bfloat16),
            field,
            field,
            field,
            pltpu.VMEM((panels, height, LANES), f32),
            pltpu.VMEM((KB + 1, panels, rows, LANES), f32),
            field,
            field,
            field,
            field,
            field,
            field,
            field,
            pltpu.VMEM((2, height // GROUPS, LANES), f32),
            pltpu.VMEM((2, height // GROUPS, LANES), f32),
            pltpu.VMEM((4, DEPTH, LANES), f32),
            pltpu.VMEM((4, DEPTH, LANES), f32),
            pltpu.VMEM((2, 2, DEPTH, breadth), f32),
            tiles(bands),
            pltpu.VMEM((wanted, n_agg), f32),
            pltpu.VMEM((size_x, wanted, LANES), f32),
            pltpu.VMEM((size_x, bands, n_agg), f32),
            pltpu.VMEM((size_y, size_x * bands, n_agg), f32),
            pltpu.VMEM((LANES, LANES), f32),
            tiles(2 * KB + 1),
            tiles(size_x, 2),
            tiles(size_y, 2),
            tiles(size_x),
            tiles(size_y),
            tiles(size_x),
            tiles(size_y),
            tiles(CYCLES, size_x),
            tiles(CYCLES, size_y),
            dma((4,)),
            dma((10,)),
            dma((10,)),
            dma((14,)),
            dma((14,)),
        ],
        compiler_params=pltpu.CompilerParams(
            collective_id=0, has_side_effects=True, vmem_limit_bytes=40 * 1024 * 1024
        ),
    )(forcing, bathymetry, ocean_mask, aggregate_id, coarse_inverse)
    part = 64
    count = 2 * (height // part)
    return pl.pallas_call(
        to_natural,
        out_shape=(jax.ShapeDtypeStruct((height, breadth), f32),) * 2,
        in_specs=[vmem, vmem, vmem],
        out_specs=(any_spec, any_spec),
        scratch_shapes=[pltpu.VMEM((count, part, breadth), f32), dma((count,))],
        compiler_params=pltpu.CompilerParams(vmem_limit_bytes=16 * 1024 * 1024),
    )(answer, residual, back)


def solution(mesh):
    return jax.shard_map(
        functools.partial(on_device, mesh.shape["gx"], mesh.shape["gy"]),
        mesh=mesh,
        in_specs=(
            P("gx", "gy"),
            P("gx", "gy"),
            P("gx", "gy"),
            P("gx", "gy"),
            P(("gx", "gy"), None),
        ),
        out_specs=(P("gx", "gy"), P("gx", "gy")),
        check_vma=False,
    )
```

```python
import functools

import jax
import jax.numpy as jnp
from jax import lax
from jax.experimental import pallas as pl
from jax.experimental.pallas import tpu as pltpu
from jax.sharding import PartitionSpec as P

TILE = 64
KB = 8
CYCLES = 2
SHIFT_REL = 0.001
DEPTH = KB * CYCLES
LANES = 128
PAD = 8
OWN = PAD + DEPTH
ROW_STEP = 16
GROUPS = 4
FIRST = 20
MESH = pl.DeviceIdType.MESH
highest = lax.Precision.HIGHEST
SIDES = ((-1, 0), (1, 0), (0, -1), (0, 1), (-1, -1), (-1, 1), (1, -1), (1, 1))
NORTH, SOUTH, WEST, EAST, NW, NE, SW, SE = range(8)


def sub_total(x):
    for shift in (4, 2, 1):
        x = x + pltpu.roll(x, shift, 0)
    return x


def splat_sum(x):
    return jnp.broadcast_to(jnp.sum(sub_total(x), axis=1, keepdims=True), x.shape)


def fold(x):
    total = x[0:8]
    for start in range(8, x.shape[0], 8):
        total = total + x[start : start + 8]
    return total


def tall(x, rows):
    return jnp.concatenate([x] * (rows // 8), axis=0)


def split(x):
    high = x.astype(jnp.bfloat16)
    return high, (x - high.astype(jnp.float32)).astype(jnp.bfloat16)


def placed(x, chooser):
    high, low = split(x)
    return jnp.dot(high, chooser, preferred_element_type=jnp.float32) + jnp.dot(
        low, chooser, preferred_element_type=jnp.float32
    )


def exact_placed(chooser, x):
    high, rest = split(x)
    low = (x - high.astype(jnp.float32) - rest.astype(jnp.float32)).astype(jnp.bfloat16)
    return sum(jnp.dot(chooser, part, preferred_element_type=jnp.float32) for part in (high, rest, low))


def exact_moved(x, chooser):
    high, rest = split(x)
    low = (x - high.astype(jnp.float32) - rest.astype(jnp.float32)).astype(jnp.bfloat16)
    return sum(jnp.dot(part, chooser, preferred_element_type=jnp.float32) for part in (high, rest, low))


def small_solve(vv, vp):
    n = KB + 1
    moment = [None] * (2 * KB + 1)
    moment[0], moment[1] = vv[0], vp[1]
    for k in range(1, n):
        moment[2 * k] = 2.0 * vv[k] - vv[0]
    for k in range(2, n):
        moment[2 * k - 1] = 2.0 * vp[k] - vp[1]
    upper = [[None] * n for _ in range(n)]
    for j in range(n):
        reduced = vv[j] * (1.0 + SHIFT_REL)
        for k in range(j):
            reduced = reduced - upper[k][j] * upper[k][j]
        root = jnp.sqrt(reduced)
        upper[j][j] = root
        inverse = 1.0 / root
        for i in range(j + 1, n):
            if i - j == 1:
                entry = vp[i]
            else:
                entry = 0.5 * (moment[i + j] + moment[i - j])
            for k in range(j):
                entry = entry - upper[k][j] * upper[k][i]
            upper[j][i] = entry * inverse
    hess = [[None] * KB for _ in range(n)]
    for j in range(KB):
        below = 1.0 if j == 0 else 0.5
        for i in range(j + 2):
            entry = below * upper[i][j + 1]
            if i <= j:
                entry = entry + upper[i][j]
            if i <= j - 1:
                entry = entry + 0.5 * upper[i][j - 1]
            hess[i][j] = entry
    right = [upper[0][0]] + [None] * KB
    for j in range(KB):
        a, b = hess[j][j], hess[j + 1][j]
        inverse = 1.0 / jnp.sqrt(a * a + b * b)
        c, s = a * inverse, b * inverse
        for k in range(j, KB):
            x, y = hess[j][k], hess[j + 1][k]
            if k == j:
                hess[j][k] = c * x + s * y
            else:
                hess[j][k] = c * x + s * y
                hess[j + 1][k] = c * y - s * x
        x = right[j]
        right[j] = c * x
        right[j + 1] = -s * x
    weight = [None] * KB
    for j in range(KB - 1, -1, -1):
        rest = right[j]
        for k in range(j + 1, KB):
            rest = rest - hess[j][k] * weight[k]
        weight[j] = rest / hess[j][j]
    combined = []
    for i in range(n):
        terms = []
        if i < KB:
            terms.append(weight[i])
        if i >= 1:
            terms.append((1.0 if i == 1 else 0.5) * weight[i - 1])
        if i + 1 < KB:
            terms.append(0.5 * weight[i + 1])
        combined.append(functools.reduce(jnp.add, terms))
    return weight, combined


def kernel(
    size_x,
    size_y,
    forcing_ref,
    depth_ref,
    mask_ref,
    agg_ref,
    inverse_ref,
    solution_ref,
    residual_ref,
    back,
    in_f,
    in_b,
    in_m,
    side_w,
    side_r,
    chooser,
    wet,
    ocean,
    res,
    sol,
    basis,
    even,
    odd,
    k_south,
    k_north,
    k_east,
    k_west,
    centre,
    send_col,
    got_col,
    send_corner,
    got_corner,
    got_row,
    inverse_rows,
    selector,
    chosen,
    bulk_x,
    bulk_y,
    sums,
    factors,
    first_all,
    max_all,
    coarse_all,
    gram_all,
    in_sem,
    halo_send,
    halo_recv,
    phase_send,
    phase_recv,
):
    height, breadth = in_f.shape
    own_panels = breadth // LANES
    panels = own_panels + 1
    bands = height // TILE
    n_agg = inverse_ref.shape[1]
    rows_all = wet.shape[1]
    group_rows = height // GROUPS
    gx, gy = lax.axis_index("gx"), lax.axis_index("gy")

    loads = []
    for index, (source, target) in enumerate(
        ((depth_ref, in_b), (mask_ref, in_m), (forcing_ref, in_f), (inverse_ref, bulk_x.at[gx]))
    ):
        copy = pltpu.make_async_copy(source, target, in_sem.at[index])
        copy.start()
        loads.append(copy)
    barrier = pltpu.get_barrier_semaphore()

    def peer_x(d):
        return (lax.rem(gx + d, size_x), gy)

    def peer_y(d):
        return (gx, lax.rem(gy + d, size_y))

    def neighbour(side):
        dx, dy = SIDES[side]
        return (lax.rem(gx + dx + size_x, size_x), lax.rem(gy + dy + size_y, size_y))

    others = size_x * size_y - 1

    xs = [lax.rem(gx + d, size_x) for d in range(size_x)]
    ys = [lax.rem(gy + d, size_y) for d in range(size_y)]

    def hops(d):
        ring = lambda k: min(k, 4 - k)
        dx, dy = divmod(d, size_y)
        return ring(dx // 2) + ring(dy % 4) + ring(dy // 4)

    far_first = sorted(range(1, others + 1), key=lambda d: -hops(d))

    def peer(d):
        return (xs[d // size_y], ys[d % size_y])

    for d in far_first:
        pl.semaphore_signal(barrier, inc=1, device_id=peer(d), device_id_type=MESH)

    sub = lax.broadcasted_iota(jnp.int32, (8, LANES), 0)
    lane8 = lax.broadcasted_iota(jnp.int32, (8, LANES), 1)
    lane16 = lax.broadcasted_iota(jnp.int32, (ROW_STEP, LANES), 1)
    zero8 = jnp.zeros((8, LANES), jnp.float32)

    for p in range(panels):
        for start in (0, rows_all - PAD):
            for array in (wet, even, odd):
                array[p, start : start + PAD, :] = zero8
    sums[...] = jnp.zeros_like(sums)
    def place(rows, columns, column_base, transposed):
        line = lax.broadcasted_iota(jnp.int32, (rows, columns), 1 if transposed else 0) + column_base
        spot = lax.broadcasted_iota(jnp.int32, (rows, columns), 0 if transposed else 1)
        return jnp.where(line < breadth + LANES // 2, line, line - panels * LANES) + FIRST, spot

    def choose(c, carry):
        rows = pl.ds(c * 16, 16)
        for p in range(panels):
            goal, lane = place(16, LANES, c * 16, False)
            chooser[rows, p * LANES : (p + 1) * LANES] = jnp.where(goal == lane * panels + p, 1.0, 0.0).astype(
                jnp.bfloat16
            )
        return carry

    lax.fori_loop(0, panels * LANES // 16, choose, 0)

    for copy in loads:
        copy.wait()
    inverse_rows[...] = jnp.zeros_like(inverse_rows)
    chosen[...] = jnp.zeros_like(chosen)
    inverse_rows[0:bands, 0:n_agg] = bulk_x[gx]

    band_sums = []
    for t in range(bands):

        def prepare(c, total, t=t):
            rows = pl.ds(t * TILE + c * ROW_STEP, ROW_STEP)
            for p in range(own_panels):
                at = pl.ds(p * LANES, LANES)
                sea = in_m[rows, at].astype(jnp.float32)
                value = in_f[rows, at] * sea
                in_b[rows, at] = in_b[rows, at] * sea
                in_f[rows, at] = value
                total = total + fold(value * sea)
            return total

        band_sums.append(splat_sum(lax.fori_loop(0, TILE // ROW_STEP, prepare, zero8)))

    def pack(c, carry):
        r = c * ROW_STEP
        for side, p, base in ((WEST, 0, 0), (EAST, own_panels - 1, LANES - DEPTH)):
            packed = jnp.zeros((ROW_STEP, LANES), jnp.float32)
            for g in range(GROUPS):
                at = pl.ds(g * group_rows + r, ROW_STEP)
                for part, array in enumerate((in_b, in_f)):
                    start = (2 * g + part) * DEPTH
                    moved = pltpu.roll(array[at, p * LANES : (p + 1) * LANES], (start - base) % LANES, 1)
                    packed = jnp.where((lane16 >= start) & (lane16 < start + DEPTH), moved, packed)
            send_col[side - WEST, pl.ds(r, ROW_STEP), :] = packed
        return carry

    lax.fori_loop(0, group_rows // ROW_STEP, pack, 0)
    for index, side in enumerate((NW, NE, SW, SE)):
        dx, dy = SIDES[side]
        p, base = (0, 0) if dy < 0 else (own_panels - 1, LANES - DEPTH)
        start = 0 if dx < 0 else height - DEPTH
        packed = jnp.zeros((DEPTH, LANES), jnp.float32)
        for part, array in enumerate((in_b, in_f)):
            corner = array[start : start + DEPTH, p * LANES : (p + 1) * LANES]
            moved = pltpu.roll(corner, (part * DEPTH - base) % LANES, 1)
            packed = jnp.where((lane16 >= part * DEPTH) & (lane16 < (part + 1) * DEPTH), moved, packed)
        send_corner[index] = packed

    halos = []
    for side in range(8):
        if side in (NORTH, SOUTH):
            start = 0 if side == NORTH else height - DEPTH
            pairs = [
                (array.at[pl.ds(start, DEPTH), :], got_row.at[side, part]) for part, array in enumerate((in_b, in_f))
            ]
        elif side in (WEST, EAST):
            pairs = [(send_col.at[side - WEST], got_col.at[side - WEST])]
        else:
            pairs = [(send_corner.at[side - NW], got_corner.at[side - NW])]
        for part, (source, target) in enumerate(pairs):
            slot = side if part == 0 else 8 + side
            halos.append(
                pltpu.make_async_remote_copy(
                    src_ref=source,
                    dst_ref=target,
                    send_sem=halo_send.at[slot],
                    recv_sem=halo_recv.at[slot],
                    device_id=neighbour(side),
                    device_id_type=MESH,
                )
            )

    def phase(buffer, index, along_x):
        size, me, peer = (size_x, gx, peer_x) if along_x else (size_y, gy, peer_y)

        def far(d):
            ring = lambda k: -min(k, 4 - k)
            return ring(d // 2) if along_x else ring(d % 4) + ring(d // 4)

        def start():
            for d in sorted(range(1, size), key=far):
                pltpu.make_async_remote_copy(
                    src_ref=buffer.at[me],
                    dst_ref=buffer.at[me],
                    send_sem=phase_send.at[index],
                    recv_sem=phase_recv.at[index],
                    device_id=peer(d),
                    device_id_type=MESH,
                ).start()

        def whole():
            part = buffer.at[pl.ds(0, size - 1)]
            return pltpu.make_async_remote_copy(
                src_ref=part,
                dst_ref=part,
                send_sem=phase_send.at[index],
                recv_sem=phase_recv.at[index],
                device_id=peer(1),
                device_id_type=MESH,
            )

        return start, (lambda: whole().wait_recv()), (lambda: whole().wait_send())

    me = gx * size_y + gy

    def direct(buffer, index):
        def start(row):
            buffer[pl.ds(me, 1), :] = row
            mine = buffer.at[pl.ds(me, 1), :]

            for d in far_first:
                pltpu.make_async_remote_copy(
                    src_ref=mine,
                    dst_ref=mine,
                    send_sem=phase_send.at[index],
                    recv_sem=phase_recv.at[index],
                    device_id=peer(d),
                    device_id_type=MESH,
                ).start()

        def whole():
            part = buffer.at[pl.ds(0, others), :]
            return pltpu.make_async_remote_copy(
                src_ref=part,
                dst_ref=part,
                send_sem=phase_send.at[index],
                recv_sem=phase_recv.at[index],
                device_id=peer(1),
                device_id_type=MESH,
            )

        return start, (lambda: whole().wait_recv()), (lambda: whole().wait_send())

    groups = -(-(others + 1) // 8)

    def rows_of(buffer, i):
        return buffer[8 * i : 8 * i + 8, :]

    def by_label(values):
        total = [zero8] * pieces
        for i in range(groups):
            table = rows_of(first_all, i)
            for t in range(bands):
                label = jnp.broadcast_to(table[:, bands + t : bands + t + 1], (8, LANES))
                value = jnp.broadcast_to(values[i][:, t : t + 1], (8, LANES))
                for c in range(pieces):
                    total[c] = total[c] + jnp.where(label == numbers[c], value, 0.0)
        return jnp.concatenate([jnp.sum(x, axis=0, keepdims=True) for x in total], axis=1)

    finish = []

    pieces = -(-n_agg // LANES)
    numbers = [(lane8 + (c * LANES + 1)).astype(jnp.float32) for c in range(pieces)]
    first_row_values = zero8
    for t in range(bands):
        first_row_values = jnp.where(lane8 == t, band_sums[t], first_row_values)
        label = (agg_ref[t, 0] + 1).astype(jnp.float32)
        first_row_values = jnp.where(lane8 == bands + t, label, first_row_values)

    pl.semaphore_wait(barrier, others)
    for copy in halos:
        copy.start()
    start_f, wait_f, done_f = direct(first_all, 0)
    start_m, wait_m, done_m = direct(max_all, 1)
    start_c, wait_c, done_c = direct(coarse_all, 2)
    finish += [done_f, done_m, done_c]
    start_f(first_row_values[0:1])
    start_bx, wait_bx, done_bx = phase(bulk_x, 5, True)
    start_by, wait_by, done_by = phase(bulk_y, 6, False)
    finish += [done_bx, done_by]
    start_bx()

    own_rows = pl.ds(0, breadth)
    block_rows = 64

    def settle(c, carry):
        rows = pl.ds(c * block_rows, block_rows)
        for source, target in ((in_b, wet), (in_f, res)):
            moved = placed(source[rows, :], chooser[own_rows, :])
            for p in range(panels):
                target[p, pl.ds(OWN + c * block_rows, block_rows), :] = moved[:, p * LANES : (p + 1) * LANES]
        return carry

    lax.fori_loop(0, height // block_rows, settle, 0)

    for copy in halos:
        copy.wait()

    east_lanes = jnp.where(gy < size_y - 1, DEPTH, 0)
    west_lane = jnp.where(gy > 0, LANES - DEPTH, LANES)
    for side, start, inside in ((SOUTH, PAD, gx > 0), (NORTH, OWN + height, gx < size_x - 1)):
        from_east, from_west = (SW, SE) if side == SOUTH else (NW, NE)
        for part, target in enumerate((wet, res)):
            east = pltpu.roll(got_corner[from_east - NW], (-part * DEPTH) % LANES, 1)
            west = pltpu.roll(got_corner[from_west - NW], (-(part + 1) * DEPTH) % LANES, 1)
            corner = jnp.where(lane16 < east_lanes, east, jnp.where(lane16 >= west_lane, west, 0.0))
            whole_row = jnp.concatenate([got_row[side, part], corner], axis=1)
            moved = placed(jnp.where(inside, whole_row, 0.0), chooser[...])
            for p in range(panels):
                target[p, start : start + DEPTH, :] = moved[:, p * LANES : (p + 1) * LANES]

    def unpack(c, carry):
        r = c * ROW_STEP
        east_all = got_col[WEST - WEST, pl.ds(r, ROW_STEP), :]
        west_all = got_col[EAST - WEST, pl.ds(r, ROW_STEP), :]
        for g in range(GROUPS):
            for part, target in enumerate((side_w, side_r)):
                start = (2 * g + part) * DEPTH
                east = pltpu.roll(east_all, (-start) % LANES, 1)
                west = pltpu.roll(west_all, (LANES - DEPTH - start) % LANES, 1)
                target[pl.ds(g * group_rows + r, ROW_STEP), :] = jnp.where(
                    lane16 < east_lanes, east, jnp.where(lane16 >= west_lane, west, 0.0)
                )
        return carry

    lax.fori_loop(0, group_rows // ROW_STEP, unpack, 0)

    def settle_sides(c, carry):
        rows = pl.ds(c * block_rows, block_rows)
        at = pl.ds(OWN + c * block_rows, block_rows)
        for source, target in ((side_w, wet), (side_r, res)):
            moved = placed(source[rows, :], chooser[pl.ds(breadth, LANES), :])
            for p in range(panels):
                target[p, at, :] = target[p, at, :] + moved[:, p * LANES : (p + 1) * LANES]
        return carry

    lax.fori_loop(0, height // block_rows, settle_sides, 0)

    def east_west(values):
        easts = values[1:] + [pltpu.roll(values[0], LANES - 1, 1)]
        wests = [pltpu.roll(values[-1], 1, 1)] + values[:-1]
        return easts, wests

    last, extra = divmod(breadth + FIRST, panels)
    first_lane = FIRST // panels

    def own_lanes(x, p):
        lane = lax.broadcasted_iota(jnp.int32, x.shape, 1)
        return (lane >= first_lane) & (lane < last + (1 if p < extra else 0))

    def kind(p):
        return 0 if p < extra else 1

    def own_total(parts):
        return jnp.where(own_lanes(parts[0], 0), parts[0], 0.0) + jnp.where(
            own_lanes(parts[1], panels - 1), parts[1], 0.0
        )

    def add_to(pair, p, x):
        return tuple(total + x if i == kind(p) else total for i, total in enumerate(pair))

    zero_pair = (zero8, zero8)

    def row_at(i):
        return pl.ds(i, 1)

    def faces(r, top):
        values = [wet[p, pl.ds(r, ROW_STEP), :] for p in range(panels)]
        easts, wests = east_west(values)
        for p in range(panels):
            at = pl.ds(r, ROW_STEP)
            south = jnp.minimum(values[p], wet[p, pl.ds(r + 1, ROW_STEP), :])
            north = jnp.minimum(values[p], wet[p, pl.ds(r - 1, ROW_STEP), :])
            east = jnp.minimum(values[p], easts[p])
            west = jnp.minimum(values[p], wests[p])
            k_south[p, at, :] = south
            k_north[p, at, :] = north
            k_east[p, at, :] = east
            k_west[p, at, :] = west
            diagonal = 1.0 + south + north + east + west
            centre[p, at, :] = diagonal
            ocean[p, at, :] = jnp.where(values[p] > 0.0, 1.0, 0.0)
            if top is not None:
                for start in range(0, ROW_STEP, 8):
                    part = diagonal[start : start + 8]
                    top = tuple(jnp.maximum(t, part) if i == kind(p) else t for i, t in enumerate(top))
        return top

    top = lax.fori_loop(
        0, height // ROW_STEP, lambda c, top: faces(OWN + c * ROW_STEP, top), (jnp.ones((8, LANES), jnp.float32),) * 2
    )
    top = jnp.maximum(
        jnp.where(own_lanes(top[0], 0), top[0], 1.0), jnp.where(own_lanes(top[1], panels - 1), top[1], 1.0)
    )
    start_m(jnp.max(top, axis=0, keepdims=True))
    faces(PAD, None)
    faces(OWN + height, None)

    wait_f()
    rhs = by_label([rows_of(first_all, i) for i in range(groups)])
    coarse_row = jnp.zeros((1, LANES), jnp.float32)
    lane1 = lax.broadcasted_iota(jnp.int32, (1, LANES), 1)
    for s in range(bands):
        product = jnp.sum(inverse_rows[s : s + 1, :] * rhs, axis=1, keepdims=True)
        coarse_row = jnp.where(lax.rem(lane1, bands) == s, product, coarse_row)
    start_c(coarse_row)

    strips = [(-1, bands - 1)] + [(0, t) for t in range(bands)] + [(1, 0)]
    labels = []
    for dx, t in strips:
        for dy in (-1, 0, 1):
            inside = (gx + dx >= 0) & (gx + dx < size_x) & (gy + dy >= 0) & (gy + dy < size_y)
            device = jnp.where(inside, me + dx * size_y + dy, me)
            label = first_all[pl.ds(device, 1), :][:, bands + t : bands + t + 1]
            label = jnp.broadcast_to(label, (1, LANES))
            labels.append(jnp.where(inside, label, 0.0))

    wait_bx()
    for i in range(size_x):
        bulk_y[gy, i * bands : (i + 1) * bands, :] = bulk_x[i]

    wait_m()
    largest = functools.reduce(jnp.maximum, [rows_of(max_all, i) for i in range(groups)])
    for move in (4, 2, 1):
        largest = jnp.maximum(largest, pltpu.roll(largest, move, 0))
    shift = jnp.broadcast_to(jnp.max(largest, axis=1, keepdims=True), (8, LANES))
    scale = 2.0 / shift
    scale16 = tall(scale, ROW_STEP)

    def rescale(c, carry):
        at = pl.ds(PAD + c * ROW_STEP, ROW_STEP)
        for p in range(panels):
            for array in (k_south, k_north, k_east, k_west):
                array[p, at, :] = array[p, at, :] * scale16
            centre[p, at, :] = centre[p, at, :] * scale16 - 2.0
        return carry

    chunks_all = (rows_all - 2 * PAD) // ROW_STEP
    lax.fori_loop(0, chunks_all, rescale, 0)

    def stencil(array, r):
        at = pl.ds(r, ROW_STEP)
        values = [array[p, at, :] for p in range(panels)]
        easts, wests = east_west(values)
        out = []
        for p in range(panels):
            south = array[p, pl.ds(r + 1, ROW_STEP), :]
            north = array[p, pl.ds(r - 1, ROW_STEP), :]
            flow = k_south[p, at, :] * south + k_north[p, at, :] * north
            flow = flow + (k_east[p, at, :] * easts[p] + k_west[p, at, :] * wests[p])
            out.append(centre[p, at, :] * values[p] - flow)
        return out, values

    def over_bands(chunk, first_sums, run):
        chunk(PAD, None)
        chunk(OWN + height, None)

        def band(t, carry):
            carry = carry + (zero_pair,)
            for c in range(TILE // ROW_STEP):
                carry = chunk(pl.multiple_of(OWN + t * TILE + c * ROW_STEP, 8), carry)
            sums[pl.ds(first_sums + t, 1), :] = jnp.sum(own_total(carry[-1]), axis=0, keepdims=True)
            return carry[:-1]

        return lax.fori_loop(0, bands, band, run)

    shift16 = tall(shift, ROW_STEP)
    grams = [direct(gram_all.at[c], 3 + c) for c in range(CYCLES)]
    finish += [p[2] for p in grams]

    def coarse_values():
        row = jnp.zeros((1, LANES), jnp.float32)
        for k, label in enumerate(labels):
            row = jnp.where(lax.div(lane1, bands) == k, label, row)
        total = zero8
        for i in range(groups):
            number = ((8 * i + sub) * bands + lax.rem(lane8, bands) + 1).astype(jnp.float32)
            total = total + jnp.where(number == row, rows_of(coarse_all, i), 0.0)
        total = sub_total(total)
        found = []
        for k in range(len(labels)):
            picked = jnp.where(lax.div(lane8, bands) == k, total, 0.0)
            found.append(jnp.broadcast_to(jnp.sum(picked, axis=1, keepdims=True), (8, LANES)))
        return found

    def choose_rows():
        slot = lax.broadcasted_iota(jnp.int32, (1, n_agg), 1)
        in_slot = lax.rem(slot, size_x * bands)
        row = (lax.div(in_slot, bands) * size_y + lax.div(slot, size_x * bands)) * bands + lax.rem(in_slot, bands)
        selector[...] = jnp.zeros_like(selector)
        for k, label in enumerate(labels):
            wide = jnp.concatenate([label] * pieces, axis=1)[:, 0:n_agg]
            selector[k : k + 1, :] = jnp.where((row + 1).astype(jnp.float32) == wide, 1.0, 0.0)

    def permute_rows():
        chunks = max(1, n_agg // LANES)
        width, per = n_agg // chunks, size_y // chunks
        rows = None
        for c in range(chunks):
            part = exact_placed(
                selector[:, c * width : (c + 1) * width].astype(jnp.bfloat16),
                jnp.concatenate([bulk_y[c * per + i] for i in range(per)], axis=0),
            )
            rows = part if rows is None else rows + part
        chosen[:, 0:n_agg] = rows

    def choose_back(c, carry):
        for p in range(panels):
            for q in range(own_panels):
                goal, lane = place(16, LANES, q * LANES, True)
                rows = pl.ds(p * LANES + c * 16, 16)
                back[rows, q * LANES : (q + 1) * LANES] = jnp.where(
                    goal == (lane + c * 16) * panels + p, 1.0, 0.0
                ).astype(jnp.bfloat16)
        return carry

    next_values = None
    for cycle in range(CYCLES):
        if cycle == 0:
            wait_c()
            values_at = coarse_values()
        else:
            values_at = next_values

        def spread_band(strip, start, chunks):
            west, own, east = values_at[3 * strip : 3 * strip + 3]
            dx = strips[strip][0]
            side = jnp.where(lane8 < LANES // 2, west, east)
            values = [tall(jnp.where(own_lanes(own, p), own, side), ROW_STEP) for p in range(panels)]

            def body(c, carry):
                at = pl.ds(start + c * ROW_STEP, ROW_STEP)
                for p in range(panels):
                    value = ocean[p, at, :] * values[p]
                    odd[p, at, :] = value
                    if dx == 0:
                        inner = pl.ds(start - OWN + c * ROW_STEP, ROW_STEP)
                        sol[p, inner, :] = value if cycle == 0 else sol[p, inner, :] + value
                return carry

            lax.fori_loop(0, chunks, body, 0)

        spread_band(0, PAD, DEPTH // ROW_STEP)
        for t in range(bands):
            spread_band(1 + t, OWN + t * TILE, TILE // ROW_STEP)
        spread_band(1 + bands, OWN + height, DEPTH // ROW_STEP)
        if cycle == 0:
            start_by()

        with_totals = cycle < CYCLES - 1

        def first(r, carry):
            out, values = stencil(odd, r)
            at = pl.ds(r, ROW_STEP)
            for p in range(panels):
                v = res[p, at, :] - shift16 * (0.5 * out[p] + values[p])
                even[p, at, :] = v
                basis[0, p, at, :] = v
                if carry is not None:
                    square, total = carry
                    carry = (
                        add_to(square, p, fold(v * v)),
                        add_to(total, p, fold(v)) if with_totals else total,
                    )
            return carry

        (square,) = over_bands(first, 0, (zero_pair,))
        sums[64:65, :] = jnp.sum(own_total(square), axis=0, keepdims=True)

        def step(j, source, target, is_first=False):
            def chunk(r, carry):
                out, values = stencil(source, r)
                at = pl.ds(r, ROW_STEP)
                for p in range(panels):
                    v = 0.5 * out[p] if is_first else out[p] - target[p, at, :]
                    target[p, at, :] = v
                    basis[j, p, at, :] = v
                    if carry is not None:
                        square, cross, total = carry
                        carry = (
                            add_to(square, p, fold(v * v)),
                            add_to(cross, p, fold(v * values[p])),
                            add_to(total, p, fold(v)) if with_totals else total,
                        )
                return carry

            square, cross = over_bands(chunk, j * bands, (zero_pair, zero_pair))
            sums[row_at(64 + j), :] = jnp.sum(own_total(square), axis=0, keepdims=True)
            sums[row_at(80 + j), :] = jnp.sum(own_total(cross), axis=0, keepdims=True)

        def two_steps(i, carry):
            step(2 * i + 2, odd, even)
            step(2 * i + 3, even, odd)
            return carry

        step(1, even, odd, True)
        lax.fori_loop(0, KB // 2 - 1, two_steps, 0)
        step(KB, odd, even)

        row = lax.dot_general(
            jnp.ones((8, LANES), jnp.float32),
            sums[...],
            (((1,), (1,)), ((), ())),
            precision=highest,
            preferred_element_type=jnp.float32,
        )
        start_g, wait_g, _ = grams[cycle]
        start_g(row[0:1])
        if cycle == 0:
            choose_rows()
            wait_by()
            permute_rows()
        else:
            lax.fori_loop(0, LANES // 16, choose_back, 0)
        wait_g()
        gathered = [gram_all[cycle, 8 * i : 8 * i + 8, :] for i in range(groups)]
        whole = sub_total(functools.reduce(jnp.add, gathered))

        def at_lane(k):
            return jnp.broadcast_to(whole[:, k : k + 1], (8, LANES))

        vv = [at_lane(64 + a) for a in range(KB + 1)]
        vp = [None] + [at_lane(80 + a) for a in range(1, KB + 1)]
        weight, combined = small_solve(vv, vp)
        for j in range(KB):
            factors[j] = weight[j] / shift
        for a in range(KB + 1):
            factors[KB + a] = combined[a]

        if cycle < CYCLES - 1:
            group = lane8 // bands
            mix = jnp.where(group == 0, 1.0, 0.0)
            for a in range(KB + 1):
                mix = jnp.where(group == a, mix - combined[a], mix)
            mix = jnp.where(lane8 < (KB + 1) * bands, mix, 0.0)
            mixed = []
            for part in gathered:
                part = part * mix
                move = bands
                while move < LANES:
                    part = part + pltpu.roll(part, move, 1)
                    move *= 2
                mixed.append(part)
            found = chosen[...] * by_label(mixed)
            found = jnp.broadcast_to(jnp.sum(found, axis=1, keepdims=True), (found.shape[0], LANES))
            next_values = [jnp.broadcast_to(found[k : k + 1, :], (8, LANES)) for k in range(len(labels))]

        w = [tall(factors[j], ROW_STEP) for j in range(KB)]
        c_all = [tall(factors[KB + a], ROW_STEP) for a in range(KB + 1)]

        def update(r, p, inner):
            at = pl.ds(r, ROW_STEP)
            values = [basis[a, p, at, :] for a in range(KB + 1)]
            residual = values[0]
            for a in range(KB + 1):
                residual = residual - c_all[a] * values[a]
            if inner is None:
                res[p, at, :] = residual
                return
            rows = pl.ds(inner, ROW_STEP)
            answer = sol[p, rows, :]
            for j in range(KB):
                answer = answer + w[j] * values[j]
            if cycle < CYCLES - 1:
                res[p, at, :] = residual
                sol[p, rows, :] = answer
            else:
                residual_ref[p, rows, :] = residual
                solution_ref[p, rows, :] = answer

        def update_own(c, carry):
            for p in range(panels):
                update(OWN + c * ROW_STEP, p, c * ROW_STEP)
            return carry

        lax.fori_loop(0, height // ROW_STEP, update_own, 0)
        if cycle < CYCLES - 1:
            for p in range(panels):
                update(PAD, p, None)
                update(OWN + height, p, None)

    for done in finish:
        done()


def to_natural(solution_ref, residual_ref, back, solution_out, residual_out, parts, sems):
    panels, height = solution_ref.shape[:2]
    rows = parts.shape[1]
    copies = []
    for index in range(height // rows):
        at = pl.ds(index * rows, rows)
        for which, (source, target) in enumerate(((solution_ref, solution_out), (residual_ref, residual_out))):
            slot = 2 * index + which
            parts[slot] = placed(jnp.concatenate([source[p, at, :] for p in range(panels)], axis=1), back[...])
            copies.append(pltpu.make_async_copy(parts.at[slot], target.at[at, :], sems.at[slot]))
            copies[-1].start()
    for copy in copies:
        copy.wait()


def on_device(size_x, size_y, forcing, bathymetry, ocean_mask, aggregate_id, coarse_inverse):
    height, breadth = forcing.shape
    own_panels = breadth // LANES
    panels = own_panels + 1
    rows = height + 2 * (DEPTH + PAD)
    bands = height // TILE
    f32 = jnp.float32
    field = pltpu.VMEM((panels, rows, LANES), f32)
    block = pltpu.VMEM((height, breadth), f32)
    any_spec = pl.BlockSpec(memory_space=pltpu.MemorySpace.HBM)
    vmem = pl.BlockSpec(memory_space=pltpu.VMEM)
    smem = pl.BlockSpec(memory_space=pltpu.SMEM)
    rows_all = pltpu.VMEM((size_x * size_y, LANES), f32)
    tiles = lambda *lead: pltpu.VMEM(lead + (8, LANES), f32)
    dma = pltpu.SemaphoreType.DMA
    n_agg = coarse_inverse.shape[1]
    wanted = -(-3 * (bands + 2) // 8) * 8
    dealt = jax.ShapeDtypeStruct((panels, height, LANES), f32)
    back = jax.ShapeDtypeStruct((panels * LANES, breadth), jnp.bfloat16)
    forcing, bathymetry, ocean_mask, aggregate_id, coarse_inverse = (
        pltpu.with_memory_space_constraint(x, pltpu.MemorySpace.HBM)
        for x in (forcing, bathymetry, ocean_mask, aggregate_id, coarse_inverse)
    )
    answer, residual, back = pl.pallas_call(
        functools.partial(kernel, size_x, size_y),
        out_shape=(dealt, dealt, back),
        in_specs=[any_spec, any_spec, any_spec, smem, any_spec],
        out_specs=(vmem, vmem, vmem),
        scratch_shapes=[
            block,
            block,
            pltpu.VMEM((height, breadth), jnp.int32),
            pltpu.VMEM((height, LANES), f32),
            pltpu.VMEM((height, LANES), f32),
            pltpu.VMEM((panels * LANES, panels * LANES), jnp.bfloat16),
            field,
            field,
            field,
            pltpu.VMEM((panels, height, LANES), f32),
            pltpu.VMEM((KB + 1, panels, rows, LANES), f32),
            field,
            field,
            field,
            field,
            field,
            field,
            field,
            pltpu.VMEM((2, height // GROUPS, LANES), f32),
            pltpu.VMEM((2, height // GROUPS, LANES), f32),
            pltpu.VMEM((4, DEPTH, LANES), f32),
            pltpu.VMEM((4, DEPTH, LANES), f32),
            pltpu.VMEM((2, 2, DEPTH, breadth), f32),
            pltpu.VMEM((8, -(-n_agg // LANES) * LANES), f32),
            pltpu.VMEM((wanted, n_agg), f32),
            pltpu.VMEM((wanted, -(-n_agg // LANES) * LANES), f32),
            pltpu.VMEM((size_x, bands, n_agg), f32),
            pltpu.VMEM((size_y, size_x * bands, n_agg), f32),
            pltpu.VMEM((LANES, LANES), f32),
            tiles(2 * KB + 1),
            rows_all,
            rows_all,
            rows_all,
            pltpu.VMEM((CYCLES, size_x * size_y, LANES), f32),
            dma((4,)),
            dma((10,)),
            dma((10,)),
            dma((7,)),
            dma((7,)),
        ],
        compiler_params=pltpu.CompilerParams(
            collective_id=0, has_side_effects=True, vmem_limit_bytes=40 * 1024 * 1024
        ),
    )(forcing, bathymetry, ocean_mask, aggregate_id, coarse_inverse)
    part = 64
    count = 2 * (height // part)
    return pl.pallas_call(
        to_natural,
        out_shape=(jax.ShapeDtypeStruct((height, breadth), f32),) * 2,
        in_specs=[vmem, vmem, vmem],
        out_specs=(any_spec, any_spec),
        scratch_shapes=[pltpu.VMEM((count, part, breadth), f32), dma((count,))],
        compiler_params=pltpu.CompilerParams(vmem_limit_bytes=16 * 1024 * 1024),
    )(answer, residual, back)


def solution(mesh):
    return jax.shard_map(
        functools.partial(on_device, mesh.shape["gx"], mesh.shape["gy"]),
        mesh=mesh,
        in_specs=(
            P("gx", "gy"),
            P("gx", "gy"),
            P("gx", "gy"),
            P("gx", "gy"),
            P(("gx", "gy"), None),
        ),
        out_specs=(P("gx", "gy"), P("gx", "gy")),
        check_vma=False,
    )
```

```python
import functools

import jax
import jax.numpy as jnp
from jax import lax
from jax.experimental import pallas as pl
from jax.experimental.pallas import tpu as pltpu
from jax.sharding import PartitionSpec as P

TILE = 64
KB = 8
CYCLES = 2
SHIFT_REL = 0.001
DEPTH = KB * CYCLES
LANES = 128
PAD = 8
OWN = PAD + DEPTH
ROW_STEP = 16
GROUPS = 4
FIRST = 20
MESH = pl.DeviceIdType.MESH
highest = lax.Precision.HIGHEST
SIDES = ((-1, 0), (1, 0), (0, -1), (0, 1), (-1, -1), (-1, 1), (1, -1), (1, 1))
NORTH, SOUTH, WEST, EAST, NW, NE, SW, SE = range(8)


def sub_total(x):
    for shift in (4, 2, 1):
        x = x + pltpu.roll(x, shift, 0)
    return x


def splat_sum(x):
    return jnp.broadcast_to(jnp.sum(sub_total(x), axis=1, keepdims=True), x.shape)


def fold(x):
    total = x[0:8]
    for start in range(8, x.shape[0], 8):
        total = total + x[start : start + 8]
    return total


def tall(x, rows):
    return jnp.concatenate([x] * (rows // 8), axis=0)


def split(x):
    high = x.astype(jnp.bfloat16)
    return high, (x - high.astype(jnp.float32)).astype(jnp.bfloat16)


def placed(x, chooser):
    rows = x.shape[0]
    both = jnp.dot(jnp.concatenate(split(x), axis=0), chooser, preferred_element_type=jnp.float32)
    return both[0:rows] + both[rows:]


def exact_placed(chooser, x):
    high, rest = split(x)
    low = (x - high.astype(jnp.float32) - rest.astype(jnp.float32)).astype(jnp.bfloat16)
    return sum(jnp.dot(chooser, part, preferred_element_type=jnp.float32) for part in (high, rest, low))


def exact_moved(x, chooser):
    high, rest = split(x)
    low = (x - high.astype(jnp.float32) - rest.astype(jnp.float32)).astype(jnp.bfloat16)
    return sum(jnp.dot(part, chooser, preferred_element_type=jnp.float32) for part in (high, rest, low))


def small_solve(vv, vp):
    n = KB + 1
    moment = [None] * (2 * KB + 1)
    moment[0], moment[1] = vv[0], vp[1]
    for k in range(1, n):
        moment[2 * k] = 2.0 * vv[k] - vv[0]
    for k in range(2, n):
        moment[2 * k - 1] = 2.0 * vp[k] - vp[1]
    upper = [[None] * n for _ in range(n)]
    for j in range(n):
        reduced = vv[j] * (1.0 + SHIFT_REL)
        for k in range(j):
            reduced = reduced - upper[k][j] * upper[k][j]
        root = jnp.sqrt(reduced)
        upper[j][j] = root
        inverse = 1.0 / root
        for i in range(j + 1, n):
            if i - j == 1:
                entry = vp[i]
            else:
                entry = 0.5 * (moment[i + j] + moment[i - j])
            for k in range(j):
                entry = entry - upper[k][j] * upper[k][i]
            upper[j][i] = entry * inverse
    hess = [[None] * KB for _ in range(n)]
    for j in range(KB):
        below = 1.0 if j == 0 else 0.5
        for i in range(j + 2):
            entry = below * upper[i][j + 1]
            if i <= j:
                entry = entry + upper[i][j]
            if i <= j - 1:
                entry = entry + 0.5 * upper[i][j - 1]
            hess[i][j] = entry
    right = [upper[0][0]] + [None] * KB
    for j in range(KB):
        a, b = hess[j][j], hess[j + 1][j]
        inverse = 1.0 / jnp.sqrt(a * a + b * b)
        c, s = a * inverse, b * inverse
        for k in range(j, KB):
            x, y = hess[j][k], hess[j + 1][k]
            if k == j:
                hess[j][k] = c * x + s * y
            else:
                hess[j][k] = c * x + s * y
                hess[j + 1][k] = c * y - s * x
        x = right[j]
        right[j] = c * x
        right[j + 1] = -s * x
    weight = [None] * KB
    for j in range(KB - 1, -1, -1):
        rest = right[j]
        for k in range(j + 1, KB):
            rest = rest - hess[j][k] * weight[k]
        weight[j] = rest / hess[j][j]
    combined = []
    for i in range(n):
        terms = []
        if i < KB:
            terms.append(weight[i])
        if i >= 1:
            terms.append((1.0 if i == 1 else 0.5) * weight[i - 1])
        if i + 1 < KB:
            terms.append(0.5 * weight[i + 1])
        combined.append(functools.reduce(jnp.add, terms))
    return weight, combined


def kernel(
    size_x,
    size_y,
    forcing_ref,
    depth_ref,
    mask_ref,
    agg_ref,
    inverse_ref,
    natural,
    natural_sol,
    factors,
    in_f,
    in_b,
    in_m,
    side_w,
    side_r,
    chooser,
    back,
    wet,
    ocean,
    res,
    sol,
    basis,
    even,
    odd,
    k_south,
    k_north,
    k_east,
    k_west,
    centre,
    send_col,
    got_col,
    send_corner,
    got_corner,
    got_row,
    inverse_rows,
    selector,
    chosen,
    bulk_x,
    bulk_y,
    sums,
    first_all,
    max_all,
    coarse_all,
    gram_all,
    in_sem,
    halo_send,
    halo_recv,
    phase_send,
    phase_recv,
):
    height, breadth = in_f.shape
    own_panels = breadth // LANES
    panels = own_panels + 1
    bands = height // TILE
    n_agg = inverse_ref.shape[1]
    rows_all = wet.shape[1]
    group_rows = height // GROUPS
    gx, gy = lax.axis_index("gx"), lax.axis_index("gy")

    loads = []
    for index, (source, target) in enumerate(
        ((depth_ref, in_b), (mask_ref, in_m), (forcing_ref, in_f), (inverse_ref, bulk_x.at[gx]))
    ):
        copy = pltpu.make_async_copy(source, target, in_sem.at[index])
        copy.start()
        loads.append(copy)
    barrier = pltpu.get_barrier_semaphore()

    def peer_x(d):
        return (lax.rem(gx + d, size_x), gy)

    def peer_y(d):
        return (gx, lax.rem(gy + d, size_y))

    def neighbour(side):
        dx, dy = SIDES[side]
        return (lax.rem(gx + dx + size_x, size_x), lax.rem(gy + dy + size_y, size_y))

    others = size_x * size_y - 1

    xs = [lax.rem(gx + d, size_x) for d in range(size_x)]
    ys = [lax.rem(gy + d, size_y) for d in range(size_y)]

    def hops(d):
        ring = lambda k: min(k, 4 - k)
        dx, dy = divmod(d, size_y)
        return ring(dx // 2) + ring(dy % 4) + ring(dy // 4)

    far_first = sorted(range(1, others + 1), key=lambda d: -hops(d))

    def peer(d):
        return (xs[d // size_y], ys[d % size_y])

    for d in far_first:
        pl.semaphore_signal(barrier, inc=1, device_id=peer(d), device_id_type=MESH)

    sub = lax.broadcasted_iota(jnp.int32, (8, LANES), 0)
    lane8 = lax.broadcasted_iota(jnp.int32, (8, LANES), 1)
    lane16 = lax.broadcasted_iota(jnp.int32, (ROW_STEP, LANES), 1)
    zero8 = jnp.zeros((8, LANES), jnp.float32)

    for p in range(panels):
        for start in (0, rows_all - PAD):
            for array in (wet, even, odd):
                array[p, start : start + PAD, :] = zero8
    sums[...] = jnp.zeros_like(sums)
    def place(rows, columns, column_base, transposed):
        line = lax.broadcasted_iota(jnp.int32, (rows, columns), 1 if transposed else 0) + column_base
        spot = lax.broadcasted_iota(jnp.int32, (rows, columns), 0 if transposed else 1)
        return jnp.where(line < breadth + LANES // 2, line, line - panels * LANES) + FIRST, spot

    def choose(c, carry):
        rows = pl.ds(c * 16, 16)
        for p in range(panels):
            goal, lane = place(16, LANES, c * 16, False)
            chooser[rows, p * LANES : (p + 1) * LANES] = jnp.where(goal == lane * panels + p, 1.0, 0.0).astype(
                jnp.bfloat16
            )
        return carry

    lax.fori_loop(0, panels * LANES // 16, choose, 0)

    for copy in loads:
        copy.wait()
    inverse_rows[...] = jnp.zeros_like(inverse_rows)
    chosen[...] = jnp.zeros_like(chosen)
    inverse_rows[0:bands, 0:n_agg] = bulk_x[gx]

    band_sums = []
    for t in range(bands):

        def prepare(c, total, t=t):
            rows = pl.ds(t * TILE + c * ROW_STEP, ROW_STEP)
            for p in range(own_panels):
                at = pl.ds(p * LANES, LANES)
                sea = in_m[rows, at].astype(jnp.float32)
                value = in_f[rows, at] * sea
                in_b[rows, at] = in_b[rows, at] * sea
                in_f[rows, at] = value
                total = total + fold(value * sea)
            return total

        band_sums.append(splat_sum(lax.fori_loop(0, TILE // ROW_STEP, prepare, zero8)))

    def pack(c, carry):
        r = c * ROW_STEP
        for side, p, base in ((WEST, 0, 0), (EAST, own_panels - 1, LANES - DEPTH)):
            packed = jnp.zeros((ROW_STEP, LANES), jnp.float32)
            for g in range(GROUPS):
                at = pl.ds(g * group_rows + r, ROW_STEP)
                for part, array in enumerate((in_b, in_f)):
                    start = (2 * g + part) * DEPTH
                    moved = pltpu.roll(array[at, p * LANES : (p + 1) * LANES], (start - base) % LANES, 1)
                    packed = jnp.where((lane16 >= start) & (lane16 < start + DEPTH), moved, packed)
            send_col[side - WEST, pl.ds(r, ROW_STEP), :] = packed
        return carry

    lax.fori_loop(0, group_rows // ROW_STEP, pack, 0)
    for index, side in enumerate((NW, NE, SW, SE)):
        dx, dy = SIDES[side]
        p, base = (0, 0) if dy < 0 else (own_panels - 1, LANES - DEPTH)
        start = 0 if dx < 0 else height - DEPTH
        packed = jnp.zeros((DEPTH, LANES), jnp.float32)
        for part, array in enumerate((in_b, in_f)):
            corner = array[start : start + DEPTH, p * LANES : (p + 1) * LANES]
            moved = pltpu.roll(corner, (part * DEPTH - base) % LANES, 1)
            packed = jnp.where((lane16 >= part * DEPTH) & (lane16 < (part + 1) * DEPTH), moved, packed)
        send_corner[index] = packed

    halos = []
    for side in range(8):
        if side in (NORTH, SOUTH):
            start = 0 if side == NORTH else height - DEPTH
            pairs = [
                (array.at[pl.ds(start, DEPTH), :], got_row.at[side, part]) for part, array in enumerate((in_b, in_f))
            ]
        elif side in (WEST, EAST):
            pairs = [(send_col.at[side - WEST], got_col.at[side - WEST])]
        else:
            pairs = [(send_corner.at[side - NW], got_corner.at[side - NW])]
        for part, (source, target) in enumerate(pairs):
            slot = side if part == 0 else 8 + side
            halos.append(
                pltpu.make_async_remote_copy(
                    src_ref=source,
                    dst_ref=target,
                    send_sem=halo_send.at[slot],
                    recv_sem=halo_recv.at[slot],
                    device_id=neighbour(side),
                    device_id_type=MESH,
                )
            )

    def phase(buffer, index, along_x):
        size, me, peer = (size_x, gx, peer_x) if along_x else (size_y, gy, peer_y)

        def far(d):
            ring = lambda k: -min(k, 4 - k)
            return ring(d // 2) if along_x else ring(d % 4) + ring(d // 4)

        def start():
            for d in sorted(range(1, size), key=far):
                pltpu.make_async_remote_copy(
                    src_ref=buffer.at[me],
                    dst_ref=buffer.at[me],
                    send_sem=phase_send.at[index],
                    recv_sem=phase_recv.at[index],
                    device_id=peer(d),
                    device_id_type=MESH,
                ).start()

        def whole():
            part = buffer.at[pl.ds(0, size - 1)]
            return pltpu.make_async_remote_copy(
                src_ref=part,
                dst_ref=part,
                send_sem=phase_send.at[index],
                recv_sem=phase_recv.at[index],
                device_id=peer(1),
                device_id_type=MESH,
            )

        return start, (lambda: whole().wait_recv()), (lambda: whole().wait_send())

    me = gx * size_y + gy

    def direct(buffer, index):
        def start(row):
            buffer[pl.ds(me, 1), :] = row
            mine = buffer.at[pl.ds(me, 1), :]

            for d in far_first:
                pltpu.make_async_remote_copy(
                    src_ref=mine,
                    dst_ref=mine,
                    send_sem=phase_send.at[index],
                    recv_sem=phase_recv.at[index],
                    device_id=peer(d),
                    device_id_type=MESH,
                ).start()

        def whole():
            part = buffer.at[pl.ds(0, others), :]
            return pltpu.make_async_remote_copy(
                src_ref=part,
                dst_ref=part,
                send_sem=phase_send.at[index],
                recv_sem=phase_recv.at[index],
                device_id=peer(1),
                device_id_type=MESH,
            )

        return start, (lambda: whole().wait_recv()), (lambda: whole().wait_send())

    groups = -(-(others + 1) // 8)

    def rows_of(buffer, i):
        return buffer[8 * i : 8 * i + 8, :]

    def by_label(values):
        total = [zero8] * pieces
        for i in range(groups):
            table = rows_of(first_all, i)
            for t in range(bands):
                label = jnp.broadcast_to(table[:, bands + t : bands + t + 1], (8, LANES))
                value = jnp.broadcast_to(values[i][:, t : t + 1], (8, LANES))
                for c in range(pieces):
                    total[c] = total[c] + jnp.where(label == numbers[c], value, 0.0)
        return jnp.concatenate([jnp.sum(x, axis=0, keepdims=True) for x in total], axis=1)

    finish = []

    pieces = -(-n_agg // LANES)
    numbers = [(lane8 + (c * LANES + 1)).astype(jnp.float32) for c in range(pieces)]
    first_row_values = zero8
    for t in range(bands):
        first_row_values = jnp.where(lane8 == t, band_sums[t], first_row_values)
        label = (agg_ref[t, 0] + 1).astype(jnp.float32)
        first_row_values = jnp.where(lane8 == bands + t, label, first_row_values)

    def choose_back(c, carry):
        for p in range(panels):
            for q in range(own_panels):
                goal, lane = place(16, LANES, q * LANES, True)
                rows = pl.ds(p * LANES + c * 16, 16)
                back[rows, q * LANES : (q + 1) * LANES] = jnp.where(
                    goal == (lane + c * 16) * panels + p, 1.0, 0.0
                ).astype(jnp.bfloat16)
        return carry

    lax.fori_loop(0, LANES // 16, choose_back, 0)

    pl.semaphore_wait(barrier, others)
    for copy in halos:
        copy.start()
    start_f, wait_f, done_f = direct(first_all, 0)
    start_m, wait_m, done_m = direct(max_all, 1)
    start_c, wait_c, done_c = direct(coarse_all, 2)
    finish += [done_f, done_m, done_c]
    start_f(first_row_values[0:1])
    start_bx, wait_bx, done_bx = phase(bulk_x, 5, True)
    start_by, wait_by, done_by = phase(bulk_y, 6, False)
    finish += [done_bx, done_by]
    start_bx()

    own_rows = pl.ds(0, breadth)
    block_rows = min(256, height)

    def settle(c, carry):
        rows = pl.ds(c * block_rows, block_rows)
        for source, target in ((in_b, wet), (in_f, res)):
            moved = placed(source[rows, :], chooser[own_rows, :])
            for p in range(panels):
                target[p, pl.ds(OWN + c * block_rows, block_rows), :] = moved[:, p * LANES : (p + 1) * LANES]
        return carry

    lax.fori_loop(0, height // block_rows, settle, 0)

    for copy in halos:
        copy.wait()

    east_lanes = jnp.where(gy < size_y - 1, DEPTH, 0)
    west_lane = jnp.where(gy > 0, LANES - DEPTH, LANES)
    for side, start, inside in ((SOUTH, PAD, gx > 0), (NORTH, OWN + height, gx < size_x - 1)):
        from_east, from_west = (SW, SE) if side == SOUTH else (NW, NE)
        for part, target in enumerate((wet, res)):
            east = pltpu.roll(got_corner[from_east - NW], (-part * DEPTH) % LANES, 1)
            west = pltpu.roll(got_corner[from_west - NW], (-(part + 1) * DEPTH) % LANES, 1)
            corner = jnp.where(lane16 < east_lanes, east, jnp.where(lane16 >= west_lane, west, 0.0))
            whole_row = jnp.concatenate([got_row[side, part], corner], axis=1)
            moved = placed(jnp.where(inside, whole_row, 0.0), chooser[...])
            for p in range(panels):
                target[p, start : start + DEPTH, :] = moved[:, p * LANES : (p + 1) * LANES]

    def unpack(c, carry):
        r = c * ROW_STEP
        east_all = got_col[WEST - WEST, pl.ds(r, ROW_STEP), :]
        west_all = got_col[EAST - WEST, pl.ds(r, ROW_STEP), :]
        for g in range(GROUPS):
            for part, target in enumerate((side_w, side_r)):
                start = (2 * g + part) * DEPTH
                east = pltpu.roll(east_all, (-start) % LANES, 1)
                west = pltpu.roll(west_all, (LANES - DEPTH - start) % LANES, 1)
                target[pl.ds(g * group_rows + r, ROW_STEP), :] = jnp.where(
                    lane16 < east_lanes, east, jnp.where(lane16 >= west_lane, west, 0.0)
                )
        return carry

    lax.fori_loop(0, group_rows // ROW_STEP, unpack, 0)

    def settle_sides(c, carry):
        rows = pl.ds(c * block_rows, block_rows)
        at = pl.ds(OWN + c * block_rows, block_rows)
        for source, target in ((side_w, wet), (side_r, res)):
            moved = placed(source[rows, :], chooser[pl.ds(breadth, LANES), :])
            for p in range(panels):
                target[p, at, :] = target[p, at, :] + moved[:, p * LANES : (p + 1) * LANES]
        return carry

    lax.fori_loop(0, height // block_rows, settle_sides, 0)

    def east_west(values):
        easts = values[1:] + [pltpu.roll(values[0], LANES - 1, 1)]
        wests = [pltpu.roll(values[-1], 1, 1)] + values[:-1]
        return easts, wests

    last, extra = divmod(breadth + FIRST, panels)
    first_lane = FIRST // panels

    def own_lanes(x, p):
        lane = lax.broadcasted_iota(jnp.int32, x.shape, 1)
        return (lane >= first_lane) & (lane < last + (1 if p < extra else 0))

    def kind(p):
        return 0 if p < extra else 1

    def own_total(parts):
        return jnp.where(own_lanes(parts[0], 0), parts[0], 0.0) + jnp.where(
            own_lanes(parts[1], panels - 1), parts[1], 0.0
        )

    def add_to(pair, p, x):
        return tuple(total + x if i == kind(p) else total for i, total in enumerate(pair))

    zero_pair = (zero8, zero8)

    def row_at(i):
        return pl.ds(i, 1)

    def faces(r, top):
        values = [wet[p, pl.ds(r, ROW_STEP), :] for p in range(panels)]
        easts, wests = east_west(values)
        for p in range(panels):
            at = pl.ds(r, ROW_STEP)
            south = jnp.minimum(values[p], wet[p, pl.ds(r + 1, ROW_STEP), :])
            north = jnp.minimum(values[p], wet[p, pl.ds(r - 1, ROW_STEP), :])
            east = jnp.minimum(values[p], easts[p])
            west = jnp.minimum(values[p], wests[p])
            k_south[p, at, :] = south
            k_north[p, at, :] = north
            k_east[p, at, :] = east
            k_west[p, at, :] = west
            diagonal = 1.0 + south + north + east + west
            centre[p, at, :] = diagonal
            ocean[p, at, :] = jnp.where(values[p] > 0.0, 1.0, 0.0)
            if top is not None:
                for start in range(0, ROW_STEP, 8):
                    part = diagonal[start : start + 8]
                    top = tuple(jnp.maximum(t, part) if i == kind(p) else t for i, t in enumerate(top))
        return top

    top = lax.fori_loop(
        0, height // ROW_STEP, lambda c, top: faces(OWN + c * ROW_STEP, top), (jnp.ones((8, LANES), jnp.float32),) * 2
    )
    top = jnp.maximum(
        jnp.where(own_lanes(top[0], 0), top[0], 1.0), jnp.where(own_lanes(top[1], panels - 1), top[1], 1.0)
    )
    start_m(jnp.max(top, axis=0, keepdims=True))
    faces(PAD, None)
    faces(OWN + height, None)

    wait_f()
    rhs = by_label([rows_of(first_all, i) for i in range(groups)])
    coarse_row = jnp.zeros((1, LANES), jnp.float32)
    lane1 = lax.broadcasted_iota(jnp.int32, (1, LANES), 1)
    for s in range(bands):
        product = jnp.sum(inverse_rows[s : s + 1, :] * rhs, axis=1, keepdims=True)
        coarse_row = jnp.where(lax.rem(lane1, bands) == s, product, coarse_row)
    start_c(coarse_row)

    strips = [(-1, bands - 1)] + [(0, t) for t in range(bands)] + [(1, 0)]
    labels = []
    for dx, t in strips:
        for dy in (-1, 0, 1):
            inside = (gx + dx >= 0) & (gx + dx < size_x) & (gy + dy >= 0) & (gy + dy < size_y)
            device = jnp.where(inside, me + dx * size_y + dy, me)
            label = first_all[pl.ds(device, 1), :][:, bands + t : bands + t + 1]
            label = jnp.broadcast_to(label, (1, LANES))
            labels.append(jnp.where(inside, label, 0.0))

    wait_bx()
    for i in range(size_x):
        bulk_y[gy, i * bands : (i + 1) * bands, :] = bulk_x[i]

    wait_m()
    largest = functools.reduce(jnp.maximum, [rows_of(max_all, i) for i in range(groups)])
    for move in (4, 2, 1):
        largest = jnp.maximum(largest, pltpu.roll(largest, move, 0))
    shift = jnp.broadcast_to(jnp.max(largest, axis=1, keepdims=True), (8, LANES))
    scale = 2.0 / shift
    scale16 = tall(scale, ROW_STEP)

    def rescale(c, carry):
        at = pl.ds(PAD + c * ROW_STEP, ROW_STEP)
        for p in range(panels):
            for array in (k_south, k_north, k_east, k_west):
                array[p, at, :] = array[p, at, :] * scale16
            centre[p, at, :] = centre[p, at, :] * scale16 - 2.0
        return carry

    chunks_all = (rows_all - 2 * PAD) // ROW_STEP
    lax.fori_loop(0, chunks_all, rescale, 0)

    def stencil(array, r):
        at = pl.ds(r, ROW_STEP)
        values = [array[p, at, :] for p in range(panels)]
        easts, wests = east_west(values)
        out = []
        for p in range(panels):
            south = array[p, pl.ds(r + 1, ROW_STEP), :]
            north = array[p, pl.ds(r - 1, ROW_STEP), :]
            flow = k_south[p, at, :] * south + k_north[p, at, :] * north
            flow = flow + (k_east[p, at, :] * easts[p] + k_west[p, at, :] * wests[p])
            out.append(centre[p, at, :] * values[p] - flow)
        return out, values

    def over_bands(chunk, first_sums, run):
        chunk(PAD, None)
        chunk(OWN + height, None)

        def band(t, carry):
            carry = carry + (zero_pair,)
            for c in range(TILE // ROW_STEP):
                carry = chunk(pl.multiple_of(OWN + t * TILE + c * ROW_STEP, 8), carry)
            sums[pl.ds(first_sums + t, 1), :] = jnp.sum(own_total(carry[-1]), axis=0, keepdims=True)
            return carry[:-1]

        return lax.fori_loop(0, bands, band, run)

    shift16 = tall(shift, ROW_STEP)
    grams = [direct(gram_all.at[c], 3 + c) for c in range(CYCLES)]
    finish += [p[2] for p in grams]

    def coarse_values():
        row = jnp.zeros((1, LANES), jnp.float32)
        for k, label in enumerate(labels):
            row = jnp.where(lax.div(lane1, bands) == k, label, row)
        total = zero8
        for i in range(groups):
            number = ((8 * i + sub) * bands + lax.rem(lane8, bands) + 1).astype(jnp.float32)
            total = total + jnp.where(number == row, rows_of(coarse_all, i), 0.0)
        total = sub_total(total)
        found = []
        for k in range(len(labels)):
            picked = jnp.where(lax.div(lane8, bands) == k, total, 0.0)
            found.append(jnp.broadcast_to(jnp.sum(picked, axis=1, keepdims=True), (8, LANES)))
        return found

    def choose_rows():
        slot = lax.broadcasted_iota(jnp.int32, (1, n_agg), 1)
        in_slot = lax.rem(slot, size_x * bands)
        row = (lax.div(in_slot, bands) * size_y + lax.div(slot, size_x * bands)) * bands + lax.rem(in_slot, bands)
        selector[...] = jnp.zeros_like(selector)
        for k, label in enumerate(labels):
            wide = jnp.concatenate([label] * pieces, axis=1)[:, 0:n_agg]
            selector[k : k + 1, :] = jnp.where((row + 1).astype(jnp.float32) == wide, 1.0, 0.0)

    def permute_rows():
        chunks = max(1, n_agg // LANES)
        width, per = n_agg // chunks, size_y // chunks
        rows = None
        for c in range(chunks):
            part = exact_placed(
                selector[:, c * width : (c + 1) * width].astype(jnp.bfloat16),
                jnp.concatenate([bulk_y[c * per + i] for i in range(per)], axis=0),
            )
            rows = part if rows is None else rows + part
        chosen[:, 0:n_agg] = rows

    blocks = height // block_rows

    def basis_to_natural(i, carry):
        a, c = lax.div(i, blocks), lax.rem(i, blocks)
        at = pl.ds(pl.multiple_of(OWN + c * block_rows, 8), block_rows)
        rows = pl.ds(pl.multiple_of(c * block_rows, 8), block_rows)
        natural[a, rows, :] = placed(jnp.concatenate([basis[a, p, at, :] for p in range(panels)], axis=1), back[...])
        return carry

    def sol_to_natural(c, carry):
        rows = pl.ds(c * block_rows, block_rows)
        natural_sol[rows, :] = placed(jnp.concatenate([sol[p, rows, :] for p in range(panels)], axis=1), back[...])
        return carry

    next_values = None
    for cycle in range(CYCLES):
        if cycle == 0:
            wait_c()
            values_at = coarse_values()
        else:
            values_at = next_values

        def spread_band(strip, start, chunks):
            west, own, east = values_at[3 * strip : 3 * strip + 3]
            dx = strips[strip][0]
            side = jnp.where(lane8 < LANES // 2, west, east)
            values = [tall(jnp.where(own_lanes(own, p), own, side), ROW_STEP) for p in range(panels)]

            def body(c, carry):
                at = pl.ds(start + c * ROW_STEP, ROW_STEP)
                for p in range(panels):
                    value = ocean[p, at, :] * values[p]
                    odd[p, at, :] = value
                    if dx == 0:
                        inner = pl.ds(start - OWN + c * ROW_STEP, ROW_STEP)
                        sol[p, inner, :] = value if cycle == 0 else sol[p, inner, :] + value
                return carry

            lax.fori_loop(0, chunks, body, 0)

        spread_band(0, PAD, DEPTH // ROW_STEP)
        for t in range(bands):
            spread_band(1 + t, OWN + t * TILE, TILE // ROW_STEP)
        spread_band(1 + bands, OWN + height, DEPTH // ROW_STEP)
        if cycle == 0:
            start_by()

        with_totals = cycle < CYCLES - 1

        def first(r, carry):
            out, values = stencil(odd, r)
            at = pl.ds(r, ROW_STEP)
            for p in range(panels):
                v = res[p, at, :] - shift16 * (0.5 * out[p] + values[p])
                even[p, at, :] = v
                basis[0, p, at, :] = v
                if carry is not None:
                    square, total = carry
                    carry = (
                        add_to(square, p, fold(v * v)),
                        add_to(total, p, fold(v)) if with_totals else total,
                    )
            return carry

        (square,) = over_bands(first, 0, (zero_pair,))
        sums[64:65, :] = jnp.sum(own_total(square), axis=0, keepdims=True)

        def step(j, source, target, is_first=False):
            def chunk(r, carry):
                out, values = stencil(source, r)
                at = pl.ds(r, ROW_STEP)
                for p in range(panels):
                    v = 0.5 * out[p] if is_first else out[p] - target[p, at, :]
                    target[p, at, :] = v
                    basis[j, p, at, :] = v
                    if carry is not None:
                        square, cross, total = carry
                        carry = (
                            add_to(square, p, fold(v * v)),
                            add_to(cross, p, fold(v * values[p])),
                            add_to(total, p, fold(v)) if with_totals else total,
                        )
                return carry

            square, cross = over_bands(chunk, j * bands, (zero_pair, zero_pair))
            sums[row_at(64 + j), :] = jnp.sum(own_total(square), axis=0, keepdims=True)
            sums[row_at(80 + j), :] = jnp.sum(own_total(cross), axis=0, keepdims=True)

        def two_steps(i, carry):
            step(2 * i + 2, odd, even)
            step(2 * i + 3, even, odd)
            return carry

        step(1, even, odd, True)
        lax.fori_loop(0, KB // 2 - 1, two_steps, 0)
        step(KB, odd, even)

        row = lax.dot_general(
            jnp.ones((8, LANES), jnp.float32),
            sums[...],
            (((1,), (1,)), ((), ())),
            precision=highest,
            preferred_element_type=jnp.float32,
        )
        start_g, wait_g, _ = grams[cycle]
        start_g(row[0:1])
        if cycle == 0:
            choose_rows()
            wait_by()
            permute_rows()
        else:
            lax.fori_loop(0, (KB + 1) * blocks, basis_to_natural, 0)
            lax.fori_loop(0, blocks, sol_to_natural, 0)
        wait_g()
        gathered = [gram_all[cycle, 8 * i : 8 * i + 8, :] for i in range(groups)]
        whole = sub_total(functools.reduce(jnp.add, gathered))

        def at_lane(k):
            return jnp.broadcast_to(whole[:, k : k + 1], (8, LANES))

        vv = [at_lane(64 + a) for a in range(KB + 1)]
        vp = [None] + [at_lane(80 + a) for a in range(1, KB + 1)]
        weight, combined = small_solve(vv, vp)
        for j in range(KB):
            factors[j] = weight[j] / shift
        for a in range(KB + 1):
            factors[KB + a] = combined[a]

        if cycle < CYCLES - 1:
            group = lane8 // bands
            mix = jnp.where(group == 0, 1.0, 0.0)
            for a in range(KB + 1):
                mix = jnp.where(group == a, mix - combined[a], mix)
            mix = jnp.where(lane8 < (KB + 1) * bands, mix, 0.0)
            mixed = []
            for part in gathered:
                part = part * mix
                move = bands
                while move < LANES:
                    part = part + pltpu.roll(part, move, 1)
                    move *= 2
                mixed.append(part)
            found = chosen[...] * by_label(mixed)
            found = jnp.broadcast_to(jnp.sum(found, axis=1, keepdims=True), (found.shape[0], LANES))
            next_values = [jnp.broadcast_to(found[k : k + 1, :], (8, LANES)) for k in range(len(labels))]

        if cycle == CYCLES - 1:
            break
        w = [tall(factors[j], ROW_STEP) for j in range(KB)]
        c_all = [tall(factors[KB + a], ROW_STEP) for a in range(KB + 1)]

        def update(r, p, inner):
            at = pl.ds(r, ROW_STEP)
            values = [basis[a, p, at, :] for a in range(KB + 1)]
            residual = values[0]
            for a in range(KB + 1):
                residual = residual - c_all[a] * values[a]
            if inner is None:
                res[p, at, :] = residual
                return
            rows = pl.ds(inner, ROW_STEP)
            answer = sol[p, rows, :]
            for j in range(KB):
                answer = answer + w[j] * values[j]
            res[p, at, :] = residual
            sol[p, rows, :] = answer

        def update_own(c, carry):
            for p in range(panels):
                update(OWN + c * ROW_STEP, p, c * ROW_STEP)
            return carry

        lax.fori_loop(0, height // ROW_STEP, update_own, 0)
        for p in range(panels):
            update(PAD, p, None)
            update(OWN + height, p, None)

    for done in finish:
        done()


def combine(natural, natural_sol, factors, solution_out, residual_out, parts, sems):
    height, breadth = natural_sol.shape
    rows = parts.shape[1]
    copies = []
    for index in range(height // rows):

        def chunk(c, carry, index=index):
            at = pl.ds(index * rows + c * ROW_STEP, ROW_STEP)
            there = pl.ds(c * ROW_STEP, ROW_STEP)
            for p in range(breadth // LANES):
                columns = slice(p * LANES, (p + 1) * LANES)
                values = [natural[a, at, columns] for a in range(KB + 1)]
                answer, residual = natural_sol[at, columns], values[0]
                for a in range(KB + 1):
                    residual = residual - tall(factors[KB + a], ROW_STEP) * values[a]
                for j in range(KB):
                    answer = answer + tall(factors[j], ROW_STEP) * values[j]
                parts[2 * index, there, columns] = answer
                parts[2 * index + 1, there, columns] = residual
            return carry

        lax.fori_loop(0, rows // ROW_STEP, chunk, 0)
        for which, target in enumerate((solution_out, residual_out)):
            slot = 2 * index + which
            copy = pltpu.make_async_copy(parts.at[slot], target.at[pl.ds(index * rows, rows), :], sems.at[slot])
            copy.start()
            copies.append(copy)
    for copy in copies:
        copy.wait()


def on_device(size_x, size_y, forcing, bathymetry, ocean_mask, aggregate_id, coarse_inverse):
    height, breadth = forcing.shape
    own_panels = breadth // LANES
    panels = own_panels + 1
    rows = height + 2 * (DEPTH + PAD)
    bands = height // TILE
    f32 = jnp.float32
    field = pltpu.VMEM((panels, rows, LANES), f32)
    block = pltpu.VMEM((height, breadth), f32)
    any_spec = pl.BlockSpec(memory_space=pltpu.MemorySpace.HBM)
    vmem = pl.BlockSpec(memory_space=pltpu.VMEM)
    smem = pl.BlockSpec(memory_space=pltpu.SMEM)
    rows_all = pltpu.VMEM((size_x * size_y, LANES), f32)
    tiles = lambda *lead: pltpu.VMEM(lead + (8, LANES), f32)
    dma = pltpu.SemaphoreType.DMA
    n_agg = coarse_inverse.shape[1]
    wanted = -(-3 * (bands + 2) // 8) * 8
    results = (
        jax.ShapeDtypeStruct((KB + 1, height, breadth), f32),
        jax.ShapeDtypeStruct((height, breadth), f32),
        jax.ShapeDtypeStruct((2 * KB + 1, 8, LANES), f32),
    )
    forcing, bathymetry, ocean_mask, aggregate_id, coarse_inverse = (
        pltpu.with_memory_space_constraint(x, pltpu.MemorySpace.HBM)
        for x in (forcing, bathymetry, ocean_mask, aggregate_id, coarse_inverse)
    )
    natural, natural_sol, factors = pl.pallas_call(
        functools.partial(kernel, size_x, size_y),
        out_shape=results,
        in_specs=[any_spec, any_spec, any_spec, smem, any_spec],
        out_specs=(vmem, vmem, vmem),
        scratch_shapes=[
            block,
            block,
            pltpu.VMEM((height, breadth), jnp.int32),
            pltpu.VMEM((height, LANES), f32),
            pltpu.VMEM((height, LANES), f32),
            pltpu.VMEM((panels * LANES, panels * LANES), jnp.bfloat16),
            pltpu.VMEM((panels * LANES, breadth), jnp.bfloat16),
            field,
            field,
            field,
            pltpu.VMEM((panels, height, LANES), f32),
            pltpu.VMEM((KB + 1, panels, rows, LANES), f32),
            field,
            field,
            field,
            field,
            field,
            field,
            field,
            pltpu.VMEM((2, height // GROUPS, LANES), f32),
            pltpu.VMEM((2, height // GROUPS, LANES), f32),
            pltpu.VMEM((4, DEPTH, LANES), f32),
            pltpu.VMEM((4, DEPTH, LANES), f32),
            pltpu.VMEM((2, 2, DEPTH, breadth), f32),
            pltpu.VMEM((8, -(-n_agg // LANES) * LANES), f32),
            pltpu.VMEM((wanted, n_agg), f32),
            pltpu.VMEM((wanted, -(-n_agg // LANES) * LANES), f32),
            pltpu.VMEM((size_x, bands, n_agg), f32),
            pltpu.VMEM((size_y, size_x * bands, n_agg), f32),
            pltpu.VMEM((LANES, LANES), f32),
            rows_all,
            rows_all,
            rows_all,
            pltpu.VMEM((CYCLES, size_x * size_y, LANES), f32),
            dma((4,)),
            dma((10,)),
            dma((10,)),
            dma((7,)),
            dma((7,)),
        ],
        compiler_params=pltpu.CompilerParams(
            collective_id=0, has_side_effects=True, vmem_limit_bytes=40 * 1024 * 1024
        ),
    )(forcing, bathymetry, ocean_mask, aggregate_id, coarse_inverse)
    part = 64
    count = 2 * (height // part)
    return pl.pallas_call(
        combine,
        out_shape=(jax.ShapeDtypeStruct((height, breadth), f32),) * 2,
        in_specs=[vmem, vmem, vmem],
        out_specs=(any_spec, any_spec),
        scratch_shapes=[pltpu.VMEM((count, part, breadth), f32), dma((count,))],
        compiler_params=pltpu.CompilerParams(vmem_limit_bytes=16 * 1024 * 1024),
    )(natural, natural_sol, factors)


def solution(mesh):
    return jax.shard_map(
        functools.partial(on_device, mesh.shape["gx"], mesh.shape["gy"]),
        mesh=mesh,
        in_specs=(
            P("gx", "gy"),
            P("gx", "gy"),
            P("gx", "gy"),
            P("gx", "gy"),
            P(("gx", "gy"), None),
        ),
        out_specs=(P("gx", "gy"), P("gx", "gy")),
        check_vma=False,
    )
```

```python
import functools

import jax
import jax.numpy as jnp
from jax import lax
from jax.experimental import pallas as pl
from jax.experimental.pallas import tpu as pltpu
from jax.sharding import PartitionSpec as P

TILE = 64
KB = 8
CYCLES = 2
SHIFT_REL = 0.001
DEPTH = KB * CYCLES
LANES = 128
PAD = 8
OWN = PAD + DEPTH
ROW_STEP = 16
GROUPS = 4
FIRST = 20
MESH = pl.DeviceIdType.MESH
highest = lax.Precision.HIGHEST
SIDES = ((-1, 0), (1, 0), (0, -1), (0, 1), (-1, -1), (-1, 1), (1, -1), (1, 1))
NORTH, SOUTH, WEST, EAST, NW, NE, SW, SE = range(8)


def sub_total(x):
    for shift in (4, 2, 1):
        x = x + pltpu.roll(x, shift, 0)
    return x


def splat_sum(x):
    return jnp.broadcast_to(jnp.sum(sub_total(x), axis=1, keepdims=True), x.shape)


def fold(x):
    total = x[0:8]
    for start in range(8, x.shape[0], 8):
        total = total + x[start : start + 8]
    return total


def tall(x, rows):
    return jnp.concatenate([x] * (rows // 8), axis=0)


def split(x):
    high = x.astype(jnp.bfloat16)
    return high, (x - high.astype(jnp.float32)).astype(jnp.bfloat16)


def placed(x, chooser):
    rows = x.shape[0]
    both = jnp.dot(jnp.concatenate(split(x), axis=0), chooser, preferred_element_type=jnp.float32)
    return both[0:rows] + both[rows:]


def exact_placed(chooser, x):
    high, rest = split(x)
    low = (x - high.astype(jnp.float32) - rest.astype(jnp.float32)).astype(jnp.bfloat16)
    return sum(jnp.dot(chooser, part, preferred_element_type=jnp.float32) for part in (high, rest, low))


def exact_moved(x, chooser):
    high, rest = split(x)
    low = (x - high.astype(jnp.float32) - rest.astype(jnp.float32)).astype(jnp.bfloat16)
    return sum(jnp.dot(part, chooser, preferred_element_type=jnp.float32) for part in (high, rest, low))


def small_solve(vv, vp):
    n = KB + 1
    moment = [None] * (2 * KB + 1)
    moment[0], moment[1] = vv[0], vp[1]
    for k in range(1, n):
        moment[2 * k] = 2.0 * vv[k] - vv[0]
    for k in range(2, n):
        moment[2 * k - 1] = 2.0 * vp[k] - vp[1]
    upper = [[None] * n for _ in range(n)]
    for j in range(n):
        reduced = vv[j] * (1.0 + SHIFT_REL)
        for k in range(j):
            reduced = reduced - upper[k][j] * upper[k][j]
        root = jnp.sqrt(reduced)
        upper[j][j] = root
        inverse = 1.0 / root
        for i in range(j + 1, n):
            if i - j == 1:
                entry = vp[i]
            else:
                entry = 0.5 * (moment[i + j] + moment[i - j])
            for k in range(j):
                entry = entry - upper[k][j] * upper[k][i]
            upper[j][i] = entry * inverse
    hess = [[None] * KB for _ in range(n)]
    for j in range(KB):
        below = 1.0 if j == 0 else 0.5
        for i in range(j + 2):
            entry = below * upper[i][j + 1]
            if i <= j:
                entry = entry + upper[i][j]
            if i <= j - 1:
                entry = entry + 0.5 * upper[i][j - 1]
            hess[i][j] = entry
    right = [upper[0][0]] + [None] * KB
    for j in range(KB):
        a, b = hess[j][j], hess[j + 1][j]
        inverse = 1.0 / jnp.sqrt(a * a + b * b)
        c, s = a * inverse, b * inverse
        for k in range(j, KB):
            x, y = hess[j][k], hess[j + 1][k]
            if k == j:
                hess[j][k] = c * x + s * y
            else:
                hess[j][k] = c * x + s * y
                hess[j + 1][k] = c * y - s * x
        x = right[j]
        right[j] = c * x
        right[j + 1] = -s * x
    weight = [None] * KB
    for j in range(KB - 1, -1, -1):
        rest = right[j]
        for k in range(j + 1, KB):
            rest = rest - hess[j][k] * weight[k]
        weight[j] = rest / hess[j][j]
    combined = []
    for i in range(n):
        terms = []
        if i < KB:
            terms.append(weight[i])
        if i >= 1:
            terms.append((1.0 if i == 1 else 0.5) * weight[i - 1])
        if i + 1 < KB:
            terms.append(0.5 * weight[i + 1])
        combined.append(functools.reduce(jnp.add, terms))
    return weight, combined


def kernel(
    size_x,
    size_y,
    forcing_ref,
    depth_ref,
    mask_ref,
    agg_ref,
    inverse_ref,
    natural,
    natural_sol,
    factors,
    in_f,
    in_b,
    in_m,
    side_w,
    side_r,
    chooser,
    back,
    wet,
    ocean,
    res,
    sol,
    basis,
    even,
    odd,
    k_south,
    k_north,
    k_east,
    k_west,
    centre,
    send_col,
    got_col,
    send_corner,
    got_corner,
    got_row,
    inverse_rows,
    selector,
    chosen,
    bulk_x,
    bulk_y,
    sums,
    first_all,
    max_all,
    coarse_all,
    gram_all,
    in_sem,
    halo_send,
    halo_recv,
    phase_send,
    phase_recv,
):
    height, breadth = in_f.shape
    own_panels = breadth // LANES
    panels = own_panels + 1
    bands = height // TILE
    n_agg = inverse_ref.shape[1]
    rows_all = wet.shape[1]
    group_rows = height // GROUPS
    gx, gy = lax.axis_index("gx"), lax.axis_index("gy")

    loads = []
    for index, (source, target) in enumerate(
        ((depth_ref, in_b), (mask_ref, in_m), (forcing_ref, in_f), (inverse_ref, bulk_x.at[gx]))
    ):
        copy = pltpu.make_async_copy(source, target, in_sem.at[index])
        copy.start()
        loads.append(copy)
    barrier = pltpu.get_barrier_semaphore()

    def peer_x(d):
        return (lax.rem(gx + d, size_x), gy)

    def peer_y(d):
        return (gx, lax.rem(gy + d, size_y))

    def neighbour(side):
        dx, dy = SIDES[side]
        return (lax.rem(gx + dx + size_x, size_x), lax.rem(gy + dy + size_y, size_y))

    others = size_x * size_y - 1

    xs = [lax.rem(gx + d, size_x) for d in range(size_x)]
    ys = [lax.rem(gy + d, size_y) for d in range(size_y)]

    def hops(d):
        ring = lambda k: min(k, 4 - k)
        dx, dy = divmod(d, size_y)
        return ring(dx // 2) + ring(dy % 4) + ring(dy // 4)

    far_first = sorted(range(1, others + 1), key=lambda d: -hops(d))

    def peer(d):
        return (xs[d // size_y], ys[d % size_y])

    for d in far_first:
        pl.semaphore_signal(barrier, inc=1, device_id=peer(d), device_id_type=MESH)

    sub = lax.broadcasted_iota(jnp.int32, (8, LANES), 0)
    lane8 = lax.broadcasted_iota(jnp.int32, (8, LANES), 1)
    lane16 = lax.broadcasted_iota(jnp.int32, (ROW_STEP, LANES), 1)
    zero8 = jnp.zeros((8, LANES), jnp.float32)

    for p in range(panels):
        for start in (0, rows_all - PAD):
            for array in (wet, even, odd):
                array[p, start : start + PAD, :] = zero8
    sums[...] = jnp.zeros_like(sums)
    def place(rows, columns, column_base, transposed):
        line = lax.broadcasted_iota(jnp.int32, (rows, columns), 1 if transposed else 0) + column_base
        spot = lax.broadcasted_iota(jnp.int32, (rows, columns), 0 if transposed else 1)
        return jnp.where(line < breadth + LANES // 2, line, line - panels * LANES) + FIRST, spot

    def choose(c, carry):
        rows = pl.ds(c * 16, 16)
        for p in range(panels):
            goal, lane = place(16, LANES, c * 16, False)
            chooser[rows, p * LANES : (p + 1) * LANES] = jnp.where(goal == lane * panels + p, 1.0, 0.0).astype(
                jnp.bfloat16
            )
        return carry

    lax.fori_loop(0, panels * LANES // 16, choose, 0)

    for copy in loads:
        copy.wait()
    inverse_rows[...] = jnp.zeros_like(inverse_rows)
    chosen[...] = jnp.zeros_like(chosen)
    inverse_rows[0:bands, 0:n_agg] = bulk_x[gx]

    band_sums = []
    for t in range(bands):

        def prepare(c, total, t=t):
            rows = pl.ds(t * TILE + c * ROW_STEP, ROW_STEP)
            for p in range(own_panels):
                at = pl.ds(p * LANES, LANES)
                sea = in_m[rows, at].astype(jnp.float32)
                value = in_f[rows, at] * sea
                in_b[rows, at] = in_b[rows, at] * sea
                in_f[rows, at] = value
                total = total + fold(value * sea)
            return total

        band_sums.append(splat_sum(lax.fori_loop(0, TILE // ROW_STEP, prepare, zero8)))

    def pack(c, carry):
        r = c * ROW_STEP
        for side, p, base in ((WEST, 0, 0), (EAST, own_panels - 1, LANES - DEPTH)):
            packed = jnp.zeros((ROW_STEP, LANES), jnp.float32)
            for g in range(GROUPS):
                at = pl.ds(g * group_rows + r, ROW_STEP)
                for part, array in enumerate((in_b, in_f)):
                    start = (2 * g + part) * DEPTH
                    moved = pltpu.roll(array[at, p * LANES : (p + 1) * LANES], (start - base) % LANES, 1)
                    packed = jnp.where((lane16 >= start) & (lane16 < start + DEPTH), moved, packed)
            send_col[side - WEST, pl.ds(r, ROW_STEP), :] = packed
        return carry

    lax.fori_loop(0, group_rows // ROW_STEP, pack, 0)
    for index, side in enumerate((NW, NE, SW, SE)):
        dx, dy = SIDES[side]
        p, base = (0, 0) if dy < 0 else (own_panels - 1, LANES - DEPTH)
        start = 0 if dx < 0 else height - DEPTH
        packed = jnp.zeros((DEPTH, LANES), jnp.float32)
        for part, array in enumerate((in_b, in_f)):
            corner = array[start : start + DEPTH, p * LANES : (p + 1) * LANES]
            moved = pltpu.roll(corner, (part * DEPTH - base) % LANES, 1)
            packed = jnp.where((lane16 >= part * DEPTH) & (lane16 < (part + 1) * DEPTH), moved, packed)
        send_corner[index] = packed

    halos = []
    for side in range(8):
        if side in (NORTH, SOUTH):
            start = 0 if side == NORTH else height - DEPTH
            pairs = [
                (array.at[pl.ds(start, DEPTH), :], got_row.at[side, part]) for part, array in enumerate((in_b, in_f))
            ]
        elif side in (WEST, EAST):
            pairs = [(send_col.at[side - WEST], got_col.at[side - WEST])]
        else:
            pairs = [(send_corner.at[side - NW], got_corner.at[side - NW])]
        for part, (source, target) in enumerate(pairs):
            slot = side if part == 0 else 8 + side
            halos.append(
                pltpu.make_async_remote_copy(
                    src_ref=source,
                    dst_ref=target,
                    send_sem=halo_send.at[slot],
                    recv_sem=halo_recv.at[slot],
                    device_id=neighbour(side),
                    device_id_type=MESH,
                )
            )

    def phase(buffer, index, along_x):
        size, me, peer = (size_x, gx, peer_x) if along_x else (size_y, gy, peer_y)

        def far(d):
            ring = lambda k: -min(k, 4 - k)
            return ring(d // 2) if along_x else ring(d % 4) + ring(d // 4)

        def start():
            for d in sorted(range(1, size), key=far):
                pltpu.make_async_remote_copy(
                    src_ref=buffer.at[me],
                    dst_ref=buffer.at[me],
                    send_sem=phase_send.at[index],
                    recv_sem=phase_recv.at[index],
                    device_id=peer(d),
                    device_id_type=MESH,
                ).start()

        def whole():
            part = buffer.at[pl.ds(0, size - 1)]
            return pltpu.make_async_remote_copy(
                src_ref=part,
                dst_ref=part,
                send_sem=phase_send.at[index],
                recv_sem=phase_recv.at[index],
                device_id=peer(1),
                device_id_type=MESH,
            )

        return start, (lambda: whole().wait_recv()), (lambda: whole().wait_send())

    me = gx * size_y + gy

    def direct(buffer, index):
        def start(row):
            buffer[pl.ds(me, 1), :] = row
            mine = buffer.at[pl.ds(me, 1), :]

            for d in far_first:
                pltpu.make_async_remote_copy(
                    src_ref=mine,
                    dst_ref=mine,
                    send_sem=phase_send.at[index],
                    recv_sem=phase_recv.at[index],
                    device_id=peer(d),
                    device_id_type=MESH,
                ).start()

        def whole():
            part = buffer.at[pl.ds(0, others), :]
            return pltpu.make_async_remote_copy(
                src_ref=part,
                dst_ref=part,
                send_sem=phase_send.at[index],
                recv_sem=phase_recv.at[index],
                device_id=peer(1),
                device_id_type=MESH,
            )

        return start, (lambda: whole().wait_recv()), (lambda: whole().wait_send())

    groups = -(-(others + 1) // 8)

    def rows_of(buffer, i):
        return buffer[8 * i : 8 * i + 8, :]

    def by_label(values):
        total = [zero8] * pieces
        for i in range(groups):
            table = rows_of(first_all, i)
            for t in range(bands):
                label = jnp.broadcast_to(table[:, bands + t : bands + t + 1], (8, LANES))
                value = jnp.broadcast_to(values[i][:, t : t + 1], (8, LANES))
                for c in range(pieces):
                    total[c] = total[c] + jnp.where(label == numbers[c], value, 0.0)
        return jnp.concatenate([jnp.sum(x, axis=0, keepdims=True) for x in total], axis=1)

    finish = []

    pieces = -(-n_agg // LANES)
    numbers = [(lane8 + (c * LANES + 1)).astype(jnp.float32) for c in range(pieces)]
    first_row_values = zero8
    for t in range(bands):
        first_row_values = jnp.where(lane8 == t, band_sums[t], first_row_values)
        label = (agg_ref[t, 0] + 1).astype(jnp.float32)
        first_row_values = jnp.where(lane8 == bands + t, label, first_row_values)

    def choose_back(c, carry):
        for p in range(panels):
            for q in range(own_panels):
                goal, lane = place(16, LANES, q * LANES, True)
                rows = pl.ds(p * LANES + c * 16, 16)
                back[rows, q * LANES : (q + 1) * LANES] = jnp.where(
                    goal == (lane + c * 16) * panels + p, 1.0, 0.0
                ).astype(jnp.bfloat16)
        return carry

    lax.fori_loop(0, LANES // 16, choose_back, 0)

    pl.semaphore_wait(barrier, others)
    for copy in halos:
        copy.start()
    start_f, wait_f, done_f = direct(first_all, 0)
    start_m, wait_m, done_m = direct(max_all, 1)
    start_c, wait_c, done_c = direct(coarse_all, 2)
    finish += [done_f, done_m, done_c]
    start_f(first_row_values[0:1])
    start_bx, wait_bx, done_bx = phase(bulk_x, 5, True)
    start_by, wait_by, done_by = phase(bulk_y, 6, False)
    finish += [done_bx, done_by]
    start_bx()

    own_rows = pl.ds(0, breadth)
    block_rows = min(256, height)

    def settle(c, carry):
        rows = pl.ds(c * block_rows, block_rows)
        for source, target in ((in_b, wet), (in_f, res)):
            moved = placed(source[rows, :], chooser[own_rows, :])
            for p in range(panels):
                target[p, pl.ds(OWN + c * block_rows, block_rows), :] = moved[:, p * LANES : (p + 1) * LANES]
        return carry

    lax.fori_loop(0, height // block_rows, settle, 0)

    for copy in halos:
        copy.wait()

    east_lanes = jnp.where(gy < size_y - 1, DEPTH, 0)
    west_lane = jnp.where(gy > 0, LANES - DEPTH, LANES)
    for side, start, inside in ((SOUTH, PAD, gx > 0), (NORTH, OWN + height, gx < size_x - 1)):
        from_east, from_west = (SW, SE) if side == SOUTH else (NW, NE)
        for part, target in enumerate((wet, res)):
            east = pltpu.roll(got_corner[from_east - NW], (-part * DEPTH) % LANES, 1)
            west = pltpu.roll(got_corner[from_west - NW], (-(part + 1) * DEPTH) % LANES, 1)
            corner = jnp.where(lane16 < east_lanes, east, jnp.where(lane16 >= west_lane, west, 0.0))
            whole_row = jnp.concatenate([got_row[side, part], corner], axis=1)
            moved = placed(jnp.where(inside, whole_row, 0.0), chooser[...])
            for p in range(panels):
                target[p, start : start + DEPTH, :] = moved[:, p * LANES : (p + 1) * LANES]

    def unpack(c, carry):
        r = c * ROW_STEP
        east_all = got_col[WEST - WEST, pl.ds(r, ROW_STEP), :]
        west_all = got_col[EAST - WEST, pl.ds(r, ROW_STEP), :]
        for g in range(GROUPS):
            for part, target in enumerate((side_w, side_r)):
                start = (2 * g + part) * DEPTH
                east = pltpu.roll(east_all, (-start) % LANES, 1)
                west = pltpu.roll(west_all, (LANES - DEPTH - start) % LANES, 1)
                target[pl.ds(g * group_rows + r, ROW_STEP), :] = jnp.where(
                    lane16 < east_lanes, east, jnp.where(lane16 >= west_lane, west, 0.0)
                )
        return carry

    lax.fori_loop(0, group_rows // ROW_STEP, unpack, 0)

    def settle_sides(c, carry):
        rows = pl.ds(c * block_rows, block_rows)
        at = pl.ds(OWN + c * block_rows, block_rows)
        for source, target in ((side_w, wet), (side_r, res)):
            moved = placed(source[rows, :], chooser[pl.ds(breadth, LANES), :])
            for p in range(panels):
                target[p, at, :] = target[p, at, :] + moved[:, p * LANES : (p + 1) * LANES]
        return carry

    lax.fori_loop(0, height // block_rows, settle_sides, 0)

    def east_west(values):
        easts = values[1:] + [pltpu.roll(values[0], LANES - 1, 1)]
        wests = [pltpu.roll(values[-1], 1, 1)] + values[:-1]
        return easts, wests

    last, extra = divmod(breadth + FIRST, panels)
    first_lane = FIRST // panels

    def own_lanes(x, p):
        lane = lax.broadcasted_iota(jnp.int32, x.shape, 1)
        return (lane >= first_lane) & (lane < last + (1 if p < extra else 0))

    def kind(p):
        return 0 if p < extra else 1

    def own_total(parts):
        return jnp.where(own_lanes(parts[0], 0), parts[0], 0.0) + jnp.where(
            own_lanes(parts[1], panels - 1), parts[1], 0.0
        )

    def add_to(pair, p, x):
        return tuple(total + x if i == kind(p) else total for i, total in enumerate(pair))

    zero_pair = (zero8, zero8)

    def row_at(i):
        return pl.ds(i, 1)

    def faces(r, top):
        values = [wet[p, pl.ds(r, ROW_STEP), :] for p in range(panels)]
        easts, wests = east_west(values)
        for p in range(panels):
            at = pl.ds(r, ROW_STEP)
            south = jnp.minimum(values[p], wet[p, pl.ds(r + 1, ROW_STEP), :])
            north = jnp.minimum(values[p], wet[p, pl.ds(r - 1, ROW_STEP), :])
            east = jnp.minimum(values[p], easts[p])
            west = jnp.minimum(values[p], wests[p])
            k_south[p, at, :] = south
            k_north[p, at, :] = north
            k_east[p, at, :] = east
            k_west[p, at, :] = west
            diagonal = 1.0 + south + north + east + west
            centre[p, at, :] = diagonal
            ocean[p, at, :] = jnp.where(values[p] > 0.0, 1.0, 0.0)
            if top is not None:
                for start in range(0, ROW_STEP, 8):
                    part = diagonal[start : start + 8]
                    top = tuple(jnp.maximum(t, part) if i == kind(p) else t for i, t in enumerate(top))
        return top

    top = lax.fori_loop(
        0, height // ROW_STEP, lambda c, top: faces(OWN + c * ROW_STEP, top), (jnp.ones((8, LANES), jnp.float32),) * 2
    )
    top = jnp.maximum(
        jnp.where(own_lanes(top[0], 0), top[0], 1.0), jnp.where(own_lanes(top[1], panels - 1), top[1], 1.0)
    )
    start_m(jnp.max(top, axis=0, keepdims=True))
    faces(PAD, None)
    faces(OWN + height, None)

    wait_f()
    rhs = by_label([rows_of(first_all, i) for i in range(groups)])
    coarse_row = jnp.zeros((1, LANES), jnp.float32)
    lane1 = lax.broadcasted_iota(jnp.int32, (1, LANES), 1)
    for s in range(bands):
        product = jnp.sum(inverse_rows[s : s + 1, :] * rhs, axis=1, keepdims=True)
        coarse_row = jnp.where(lax.rem(lane1, bands) == s, product, coarse_row)
    start_c(coarse_row)

    strips = [(-1, bands - 1)] + [(0, t) for t in range(bands)] + [(1, 0)]
    labels = []
    for dx, t in strips:
        for dy in (-1, 0, 1):
            inside = (gx + dx >= 0) & (gx + dx < size_x) & (gy + dy >= 0) & (gy + dy < size_y)
            device = jnp.where(inside, me + dx * size_y + dy, me)
            label = first_all[pl.ds(device, 1), :][:, bands + t : bands + t + 1]
            label = jnp.broadcast_to(label, (1, LANES))
            labels.append(jnp.where(inside, label, 0.0))

    wait_bx()
    for i in range(size_x):
        bulk_y[gy, i * bands : (i + 1) * bands, :] = bulk_x[i]

    wait_m()
    largest = functools.reduce(jnp.maximum, [rows_of(max_all, i) for i in range(groups)])
    for move in (4, 2, 1):
        largest = jnp.maximum(largest, pltpu.roll(largest, move, 0))
    shift = jnp.broadcast_to(jnp.max(largest, axis=1, keepdims=True), (8, LANES))
    scale = 2.0 / shift
    scale16 = tall(scale, ROW_STEP)

    def rescale(c, carry):
        at = pl.ds(PAD + c * ROW_STEP, ROW_STEP)
        for p in range(panels):
            for array in (k_south, k_north, k_east, k_west):
                array[p, at, :] = array[p, at, :] * scale16
            centre[p, at, :] = centre[p, at, :] * scale16 - 2.0
        return carry

    chunks_all = (rows_all - 2 * PAD) // ROW_STEP
    lax.fori_loop(0, chunks_all, rescale, 0, unroll=3)

    def stencil(array, r):
        at = pl.ds(r, ROW_STEP)
        values = [array[p, at, :] for p in range(panels)]
        easts, wests = east_west(values)
        out = []
        for p in range(panels):
            south = array[p, pl.ds(r + 1, ROW_STEP), :]
            north = array[p, pl.ds(r - 1, ROW_STEP), :]
            flow = k_south[p, at, :] * south + k_north[p, at, :] * north
            flow = flow + (k_east[p, at, :] * easts[p] + k_west[p, at, :] * wests[p])
            out.append(centre[p, at, :] * values[p] - flow)
        return out, values

    def over_bands(chunk, first_sums, run):
        chunk(PAD, None)
        chunk(OWN + height, None)

        def band(t, carry):
            carry = carry + (zero_pair,)
            for c in range(TILE // ROW_STEP):
                carry = chunk(pl.multiple_of(OWN + t * TILE + c * ROW_STEP, 8), carry)
            sums[pl.ds(first_sums + t, 1), :] = jnp.sum(own_total(carry[-1]), axis=0, keepdims=True)
            return carry[:-1]

        return lax.fori_loop(0, bands, band, run)

    shift16 = tall(shift, ROW_STEP)
    grams = [direct(gram_all.at[c], 3 + c) for c in range(CYCLES)]
    finish += [p[2] for p in grams]

    def coarse_values():
        row = jnp.zeros((1, LANES), jnp.float32)
        for k, label in enumerate(labels):
            row = jnp.where(lax.div(lane1, bands) == k, label, row)
        total = zero8
        for i in range(groups):
            number = ((8 * i + sub) * bands + lax.rem(lane8, bands) + 1).astype(jnp.float32)
            total = total + jnp.where(number == row, rows_of(coarse_all, i), 0.0)
        total = sub_total(total)
        found = []
        for k in range(len(labels)):
            picked = jnp.where(lax.div(lane8, bands) == k, total, 0.0)
            found.append(jnp.broadcast_to(jnp.sum(picked, axis=1, keepdims=True), (8, LANES)))
        return found

    def choose_rows():
        slot = lax.broadcasted_iota(jnp.int32, (1, n_agg), 1)
        in_slot = lax.rem(slot, size_x * bands)
        row = (lax.div(in_slot, bands) * size_y + lax.div(slot, size_x * bands)) * bands + lax.rem(in_slot, bands)
        selector[...] = jnp.zeros_like(selector)
        for k, label in enumerate(labels):
            wide = jnp.concatenate([label] * pieces, axis=1)[:, 0:n_agg]
            selector[k : k + 1, :] = jnp.where((row + 1).astype(jnp.float32) == wide, 1.0, 0.0)

    def permute_rows():
        chunks = max(1, n_agg // LANES)
        width, per = n_agg // chunks, size_y // chunks
        rows = None
        for c in range(chunks):
            part = exact_placed(
                selector[:, c * width : (c + 1) * width].astype(jnp.bfloat16),
                jnp.concatenate([bulk_y[c * per + i] for i in range(per)], axis=0),
            )
            rows = part if rows is None else rows + part
        chosen[:, 0:n_agg] = rows

    blocks = height // block_rows

    def basis_to_natural(i, carry):
        a, c = lax.div(i, blocks), lax.rem(i, blocks)
        at = pl.ds(pl.multiple_of(OWN + c * block_rows, 8), block_rows)
        rows = pl.ds(pl.multiple_of(c * block_rows, 8), block_rows)
        natural[a, rows, :] = placed(jnp.concatenate([basis[a, p, at, :] for p in range(panels)], axis=1), back[...])
        return carry

    def sol_to_natural(c, carry):
        rows = pl.ds(c * block_rows, block_rows)
        natural_sol[rows, :] = placed(jnp.concatenate([sol[p, rows, :] for p in range(panels)], axis=1), back[...])
        return carry

    next_values = None
    for cycle in range(CYCLES):
        if cycle == 0:
            wait_c()
            values_at = coarse_values()
        else:
            values_at = next_values

        def spread_band(strip, start, chunks):
            west, own, east = values_at[3 * strip : 3 * strip + 3]
            dx = strips[strip][0]
            side = jnp.where(lane8 < LANES // 2, west, east)
            values = [tall(jnp.where(own_lanes(own, p), own, side), ROW_STEP) for p in range(panels)]

            def body(c, carry):
                at = pl.ds(start + c * ROW_STEP, ROW_STEP)
                for p in range(panels):
                    value = ocean[p, at, :] * values[p]
                    odd[p, at, :] = value
                    if dx == 0:
                        inner = pl.ds(start - OWN + c * ROW_STEP, ROW_STEP)
                        sol[p, inner, :] = value if cycle == 0 else sol[p, inner, :] + value
                return carry

            lax.fori_loop(0, chunks, body, 0, unroll=True)

        spread_band(0, PAD, DEPTH // ROW_STEP)
        for t in range(bands):
            spread_band(1 + t, OWN + t * TILE, TILE // ROW_STEP)
        spread_band(1 + bands, OWN + height, DEPTH // ROW_STEP)
        if cycle == 0:
            start_by()

        with_totals = cycle < CYCLES - 1

        def first(r, carry):
            out, values = stencil(odd, r)
            at = pl.ds(r, ROW_STEP)
            for p in range(panels):
                v = res[p, at, :] - shift16 * (0.5 * out[p] + values[p])
                even[p, at, :] = v
                basis[0, p, at, :] = v
                if carry is not None:
                    square, total = carry
                    carry = (
                        add_to(square, p, fold(v * v)),
                        add_to(total, p, fold(v)) if with_totals else total,
                    )
            return carry

        (square,) = over_bands(first, 0, (zero_pair,))
        sums[64:65, :] = jnp.sum(own_total(square), axis=0, keepdims=True)

        def step(j, source, target, is_first=False):
            def chunk(r, carry):
                out, values = stencil(source, r)
                at = pl.ds(r, ROW_STEP)
                for p in range(panels):
                    v = 0.5 * out[p] if is_first else out[p] - target[p, at, :]
                    target[p, at, :] = v
                    basis[j, p, at, :] = v
                    if carry is not None:
                        square, cross, total = carry
                        carry = (
                            add_to(square, p, fold(v * v)),
                            add_to(cross, p, fold(v * values[p])),
                            add_to(total, p, fold(v)) if with_totals else total,
                        )
                return carry

            square, cross = over_bands(chunk, j * bands, (zero_pair, zero_pair))
            sums[row_at(64 + j), :] = jnp.sum(own_total(square), axis=0, keepdims=True)
            sums[row_at(80 + j), :] = jnp.sum(own_total(cross), axis=0, keepdims=True)

        def two_steps(i, carry):
            step(2 * i + 2, odd, even)
            step(2 * i + 3, even, odd)
            return carry

        step(1, even, odd, True)
        lax.fori_loop(0, KB // 2 - 1, two_steps, 0)
        step(KB, odd, even)

        row = lax.dot_general(
            jnp.ones((8, LANES), jnp.float32),
            sums[...],
            (((1,), (1,)), ((), ())),
            precision=highest,
            preferred_element_type=jnp.float32,
        )
        start_g, wait_g, _ = grams[cycle]
        start_g(row[0:1])
        if cycle == 0:
            choose_rows()
            wait_by()
            permute_rows()
        else:
            lax.fori_loop(0, (KB + 1) * blocks, basis_to_natural, 0)
            lax.fori_loop(0, blocks, sol_to_natural, 0)
        wait_g()
        gathered = [gram_all[cycle, 8 * i : 8 * i + 8, :] for i in range(groups)]
        whole = sub_total(functools.reduce(jnp.add, gathered))

        def at_lane(k):
            return jnp.broadcast_to(whole[:, k : k + 1], (8, LANES))

        vv = [at_lane(64 + a) for a in range(KB + 1)]
        vp = [None] + [at_lane(80 + a) for a in range(1, KB + 1)]
        weight, combined = small_solve(vv, vp)
        for j in range(KB):
            factors[j] = weight[j] / shift
        for a in range(KB + 1):
            factors[KB + a] = combined[a]

        if cycle < CYCLES - 1:
            group = lane8 // bands
            mix = jnp.where(group == 0, 1.0, 0.0)
            for a in range(KB + 1):
                mix = jnp.where(group == a, mix - combined[a], mix)
            mix = jnp.where(lane8 < (KB + 1) * bands, mix, 0.0)
            mixed = []
            for part in gathered:
                part = part * mix
                move = bands
                while move < LANES:
                    part = part + pltpu.roll(part, move, 1)
                    move *= 2
                mixed.append(part)
            found = chosen[...] * by_label(mixed)
            found = jnp.broadcast_to(jnp.sum(found, axis=1, keepdims=True), (found.shape[0], LANES))
            next_values = [jnp.broadcast_to(found[k : k + 1, :], (8, LANES)) for k in range(len(labels))]

        if cycle == CYCLES - 1:
            break
        w = [tall(factors[j], ROW_STEP) for j in range(KB)]
        c_all = [tall(factors[KB + a], ROW_STEP) for a in range(KB + 1)]

        def update(r, p, inner):
            at = pl.ds(r, ROW_STEP)
            values = [basis[a, p, at, :] for a in range(KB + 1)]
            residual = values[0]
            for a in range(KB + 1):
                residual = residual - c_all[a] * values[a]
            if inner is None:
                res[p, at, :] = residual
                return
            rows = pl.ds(inner, ROW_STEP)
            answer = sol[p, rows, :]
            for j in range(KB):
                answer = answer + w[j] * values[j]
            res[p, at, :] = residual
            sol[p, rows, :] = answer

        def update_own(c, carry):
            for p in range(panels):
                update(OWN + c * ROW_STEP, p, c * ROW_STEP)
            return carry

        lax.fori_loop(0, height // ROW_STEP, update_own, 0, unroll=2)
        for p in range(panels):
            update(PAD, p, None)
            update(OWN + height, p, None)

    for done in finish:
        done()


def combine(natural, natural_sol, factors, solution_out, residual_out, parts, sems):
    height, breadth = natural_sol.shape
    rows = parts.shape[1]
    copies = []
    for index in range(height // rows):

        def chunk(c, carry, index=index):
            at = pl.ds(index * rows + c * ROW_STEP, ROW_STEP)
            there = pl.ds(c * ROW_STEP, ROW_STEP)
            for p in range(breadth // LANES):
                columns = slice(p * LANES, (p + 1) * LANES)
                values = [natural[a, at, columns] for a in range(KB + 1)]
                answer, residual = natural_sol[at, columns], values[0]
                for a in range(KB + 1):
                    residual = residual - tall(factors[KB + a], ROW_STEP) * values[a]
                for j in range(KB):
                    answer = answer + tall(factors[j], ROW_STEP) * values[j]
                parts[2 * index, there, columns] = answer
                parts[2 * index + 1, there, columns] = residual
            return carry

        lax.fori_loop(0, rows // ROW_STEP, chunk, 0, unroll=2)
        for which, target in enumerate((solution_out, residual_out)):
            slot = 2 * index + which
            copy = pltpu.make_async_copy(parts.at[slot], target.at[pl.ds(index * rows, rows), :], sems.at[slot])
            copy.start()
            copies.append(copy)
    for copy in copies:
        copy.wait()


def on_device(size_x, size_y, forcing, bathymetry, ocean_mask, aggregate_id, coarse_inverse):
    height, breadth = forcing.shape
    own_panels = breadth // LANES
    panels = own_panels + 1
    rows = height + 2 * (DEPTH + PAD)
    bands = height // TILE
    f32 = jnp.float32
    field = pltpu.VMEM((panels, rows, LANES), f32)
    block = pltpu.VMEM((height, breadth), f32)
    any_spec = pl.BlockSpec(memory_space=pltpu.MemorySpace.HBM)
    vmem = pl.BlockSpec(memory_space=pltpu.VMEM)
    smem = pl.BlockSpec(memory_space=pltpu.SMEM)
    rows_all = pltpu.VMEM((size_x * size_y, LANES), f32)
    tiles = lambda *lead: pltpu.VMEM(lead + (8, LANES), f32)
    dma = pltpu.SemaphoreType.DMA
    n_agg = coarse_inverse.shape[1]
    wanted = -(-3 * (bands + 2) // 8) * 8
    results = (
        jax.ShapeDtypeStruct((KB + 1, height, breadth), f32),
        jax.ShapeDtypeStruct((height, breadth), f32),
        jax.ShapeDtypeStruct((2 * KB + 1, 8, LANES), f32),
    )
    forcing, bathymetry, ocean_mask, aggregate_id, coarse_inverse = (
        pltpu.with_memory_space_constraint(x, pltpu.MemorySpace.HBM)
        for x in (forcing, bathymetry, ocean_mask, aggregate_id, coarse_inverse)
    )
    natural, natural_sol, factors = pl.pallas_call(
        functools.partial(kernel, size_x, size_y),
        out_shape=results,
        in_specs=[any_spec, any_spec, any_spec, smem, any_spec],
        out_specs=(vmem, vmem, vmem),
        scratch_shapes=[
            block,
            block,
            pltpu.VMEM((height, breadth), jnp.int32),
            pltpu.VMEM((height, LANES), f32),
            pltpu.VMEM((height, LANES), f32),
            pltpu.VMEM((panels * LANES, panels * LANES), jnp.bfloat16),
            pltpu.VMEM((panels * LANES, breadth), jnp.bfloat16),
            field,
            field,
            field,
            pltpu.VMEM((panels, height, LANES), f32),
            pltpu.VMEM((KB + 1, panels, rows, LANES), f32),
            field,
            field,
            field,
            field,
            field,
            field,
            field,
            pltpu.VMEM((2, height // GROUPS, LANES), f32),
            pltpu.VMEM((2, height // GROUPS, LANES), f32),
            pltpu.VMEM((4, DEPTH, LANES), f32),
            pltpu.VMEM((4, DEPTH, LANES), f32),
            pltpu.VMEM((2, 2, DEPTH, breadth), f32),
            pltpu.VMEM((8, -(-n_agg // LANES) * LANES), f32),
            pltpu.VMEM((wanted, n_agg), f32),
            pltpu.VMEM((wanted, -(-n_agg // LANES) * LANES), f32),
            pltpu.VMEM((size_x, bands, n_agg), f32),
            pltpu.VMEM((size_y, size_x * bands, n_agg), f32),
            pltpu.VMEM((LANES, LANES), f32),
            rows_all,
            rows_all,
            rows_all,
            pltpu.VMEM((CYCLES, size_x * size_y, LANES), f32),
            dma((4,)),
            dma((10,)),
            dma((10,)),
            dma((7,)),
            dma((7,)),
        ],
        compiler_params=pltpu.CompilerParams(
            collective_id=0, has_side_effects=True, vmem_limit_bytes=40 * 1024 * 1024
        ),
    )(forcing, bathymetry, ocean_mask, aggregate_id, coarse_inverse)
    part = 64
    count = 2 * (height // part)
    return pl.pallas_call(
        combine,
        out_shape=(jax.ShapeDtypeStruct((height, breadth), f32),) * 2,
        in_specs=[vmem, vmem, vmem],
        out_specs=(any_spec, any_spec),
        scratch_shapes=[pltpu.VMEM((count, part, breadth), f32), dma((count,))],
        compiler_params=pltpu.CompilerParams(vmem_limit_bytes=16 * 1024 * 1024),
    )(natural, natural_sol, factors)


def solution(mesh):
    return jax.shard_map(
        functools.partial(on_device, mesh.shape["gx"], mesh.shape["gy"]),
        mesh=mesh,
        in_specs=(
            P("gx", "gy"),
            P("gx", "gy"),
            P("gx", "gy"),
            P("gx", "gy"),
            P(("gx", "gy"), None),
        ),
        out_specs=(P("gx", "gy"), P("gx", "gy")),
        check_vma=False,
    )
```
